128 devices in a mesh: seq: 32 (over x, z, core), head: 4 (over y).
Axes of the slice: x: 4, y: 4, z: 4, core: 2. Of those that a mesh axis runs over, the one named last changes fastest.
Arguments:
- tokens: bfloat16 [16384, 1024], P('seq'), may hold values from -6 to 6
- segment_ids: int32 [16384], replicated, may hold values from 0 to 4, as said below
- mix_gain: float32 [1024], replicated, may hold values from 0.1 to 1.9
- in_weight: bfloat16 [1024, 3, 1024], P(None, None, 'head'), may hold values from -0.1875 to 0.1875
- conv_weight: bfloat16 [3, 1024], P(None, 'head'), may hold values from -3 to 3
- out_weight: bfloat16 [1024, 1024], P(None, 'head'), may hold values from -0.1875 to 0.1875
- ffn_gain: float32 [1024], replicated, may hold values from 0.1 to 1.9
- gate_weight: bfloat16 [1024, 4608], P(None, 'head'), may hold values from -0.1875 to 0.1875
- up_weight: bfloat16 [1024, 4608], P(None, 'head'), may hold values from -0.1875 to 0.1875
- down_weight: bfloat16 [1024, 4608], P(None, 'head'), may hold values from -0.125 to 0.125
- cotangent: bfloat16 [16384, 1024], P('seq'), may hold values from -6 to 6
Outputs:
- result: bfloat16 [16384, 1024], P('seq')
- grad_tokens: float32 [16384, 1024], P('seq')
- grad_mix_gain: float32 [1024], replicated
- grad_in_weight: float32 [1024, 3, 1024], P('seq', None, 'head')
- grad_conv_weight: float32 [3, 1024], P(None, 'head')
- grad_out_weight: float32 [1024, 1024], P('seq', 'head')
- grad_ffn_gain: float32 [1024], replicated
- grad_gate_weight: float32 [1024, 4608], P('seq', 'head')
- grad_up_weight: float32 [1024, 4608], P('seq', 'head')
- grad_down_weight: float32 [1024, 4608], P('seq', 'head')
The draws below stay inside these ranges and needn't reach their ends.
Inputs may be any that keep to these rules, and one draw needn't show every extreme that they name: `segment_ids`: ids start at 0, never fall along the tokens and rise by one at each sequence boundary; the tokens of one id form one sequence of at most 4096 tokens.
All inputs are finite; a program needn't handle non-finite values.
Results may differ from the reference program's by a relative error of at most 0.0095.
Values sent between devices are 32-bit elements; how exact they have to be, the bound alone decides.
A program may use at most 128 MiB of HBM per device.

```python
import math
import jax
import jax.numpy as jnp
from jax import lax

D = 1024
FF = 4608
TOKENS = 16384
SEQ_LEN = 4096


def draw_segment_ids(key, part):
    offset = jax.random.randint(jax.random.fold_in(key, 17), (), 3, SEQ_LEN - 2).astype(jnp.int32)
    positions = jnp.arange(TOKENS, dtype=jnp.int32)
    return ((positions + SEQ_LEN - offset) // SEQ_LEN).astype(jnp.int32)


def spiked(drawn, own_key, source, target, shards_of, factor):
    def block_of(axis_at):
        return (jnp.arange(drawn.shape[axis_at]) // (drawn.shape[axis_at] // shards_of)).reshape((-1,) + (1,) * (drawn.ndim - 1 - axis_at))

    one_side = jax.random.permutation(own_key, shards_of)[block_of(target)]
    other_side = (block_of(target) + shards_of // 2) % shards_of
    return jnp.where((block_of(source) == one_side) | (block_of(source) == other_side), factor * drawn, drawn)


def steps_of(stream_key, dims, split, least, high):
    level, own = 1.0, jax.random.fold_in(stream_key, 6)
    for axis_at, parts in split:
        heights = jnp.exp(jax.random.uniform(jax.random.fold_in(own, axis_at), (parts,), jnp.float32, least / len(split), high / len(split)))
        level = level * jnp.repeat(heights, dims[axis_at] // parts).reshape([-1 if axis == axis_at else 1 for axis in range(len(dims))])
    return level


def scatter_about(stream_key, extent, scale, bound, split=(), held_as=jnp.bfloat16):
    array = jax.random.normal(stream_key, extent, jnp.float32) * scale
    if len(split) > 0:
        array = steps_of(stream_key, extent, split, -0.22, 0.18) * array
    return jnp.clip(array, min=-bound, max=bound).astype(held_as)


def heavy_noise(own_key, shape, spread, limit, cuts, heavy, held_as=jnp.bfloat16):
    array = spread * jax.random.normal(own_key, shape, jnp.float32)
    if cuts:
        array = array * steps_of(own_key, shape, cuts, -0.22, 0.18)
    return jnp.clip(spiked(array, jax.random.fold_in(own_key, 3), *heavy), -limit, limit).astype(held_as)


def setup_inputs(seed: int = 0) -> dict:
    arg_keys = jax.random.split(jax.random.key(seed), 12)
    return {
        "tokens": scatter_about(arg_keys[0], (TOKENS, D), 1.0, 6.0, ((0, 32),)),
        "segment_ids": draw_segment_ids(jax.random.fold_in(arg_keys[11], 71), 0),
        "mix_gain": jnp.clip(1.0 + 0.18 * jax.random.normal(arg_keys[2], (D,), jnp.float32), 0.1, 1.9),
        "in_weight": scatter_about(arg_keys[3], (D, 3, D), D ** -0.5, 0.1875, ((2, 4),)),
        "conv_weight": scatter_about(arg_keys[4], (3, D), 0.6, 3.0, ((1, 4),)),
        "out_weight": scatter_about(arg_keys[5], (D, D), D ** -0.5, 0.1875, ((1, 4),)),
        "ffn_gain": jnp.clip(1.0 + 0.18 * jax.random.normal(arg_keys[6], (D,), jnp.float32), 0.1, 1.9),
        "gate_weight": scatter_about(arg_keys[7], (D, FF), D ** -0.5, 0.1875, ((1, 4),)),
        "up_weight": scatter_about(arg_keys[8], (D, FF), D ** -0.5, 0.1875, ((1, 4),)),
        "down_weight": scatter_about(arg_keys[9], (D, FF), (FF // 2) ** -0.5, 0.125, ((1, 4),)),
        "cotangent": heavy_noise(arg_keys[10], (TOKENS, D), 1.0, 6.0, ((0, 32),), (0, 1, 32, 2.75)),
    }


EPS = 1e-05

def rms_scale(values):
    return lax.rsqrt(lax.optimization_barrier(jnp.mean(values * values, axis=-1, keepdims=True)) + EPS)

def norm_back(grad_normed, values, scale, gain):
    weighted = grad_normed * gain
    inner = lax.optimization_barrier(jnp.mean(weighted * values, axis=-1, keepdims=True))
    grad_values = scale * weighted - values * (scale * scale * scale) * inner
    gain_grad = lax.optimization_barrier(jnp.sum(grad_normed * values * scale, axis=0))
    return (grad_values, gain_grad)

def reference(tokens, segment_ids, mix_gain, in_weight, conv_weight, out_weight, ffn_gain, gate_weight, up_weight, down_weight, cotangent):
    inputs = tokens.astype(jnp.float32)
    mix_scale = rms_scale(inputs)
    mix_normed = (inputs * mix_scale * mix_gain).astype(jnp.bfloat16)
    in_flat = in_weight.reshape(D, 3 * D)
    projected = jnp.dot(mix_normed, in_flat, preferred_element_type=jnp.float32).reshape(TOKENS, 3, D)
    chan_b = projected[:, 0]
    chan_c = projected[:, 1]
    chan_x = projected[:, 2]
    mixed = chan_b * chan_x
    near = jnp.concatenate([jnp.zeros((1,), jnp.float32), (segment_ids[1:] == segment_ids[:-1]).astype(jnp.float32)])
    far = jnp.concatenate([jnp.zeros((2,), jnp.float32), (segment_ids[2:] == segment_ids[:-2]).astype(jnp.float32)])
    kernel = conv_weight.astype(jnp.float32)
    prev_one = jnp.concatenate([jnp.zeros((1, D), jnp.float32), mixed[:-1]])
    prev_two = jnp.concatenate([jnp.zeros((2, D), jnp.float32), mixed[:-2]])
    conv_out = kernel[0] * mixed + kernel[1] * near[:, None] * prev_one + kernel[2] * far[:, None] * prev_two
    gated = (chan_c * conv_out).astype(jnp.bfloat16)
    resid = inputs + jnp.dot(gated, out_weight.T, preferred_element_type=jnp.float32)
    block = math.gcd(TOKENS, 4096)
    count = TOKENS // block
    gain_two = ffn_gain

    def ffn_step(carry, pieces):
        acc_gate, acc_up, acc_down, acc_gain = carry
        hidden_in, cot_block = pieces
        ffn_scale = rms_scale(hidden_in)
        ffn_normed = (hidden_in * ffn_scale * gain_two).astype(jnp.bfloat16)
        gate = jnp.dot(ffn_normed, gate_weight, preferred_element_type=jnp.float32)
        upper = jnp.dot(ffn_normed, up_weight, preferred_element_type=jnp.float32)
        sigma = jax.nn.sigmoid(gate)
        act = (gate * sigma * upper).astype(jnp.bfloat16)
        out_block = (hidden_in + jnp.dot(act, down_weight.T, preferred_element_type=jnp.float32)).astype(jnp.bfloat16)
        d_act = jnp.dot(cot_block, down_weight, preferred_element_type=jnp.float32)
        d_gate = (d_act * upper * sigma * (1.0 + gate * (1.0 - sigma))).astype(jnp.bfloat16)
        d_up = (d_act * gate * sigma).astype(jnp.bfloat16)
        acc_down = acc_down + jnp.dot(cot_block.T, act, preferred_element_type=jnp.float32)
        acc_gate = acc_gate + jnp.dot(ffn_normed.T, d_gate, preferred_element_type=jnp.float32)
        acc_up = acc_up + jnp.dot(ffn_normed.T, d_up, preferred_element_type=jnp.float32)
        d_normed = jnp.dot(d_gate, gate_weight.T, preferred_element_type=jnp.float32) + jnp.dot(d_up, up_weight.T, preferred_element_type=jnp.float32)
        d_hidden, gain_grad = norm_back(d_normed, hidden_in, ffn_scale, gain_two)
        d_hidden = d_hidden + cot_block.astype(jnp.float32)
        return ((acc_gate, acc_up, acc_down, acc_gain + gain_grad), (out_block, d_hidden))
    start_carry = (jnp.zeros((D, FF), jnp.float32), jnp.zeros((D, FF), jnp.float32), jnp.zeros((D, FF), jnp.float32), jnp.zeros((D,), jnp.float32))
    carry, outputs = lax.scan(ffn_step, start_carry, (resid.reshape(count, block, D), cotangent.reshape(count, block, D)))
    grad_gate, grad_up, grad_down, grad_ffn_gain = carry
    result = outputs[0].reshape(TOKENS, D)
    d_resid = outputs[1].reshape(TOKENS, D)
    d_resid_low = d_resid.astype(jnp.bfloat16)
    d_gated = jnp.dot(d_resid_low, out_weight, preferred_element_type=jnp.float32)
    grad_out = jnp.dot(d_resid_low.T, gated, preferred_element_type=jnp.float32)
    d_chan_c = d_gated * conv_out
    d_conv = d_gated * chan_c
    next_one = jnp.concatenate([d_conv[1:], jnp.zeros((1, D), jnp.float32)])
    next_two = jnp.concatenate([d_conv[2:], jnp.zeros((2, D), jnp.float32)])
    near_next = jnp.concatenate([near[1:], jnp.zeros((1,), jnp.float32)])
    far_next = jnp.concatenate([far[2:], jnp.zeros((2,), jnp.float32)])
    d_mixed = kernel[0] * d_conv + kernel[1] * near_next[:, None] * next_one + kernel[2] * far_next[:, None] * next_two
    grad_conv = jnp.stack([lax.optimization_barrier(jnp.sum(d_conv * mixed, axis=0)), lax.optimization_barrier(jnp.sum(d_conv * near[:, None] * prev_one, axis=0)), lax.optimization_barrier(jnp.sum(d_conv * far[:, None] * prev_two, axis=0))])
    d_projected = jnp.stack([d_mixed * chan_x, d_chan_c, d_mixed * chan_b], axis=1).astype(jnp.bfloat16).reshape(TOKENS, 3 * D)
    grad_in = jnp.dot(mix_normed.T, d_projected, preferred_element_type=jnp.float32).reshape(D, 3, D)
    d_mix_normed = jnp.dot(d_projected, in_flat.T, preferred_element_type=jnp.float32)
    d_inputs, grad_mix_gain = norm_back(d_mix_normed, inputs, mix_scale, mix_gain)
    grad_tokens = d_resid + d_inputs
    return (result, grad_tokens, grad_mix_gain, grad_in, grad_conv, grad_out, grad_ffn_gain, grad_gate, grad_up, grad_down)
```

```python
import jax
import jax.numpy as jnp
from jax import lax
from jax.experimental import pallas as pl
from jax.experimental.pallas import tpu as pltpu
from jax.sharding import PartitionSpec as P

EPS = 1e-05
MESH = pl.DeviceIdType.MESH
HEADS = 4


def norm_back_rows(grad_normed, values, gain, extra):
    scale = lax.rsqrt(jnp.mean(values * values, axis=-1, keepdims=True) + EPS)
    weighted = grad_normed * gain
    inner = jnp.mean(weighted * values, axis=-1, keepdims=True)
    return extra + (scale * weighted - values * (scale * scale * scale) * inner)


def ring_kernel(kinds, *refs):
    jobs = len(kinds)
    at = 0
    ins = []
    for kind in kinds:
        n = 4 if kind == "norm" else 2
        ins.append(refs[at : at + n])
        at += n
    outs = refs[at : at + jobs]
    at += jobs
    scratch = [refs[at + 4 * j : at + 4 * j + 4] for j in range(jobs)]
    s_sem, r_sem = refs[at + 4 * jobs : at + 4 * jobs + 2]
    T = outs[0].shape[0]
    C = T // HEADS
    H = C // 2

    me = lax.axis_index("head")
    R = lax.rem(me + 1, HEADS)
    L = lax.rem(me + HEADS - 1, HEADS)
    O = lax.rem(me + 2, HEADS)
    barrier = pltpu.get_barrier_semaphore()
    for other in (R, L):
        pl.semaphore_signal(barrier, inc=1, device_id={"head": other}, device_id_type=MESH)
    pl.semaphore_wait(barrier, 2)

    def rows(k, half):
        return pl.ds(pl.multiple_of(k * C + half * H, H), H)

    def send(src, dst, job, i, dev):
        copy = pltpu.make_async_remote_copy(
            src_ref=src,
            dst_ref=dst,
            send_sem=s_sem.at[job, i],
            recv_sem=r_sem.at[job, i],
            device_id={"head": dev},
            device_id_type=MESH,
        )
        copy.start()
        return copy

    def finish(job, half, total):
        kind = kinds[job]
        mine = pl.ds(half * H, H)
        if kind == "norm":
            _, values, gain, extra = ins[job]
            total = norm_back_rows(
                total, values[mine, :].astype(jnp.float32), gain[...], extra[mine, :].astype(jnp.float32)
            )
        else:
            total = total + ins[job][1][mine, :].astype(jnp.float32)
        outs[job][rows(me, half), :] = total

    every = []
    live = []
    for j in range(jobs):
        p = ins[j][0]
        t1, t2, fl, fr = scratch[j]
        a0 = send(p.at[rows(O, 0)], t1.at[0], j, 0, R)
        a1 = send(p.at[rows(O, 1)], t2.at[0], j, 1, L)
        a2 = send(p.at[rows(R, 1)], fl.at[1], j, 2, R)
        a3 = send(p.at[rows(L, 0)], fr.at[0], j, 3, L)
        live.append((a0, a1, a2, a3))
        every += [a0, a1, a2, a3]
    second = []
    for j in range(jobs):
        p = ins[j][0]
        t1, t2, fl, fr = scratch[j]
        a0, a1, a2, a3 = live[j]
        a0.wait_recv()
        t1[1] = p[rows(R, 0), :] + t1[0]
        a4 = send(t1.at[1], fl.at[0], j, 4, R)
        a1.wait_recv()
        t2[1] = p[rows(L, 1), :] + t2[0]
        a5 = send(t2.at[1], fr.at[1], j, 5, L)
        second.append((a2, a3, a4, a5))
        every += [a4, a5]
    shares = []
    for j in range(jobs):
        p, o = ins[j][0], outs[j]
        t1, t2, fl, fr = scratch[j]
        a2, a3, a4, a5 = second[j]
        a3.wait_recv()
        a4.wait_recv()
        finish(j, 0, p[rows(me, 0), :] + fl[0] + fr[0])
        b0 = send(o.at[rows(me, 0)], o.at[rows(me, 0)], j, 6, R)
        c0 = send(o.at[rows(me, 0)], o.at[rows(me, 0)], j, 8, L)
        a2.wait_recv()
        a5.wait_recv()
        finish(j, 1, p[rows(me, 1), :] + fl[1] + fr[1])
        b1 = send(o.at[rows(me, 1)], o.at[rows(me, 1)], j, 7, R)
        c1 = send(o.at[rows(me, 1)], o.at[rows(me, 1)], j, 9, L)
        shares.append((b0, b1, c0, c1))
        every += [b0, b1, c0, c1]
    last = []
    for j in range(jobs):
        o = outs[j]
        b0, b1, c0, c1 = shares[j]
        b0.wait_recv()
        d0 = send(o.at[rows(L, 0)], o.at[rows(L, 0)], j, 10, R)
        c1.wait_recv()
        d1 = send(o.at[rows(R, 1)], o.at[rows(R, 1)], j, 11, L)
        last += [b1, c0, d0, d1]
        every += [d0, d1]
    for copy in last:
        copy.wait_recv()
    for copy in every:
        copy.wait_send()


def ring(jobs, cid):
    kinds = tuple(job[0] for job in jobs)
    arrays = [a for job in jobs for a in job[1:]]
    T, D = jobs[0][1].shape
    H = T // HEADS // 2
    n = len(jobs)
    outs = pl.pallas_call(
        lambda *refs: ring_kernel(kinds, *refs),
        out_shape=tuple(jax.ShapeDtypeStruct((T, D), jnp.float32) for _ in jobs),
        in_specs=[pl.BlockSpec(memory_space=pltpu.VMEM)] * len(arrays),
        out_specs=tuple(pl.BlockSpec(memory_space=pltpu.VMEM) for _ in jobs),
        scratch_shapes=[pltpu.VMEM((2, H, D), jnp.float32)] * (4 * n)
        + [pltpu.SemaphoreType.DMA((n, 12))] * 2,
        compiler_params=pltpu.CompilerParams(
            collective_id=cid, has_side_effects=True, vmem_limit_bytes=32 << 20
        ),
        cost_estimate=pl.CostEstimate(flops=1, bytes_accessed=1, transcendentals=0),
        name=f"ring{cid}",
    )(*arrays)
    return outs


def from_behind(block, axis, distance):
    devices = range(lax.axis_size(axis))
    route = [(i - distance, i) for i in devices if i - distance in devices]
    return lax.ppermute(block, axis, route)


def rms_scale(values):
    return lax.rsqrt(jnp.mean(values * values, axis=-1, keepdims=True) + EPS)


def right_product(left, right):
    return lax.dot_general(
        left, right, (((1,), (1,)), ((), ())), preferred_element_type=jnp.float32
    )


def token_product(left, right):
    return lax.dot_general(
        left, right, (((0,), (0,)), ((), ())), preferred_element_type=jnp.float32
    )


def shared(grad):
    return lax.psum_scatter(grad, "seq", scatter_dimension=0, tiled=True)


def on_device(
    tokens,
    segment_ids,
    mix_gain,
    in_weight,
    conv_weight,
    out_weight,
    ffn_gain,
    gate_weight,
    up_weight,
    down_weight,
    cotangent,
):
    tok_rows = tokens.shape[0]
    own = tok_rows // HEADS
    own_at = lax.axis_index("head") * own

    def own_rows(x):
        return lax.dynamic_slice_in_dim(x, own_at, own, 0)

    first_row = lax.axis_index("seq") * tok_rows
    padded_ids = jnp.concatenate(
        [jnp.full((2,), -1, jnp.int32), segment_ids, jnp.full((2,), -2, jnp.int32)]
    )
    id_window = lax.dynamic_slice_in_dim(padded_ids, first_row, tok_rows + 4)
    near_ext = (id_window[2 : tok_rows + 4] == id_window[1 : tok_rows + 3]).astype(jnp.float32)
    far_ext = (id_window[2 : tok_rows + 4] == id_window[0 : tok_rows + 2]).astype(jnp.float32)
    near_own = near_ext[:tok_rows, None]
    far_own = far_ext[:tok_rows, None]
    inputs = tokens.astype(jnp.float32)
    mix_scale = rms_scale(inputs)
    mix_normed = (inputs * mix_scale * mix_gain).astype(jnp.bfloat16)
    projected = jnp.einsum("td,dkc->tkc", mix_normed, in_weight, preferred_element_type=jnp.float32)
    chan_b = projected[:, 0]
    chan_c = projected[:, 1]
    chan_x = projected[:, 2]
    mixed = chan_b * chan_x
    edge_rows = from_behind(mixed[tok_rows - 2 :], "seq", 1)
    extended = jnp.concatenate([edge_rows, mixed])
    kernel = conv_weight.astype(jnp.float32)
    prev_one = extended[1 : tok_rows + 1]
    prev_two = extended[0:tok_rows]
    conv_out = kernel[0] * mixed + kernel[1] * near_own * prev_one + kernel[2] * far_own * prev_two
    gated = (chan_c * conv_out).astype(jnp.bfloat16)
    (resid,) = ring([("add", right_product(gated, out_weight), own_rows(tokens))], 1)
    ffn_scale = rms_scale(resid)
    ffn_normed = (resid * ffn_scale * ffn_gain).astype(jnp.bfloat16)
    gate = jnp.dot(ffn_normed, gate_weight, preferred_element_type=jnp.float32)
    upper = jnp.dot(ffn_normed, up_weight, preferred_element_type=jnp.float32)
    sigma = jax.nn.sigmoid(gate)
    act = (gate * sigma * upper).astype(jnp.bfloat16)
    d_act = jnp.dot(cotangent, down_weight, preferred_element_type=jnp.float32)
    d_gate = (d_act * upper * sigma * (1.0 + gate * (1.0 - sigma))).astype(jnp.bfloat16)
    d_up = (d_act * gate * sigma).astype(jnp.bfloat16)
    grad_down = token_product(cotangent, act)
    grad_gate = token_product(ffn_normed, d_gate)
    grad_up = token_product(ffn_normed, d_up)
    down_share, gate_share, up_share = shared(grad_down), shared(grad_gate), shared(grad_up)
    d_normed_part = right_product(d_gate, gate_weight) + right_product(d_up, up_weight)
    grad_ffn_gain = jnp.sum(d_normed_part * resid * ffn_scale, axis=0)
    d_normed_part, _, _, _ = lax.optimization_barrier((d_normed_part, grad_down, grad_gate, grad_up))
    (d_resid,) = ring(
        [("norm", d_normed_part, own_rows(resid), ffn_gain[None], own_rows(cotangent))], 2
    )
    d_resid_low = d_resid.astype(jnp.bfloat16)
    d_gated = jnp.dot(d_resid_low, out_weight, preferred_element_type=jnp.float32)
    grad_out = token_product(d_resid_low, gated)
    d_chan_c = d_gated * conv_out
    d_conv = d_gated * chan_c
    tail_rows = from_behind(d_conv[:2], "seq", -1)
    later = jnp.concatenate([d_conv, tail_rows])
    next_one = later[1 : tok_rows + 1]
    next_two = later[2 : tok_rows + 2]
    near_next = near_ext[1 : tok_rows + 1, None]
    far_next = far_ext[2 : tok_rows + 2, None]
    d_mixed = kernel[0] * d_conv + kernel[1] * near_next * next_one + kernel[2] * far_next * next_two
    grad_conv = jnp.stack(
        [
            jnp.sum(d_conv * mixed, axis=0),
            jnp.sum(d_conv * near_own * prev_one, axis=0),
            jnp.sum(d_conv * far_own * prev_two, axis=0),
        ]
    )
    d_projected = jnp.stack([d_mixed * chan_x, d_chan_c, d_mixed * chan_b], axis=1).astype(
        jnp.bfloat16
    )
    grad_in = jnp.einsum("td,tkc->dkc", mix_normed, d_projected, preferred_element_type=jnp.float32)
    in_share = shared(grad_in)
    out_share = shared(grad_out)
    d_mix_part = jnp.einsum(
        "tkc,dkc->td", d_projected, in_weight, preferred_element_type=jnp.float32
    )
    grad_mix_gain = jnp.sum(d_mix_part * inputs * mix_scale, axis=0)
    gain_totals = lax.psum(jnp.stack([grad_mix_gain, grad_ffn_gain]), ("seq", "head"))
    conv_total = lax.psum(grad_conv, "seq")
    result_part = right_product(act, down_weight)
    d_mix_part, result_part, _, _ = lax.optimization_barrier((d_mix_part, result_part, grad_in, grad_out))
    grad_tokens, result = ring(
        [
            ("norm", d_mix_part, own_rows(tokens), mix_gain[None], own_rows(d_resid)),
            ("add", result_part, own_rows(resid)),
        ],
        3,
    )
    return (
        result.astype(jnp.bfloat16),
        grad_tokens,
        gain_totals[0],
        in_share,
        conv_total,
        out_share,
        gain_totals[1],
        gate_share,
        up_share,
        down_share,
    )


def solution(mesh):
    placed = (
        P("seq", None),
        P(),
        P(),
        P(None, None, "head"),
        P(None, "head"),
        P(None, "head"),
        P(),
        P(None, "head"),
        P(None, "head"),
        P(None, "head"),
        P("seq", None),
    )
    return jax.shard_map(
        on_device,
        mesh=mesh,
        in_specs=placed,
        out_specs=(
            P("seq", None),
            P("seq", None),
            P(),
            P("seq", None, "head"),
            P(None, "head"),
            P("seq", "head"),
            P(),
            P("seq", "head"),
            P("seq", "head"),
            P("seq", "head"),
        ),
        check_vma=False,
    )
```

```python
import jax
import jax.numpy as jnp
from jax import lax
from jax.experimental import pallas as pl
from jax.experimental.pallas import tpu as pltpu
from jax.sharding import PartitionSpec as P

EPS = 1e-05
MESH = pl.DeviceIdType.MESH
HEADS = 4


def norm_back_rows(grad_normed, values, gain, extra):
    scale = lax.rsqrt(jnp.mean(values * values, axis=-1, keepdims=True) + EPS)
    weighted = grad_normed * gain
    inner = jnp.mean(weighted * values, axis=-1, keepdims=True)
    return extra + (scale * weighted - values * (scale * scale * scale) * inner)


def ring_kernel(kinds, *refs):
    jobs = len(kinds)
    at = 0
    ins = []
    for kind in kinds:
        n = 4 if kind == "norm" else 2
        ins.append(refs[at : at + n])
        at += n
    outs = refs[at : at + jobs]
    at += jobs
    scratch = [refs[at + 4 * j : at + 4 * j + 4] for j in range(jobs)]
    s_sem, r_sem = refs[at + 4 * jobs : at + 4 * jobs + 2]
    T = outs[0].shape[0]
    C = T // HEADS
    H = C // 2

    me = lax.axis_index("head")
    R = lax.rem(me + 1, HEADS)
    L = lax.rem(me + HEADS - 1, HEADS)
    O = lax.rem(me + 2, HEADS)
    barrier = pltpu.get_barrier_semaphore()
    for other in (R, L):
        pl.semaphore_signal(barrier, inc=1, device_id={"head": other}, device_id_type=MESH)
    pl.semaphore_wait(barrier, 2)

    def rows(k, half):
        return pl.ds(pl.multiple_of(k * C + half * H, H), H)

    def send(src, dst, job, i, dev):
        copy = pltpu.make_async_remote_copy(
            src_ref=src,
            dst_ref=dst,
            send_sem=s_sem.at[job, i],
            recv_sem=r_sem.at[job, i],
            device_id={"head": dev},
            device_id_type=MESH,
        )
        copy.start()
        return copy

    def finish(job, half, total):
        kind = kinds[job]
        mine = pl.ds(half * H, H)
        if kind == "norm":
            _, values, gain, extra = ins[job]
            total = norm_back_rows(
                total, values[mine, :].astype(jnp.float32), gain[...], extra[mine, :].astype(jnp.float32)
            )
        else:
            total = total + ins[job][1][mine, :].astype(jnp.float32)
        outs[job][rows(me, half), :] = total

    every = []
    live = []
    for j in range(jobs):
        p = ins[j][0]
        t1, t2, fl, fr = scratch[j]
        a0 = send(p.at[rows(O, 0)], t1.at[0], j, 0, R)
        a1 = send(p.at[rows(O, 1)], t2.at[0], j, 1, L)
        a2 = send(p.at[rows(R, 1)], fl.at[1], j, 2, R)
        a3 = send(p.at[rows(L, 0)], fr.at[0], j, 3, L)
        live.append((a0, a1, a2, a3))
        every += [a0, a1, a2, a3]
    second = []
    for j in range(jobs):
        p = ins[j][0]
        t1, t2, fl, fr = scratch[j]
        a0, a1, a2, a3 = live[j]
        a0.wait_recv()
        t1[1] = p[rows(R, 0), :] + t1[0]
        a4 = send(t1.at[1], fl.at[0], j, 4, R)
        a1.wait_recv()
        t2[1] = p[rows(L, 1), :] + t2[0]
        a5 = send(t2.at[1], fr.at[1], j, 5, L)
        second.append((a2, a3, a4, a5))
        every += [a4, a5]
    shares = []
    for j in range(jobs):
        p, o = ins[j][0], outs[j]
        t1, t2, fl, fr = scratch[j]
        a2, a3, a4, a5 = second[j]
        a3.wait_recv()
        a4.wait_recv()
        finish(j, 0, p[rows(me, 0), :] + fl[0] + fr[0])
        b0 = send(o.at[rows(me, 0)], o.at[rows(me, 0)], j, 6, R)
        c0 = send(o.at[rows(me, 0)], o.at[rows(me, 0)], j, 8, L)
        a2.wait_recv()
        a5.wait_recv()
        finish(j, 1, p[rows(me, 1), :] + fl[1] + fr[1])
        b1 = send(o.at[rows(me, 1)], o.at[rows(me, 1)], j, 7, R)
        c1 = send(o.at[rows(me, 1)], o.at[rows(me, 1)], j, 9, L)
        shares.append((b0, b1, c0, c1))
        every += [b0, b1, c0, c1]
    last = []
    for j in range(jobs):
        o = outs[j]
        b0, b1, c0, c1 = shares[j]
        b0.wait_recv()
        d0 = send(o.at[rows(L, 0)], o.at[rows(L, 0)], j, 10, R)
        c1.wait_recv()
        d1 = send(o.at[rows(R, 1)], o.at[rows(R, 1)], j, 11, L)
        last += [b1, c0, d0, d1]
        every += [d0, d1]
    for copy in last:
        copy.wait_recv()
    for copy in every:
        copy.wait_send()


def ring(jobs, cid):
    kinds = tuple(job[0] for job in jobs)
    arrays = [a for job in jobs for a in job[1:]]
    T, D = jobs[0][1].shape
    H = T // HEADS // 2
    n = len(jobs)
    outs = pl.pallas_call(
        lambda *refs: ring_kernel(kinds, *refs),
        out_shape=tuple(jax.ShapeDtypeStruct((T, D), jnp.float32) for _ in jobs),
        in_specs=[pl.BlockSpec(memory_space=pltpu.VMEM)] * len(arrays),
        out_specs=tuple(pl.BlockSpec(memory_space=pltpu.VMEM) for _ in jobs),
        scratch_shapes=[pltpu.VMEM((2, H, D), jnp.float32)] * (4 * n)
        + [pltpu.SemaphoreType.DMA((n, 12))] * 2,
        compiler_params=pltpu.CompilerParams(
            collective_id=cid, has_side_effects=True, vmem_limit_bytes=32 << 20
        ),
        cost_estimate=pl.CostEstimate(flops=1, bytes_accessed=1, transcendentals=0),
        name=f"ring{cid}",
    )(*arrays)
    return outs


def end_kernel(*refs):
    (dm, toks, gain, d_res, rp, res, g_gate, g_up, g_down, g_in, g_out, small) = refs[:12]
    (o_tok, o_res, o_gate, o_up, o_down, o_in, o_out, o_small) = refs[12:20]
    (yt, yf, S, RC, tA, tB, fA, fB, t2A, t2B, f2A, f2B, sm, sr) = refs[20:34]
    (ys, yr, cs, cr, lc, as_, ar, bs, br, ss, sr_sem) = refs[34:]
    T, D = o_tok.shape
    C = T // HEADS
    H = C // 2
    WA, WB = tA.shape[-1], tB.shape[-1]
    seq = lax.axis_index("seq")
    me = lax.axis_index("head")
    core = lax.rem(seq, 2)
    z = lax.rem(lax.div(seq, 2), 4)
    x = lax.div(seq, 8)

    def ahead(k, n):
        return lax.rem(k + n, 4)

    def at_x(n):
        return {"seq": (ahead(x, n) * 4 + z) * 2 + core, "head": me}

    def at_z(n):
        return {"seq": (x * 4 + ahead(z, n)) * 2 + core, "head": me}

    def at_y(n):
        return {"seq": seq, "head": ahead(me, n)}

    twin = {"seq": (x * 4 + z) * 2 + (1 - core), "head": me}

    barrier = pltpu.get_barrier_semaphore()
    for n in (1, 2, 3):
        for axis in (at_x, at_z, at_y):
            pl.semaphore_signal(barrier, inc=1, device_id=axis(n), device_id_type=MESH)
    pl.semaphore_signal(barrier, inc=1, device_id=twin, device_id_type=MESH)
    pl.semaphore_wait(barrier, 10)

    every = []

    def send(src, dst, s_sem, r_sem, dev):
        copy = pltpu.make_async_remote_copy(
            src_ref=src, dst_ref=dst, send_sem=s_sem, recv_sem=r_sem, device_id=dev, device_id_type=MESH
        )
        copy.start()
        every.append(copy)
        return copy

    def add_up(dst, *srcs):
        n, r = dst.shape[:2]
        q = r // 8

        def body(i, carry):
            b, at = lax.div(i, q), pl.ds(pl.multiple_of(lax.rem(i, q) * 8, 8), 8)
            total = dst[b, at, :]
            for src in srcs:
                total = total + src[b, at, :]
            dst[b, at, :] = total
            return carry

        lax.fori_loop(0, n * q, body, 0)

    steps = []

    def when(time):
        def add(fn):
            steps.append((time, len(steps), fn))
            return fn

        return add

    def y_job(j, p, o, finish, times):
        t1, t2, fl, fr = (yt.at[j, 0], yt.at[j, 1], yf.at[j, 0], yf.at[j, 1])
        R, L, O = ahead(me, 1), ahead(me, 3), ahead(me, 2)
        c = {}

        def rows(k, half):
            return pl.ds(pl.multiple_of(k * C + half * H, H), H)

        def go(name, src, dst, i, n):
            c[name] = send(src, dst, ys.at[j, i], yr.at[j, i], at_y(n))

        @when(times[0])
        def _():
            go("a0", p.at[rows(O, 0)], t1.at[0], 0, 1)
            go("a1", p.at[rows(O, 1)], t2.at[0], 1, 3)
            go("a2", p.at[rows(R, 1)], fl.at[1], 2, 1)
            go("a3", p.at[rows(L, 0)], fr.at[0], 3, 3)

        @when(times[1])
        def _():
            c["a0"].wait_recv()
            t1[1] = p[rows(R, 0), :] + t1[0]
            go("a4", t1.at[1], fl.at[0], 4, 1)
            c["a1"].wait_recv()
            t2[1] = p[rows(L, 1), :] + t2[0]
            go("a5", t2.at[1], fr.at[1], 5, 3)

        @when(times[2])
        def _():
            c["a3"].wait_recv()
            c["a4"].wait_recv()
            o[rows(me, 0), :] = finish(0, p[rows(me, 0), :] + fl[0] + fr[0])
            go("b0", o.at[rows(me, 0)], o.at[rows(me, 0)], 6, 1)
            go("c0", o.at[rows(me, 0)], o.at[rows(me, 0)], 8, 3)
            c["a2"].wait_recv()
            c["a5"].wait_recv()
            o[rows(me, 1), :] = finish(1, p[rows(me, 1), :] + fl[1] + fr[1])
            go("c1", o.at[rows(me, 1)], o.at[rows(me, 1)], 9, 3)
            go("b1", o.at[rows(me, 1)], o.at[rows(me, 1)], 7, 1)

        @when(times[3])
        def _():
            c["b0"].wait_recv()
            go("d0", o.at[rows(L, 0)], o.at[rows(L, 0)], 10, 1)
            c["c1"].wait_recv()
            go("d1", o.at[rows(R, 1)], o.at[rows(R, 1)], 11, 3)

        @when(900)
        def _():
            for name in ("b1", "c0", "d0", "d1"):
                c[name].wait_recv()

    def finish_tokens(half, total):
        mine = pl.ds(half * H, H)
        return norm_back_rows(total, toks[mine, :].astype(jnp.float32), gain[...], d_res[mine, :])

    def finish_result(half, total):
        return total + res[pl.ds(half * H, H), :]

    y_job(0, dm, o_tok, finish_tokens, (0, 9, 20, 35))
    y_job(1, rp, o_res, finish_result, (0, 14, 27, 45))

    A = [(g_gate, 0, WA // 2), (g_up, WA // 2, WA // 2)]
    B = [(g_down, 0, 1152)] + [(g_in.at[k], 1152 + 256 * k, 256) for k in range(3)] + [(g_out, 1920, 256)]
    pairs = {}

    def cut(ref, which, k):
        return ref.at[k] if which == "A" else ref.at[:, k]

    def offer(which, turn, k, base):
        pieces, offset = (A, 0) if which == "A" else (B, WA)
        got = []
        for i, (g, at, w) in enumerate(pieces):
            n = base + i
            cols = pl.ds(offset + at, w)
            src = cut(g, which, k)
            mine = pltpu.make_async_copy(src.at[:, core], cut(S, which, k).at[:, :, cols], lc.at[n])
            mine.start()
            other = send(src.at[:, 1 - core], cut(RC, which, k).at[:, :, cols], cs.at[n], cr.at[n], twin)
            got.append((mine, other))
        pairs[which, turn] = got
        return base + len(pieces)

    pos = {"A": x, "B": z}
    turns = [("A", 2), ("B", 2), ("A", 1), ("B", 1), ("A", 3), ("B", 3), ("A", 0), ("B", 0)]

    @when(0)
    def _():
        base = 0
        for which, turn in turns:
            base = offer(which, turn, ahead(pos[which], turn), base)

    def half_cols(which):
        return pl.ds(0, WA) if which == "A" else pl.ds(WA, WB)

    def settle(which, turn):
        for mine, other in pairs[which, turn]:
            mine.wait()
            other.wait_recv()
        k = ahead(pos[which], turn)
        cols = half_cols(which)
        add_up(cut(S, which, k).at[:, :, cols], cut(RC, which, k).at[:, :, cols])

    def ring_of(chunk, t, f, s_sem, r_sem, base, to, tag, times, settle_at, done):
        c = {}

        def go(name, src, dst, i, n):
            c[name] = send(src, dst, s_sem.at[base + i], r_sem.at[base + i], to(n))

        @when(times[0])
        def _():
            settle_at(2)
            go("a0", chunk(2, 0), t.at[0], 0, 1)
            go("a1", chunk(2, 1), t.at[1], 1, 3)

        @when(times[1])
        def _():
            settle_at(1)
            go("a2", chunk(1, 1), f.at[0, 1], 2, 1)
            settle_at(3)
            go("a3", chunk(3, 0), f.at[1, 0], 3, 3)

        @when(times[2])
        def _():
            c["a0"].wait_recv()
            add_up(t.at[0], chunk(1, 0))
            go("a4", t.at[0], f.at[0, 0], 4, 1)
            c["a1"].wait_recv()
            add_up(t.at[1], chunk(3, 1))
            go("a5", t.at[1], f.at[1, 1], 5, 3)

        @when(times[3])
        def _():
            settle_at(0)

        @when(times[4])
        def _():
            c["a3"].wait_recv()
            c["a4"].wait_recv()
            add_up(chunk(0, 0), f.at[0, 0], f.at[1, 0])
            c["a2"].wait_recv()
            c["a5"].wait_recv()
            add_up(chunk(0, 1), f.at[0, 1], f.at[1, 1])
            done()

    def chunk1(which):
        def chunk(turn, half):
            k = ahead(pos[which], turn)
            return cut(S, which, k).at[pl.ds(half * 2, 2), :, half_cols(which)]

        return chunk

    def chunk2(which):
        def chunk(turn, half):
            k = ahead(z if which == "A" else x, turn)
            mine = cut(S, which, pos[which])
            return mine.at[pl.ds(k, 1), pl.ds(half * 16, 16), half_cols(which)]

        return chunk

    nothing = lambda *a: None
    ring_of(chunk1("A"), tA, fA, as_, ar, 0, at_x, "A", (1, 5, 15, 12, 33), lambda n: settle("A", n), nothing)
    ring_of(chunk1("B"), tB, fB, bs, br, 0, at_z, "B", (2, 6, 16, 13, 34), lambda n: settle("B", n), nothing)

    def out_A():
        rows = S[x, z, :, pl.ds(0, WA)]
        o_gate[...] = rows[:, : WA // 2]
        o_up[...] = rows[:, WA // 2 :]

    def out_B():
        rows = S[x, z, :, pl.ds(WA, WB)]
        o_down[...] = rows[:, :1152]
        for k in range(3):
            o_in[k] = rows[:, 1152 + 256 * k : 1408 + 256 * k]
        o_out[...] = rows[:, 1920:]

    ring_of(chunk2("A"), t2A, f2A, as_, ar, 6, at_z, "A2", (36, 37, 41, 42, 48), nothing, out_A)
    ring_of(chunk2("B"), t2B, f2B, bs, br, 6, at_x, "B2", (38, 39, 43, 44, 49), nothing, out_B)

    axes = [(at_z, z, 5), (at_x, x, 10), (at_y, me, 16)]
    first = {}

    @when(0.5)
    def _():
        first["c"] = send(small, sr.at[3, 0], ss.at[9], sr_sem.at[9], twin)

    @when(4.5)
    def _():
        first["c"].wait_recv()
        sm[0] = small[...] + sr[3, 0]

    for a, (to, here, time) in enumerate(axes):
        copies = []

        def begin(a=a, to=to, here=here, copies=copies):
            sr[a, here] = sm[a]
            for n in (1, 2, 3):
                copies.append(send(sm.at[a], sr.at[a, here], ss.at[a * 3 + n - 1], sr_sem.at[a * 3 + n - 1], to(n)))

        def end(a=a, copies=copies):
            for copy in copies:
                copy.wait_recv()
            total = (sr[a, 0] + sr[a, 1]) + (sr[a, 2] + sr[a, 3])
            if a < 2:
                sm[a + 1] = total
            else:
                o_small[0:8] = total[0:8]
                o_small[8:16] = sm[2][8:16]

        when(time)(begin)
        when(time + 4)(end)

    for _, _, fn in sorted(steps, key=lambda s: s[:2]):
        fn()
    for copy in every:
        copy.wait_send()


def finish_all(dm, toks, gain, d_res, rp, res, gate, up, down, inw, outw, small):
    T, D = dm.shape
    H = T // HEADS // 2
    wa = gate.shape[1] + up.shape[1]
    wb = down.shape[1] + inw.shape[0] * inw.shape[2] + outw.shape[1]
    f32 = jnp.float32

    def blocks(g):
        return g.reshape(*g.shape[:-2], 4, 4, 2, 32, g.shape[-1])

    vmem = pl.BlockSpec(memory_space=pltpu.VMEM)
    anywhere = pl.BlockSpec(memory_space=pl.ANY)
    shape = jax.ShapeDtypeStruct
    dma = pltpu.SemaphoreType.DMA
    return pl.pallas_call(
        end_kernel,
        out_shape=(
            shape((T, D), f32),
            shape((T, D), f32),
            shape((32, gate.shape[1]), f32),
            shape((32, up.shape[1]), f32),
            shape((32, down.shape[1]), f32),
            shape((3, 32, inw.shape[2]), f32),
            shape((32, outw.shape[1]), f32),
            shape((16, 256), f32),
        ),
        in_specs=[vmem] * 6 + [anywhere] * 5 + [vmem],
        out_specs=(vmem,) * 8,
        scratch_shapes=[
            pltpu.VMEM((2, 2, 2, H, D), f32),
            pltpu.VMEM((2, 2, 2, H, D), f32),
            pltpu.VMEM((4, 4, 32, wa + wb), f32),
            pltpu.VMEM((4, 4, 32, wa + wb), f32),
            pltpu.VMEM((2, 2, 32, wa), f32),
            pltpu.VMEM((2, 2, 32, wb), f32),
            pltpu.VMEM((2, 2, 2, 32, wa), f32),
            pltpu.VMEM((2, 2, 2, 32, wb), f32),
            pltpu.VMEM((2, 1, 16, wa), f32),
            pltpu.VMEM((2, 1, 16, wb), f32),
            pltpu.VMEM((2, 2, 1, 16, wa), f32),
            pltpu.VMEM((2, 2, 1, 16, wb), f32),
            pltpu.VMEM((3, 16, 256), f32),
            pltpu.VMEM((4, 4, 16, 256), f32),
            dma((2, 12)),
            dma((2, 12)),
            dma((28,)),
            dma((28,)),
            dma((28,)),
            dma((12,)),
            dma((12,)),
            dma((12,)),
            dma((12,)),
            dma((10,)),
            dma((10,)),
        ],
        compiler_params=pltpu.CompilerParams(
            collective_id=7, has_side_effects=True, vmem_limit_bytes=50 << 20
        ),
        cost_estimate=pl.CostEstimate(flops=1, bytes_accessed=1, transcendentals=0),
        name="end",
    )(dm, toks, gain, d_res, rp, res, *map(blocks, (gate, up, down, inw, outw)), small)


def from_behind(block, axis, distance):
    devices = range(lax.axis_size(axis))
    route = [(i - distance, i) for i in devices if i - distance in devices]
    return lax.ppermute(block, axis, route)


def rms_scale(values):
    return lax.rsqrt(jnp.mean(values * values, axis=-1, keepdims=True) + EPS)


def right_product(left, right):
    return lax.dot_general(
        left, right, (((1,), (1,)), ((), ())), preferred_element_type=jnp.float32
    )


def token_product(left, right):
    return lax.dot_general(
        left, right, (((0,), (0,)), ((), ())), preferred_element_type=jnp.float32
    )


def on_device(
    tokens,
    segment_ids,
    mix_gain,
    in_weight,
    conv_weight,
    out_weight,
    ffn_gain,
    gate_weight,
    up_weight,
    down_weight,
    cotangent,
):
    tok_rows = tokens.shape[0]
    own = tok_rows // HEADS
    own_at = lax.axis_index("head") * own

    def own_rows(x):
        return lax.dynamic_slice_in_dim(x, own_at, own, 0)

    first_row = lax.axis_index("seq") * tok_rows
    padded_ids = jnp.concatenate(
        [jnp.full((2,), -1, jnp.int32), segment_ids, jnp.full((2,), -2, jnp.int32)]
    )
    id_window = lax.dynamic_slice_in_dim(padded_ids, first_row, tok_rows + 4)
    near_ext = (id_window[2 : tok_rows + 4] == id_window[1 : tok_rows + 3]).astype(jnp.float32)
    far_ext = (id_window[2 : tok_rows + 4] == id_window[0 : tok_rows + 2]).astype(jnp.float32)
    near_own = near_ext[:tok_rows, None]
    far_own = far_ext[:tok_rows, None]
    inputs = tokens.astype(jnp.float32)
    mix_scale = rms_scale(inputs)
    mix_normed = (inputs * mix_scale * mix_gain).astype(jnp.bfloat16)
    projected = jnp.einsum("td,dkc->tkc", mix_normed, in_weight, preferred_element_type=jnp.float32)
    chan_b = projected[:, 0]
    chan_c = projected[:, 1]
    chan_x = projected[:, 2]
    mixed = chan_b * chan_x
    edge_rows = from_behind(mixed[tok_rows - 2 :], "seq", 1)
    extended = jnp.concatenate([edge_rows, mixed])
    kernel = conv_weight.astype(jnp.float32)
    prev_one = extended[1 : tok_rows + 1]
    prev_two = extended[0:tok_rows]
    conv_out = kernel[0] * mixed + kernel[1] * near_own * prev_one + kernel[2] * far_own * prev_two
    gated = (chan_c * conv_out).astype(jnp.bfloat16)
    (resid,) = ring([("add", right_product(gated, out_weight), own_rows(tokens))], 1)
    ffn_scale = rms_scale(resid)
    ffn_normed = (resid * ffn_scale * ffn_gain).astype(jnp.bfloat16)
    gate = jnp.dot(ffn_normed, gate_weight, preferred_element_type=jnp.float32)
    upper = jnp.dot(ffn_normed, up_weight, preferred_element_type=jnp.float32)
    sigma = jax.nn.sigmoid(gate)
    act = (gate * sigma * upper).astype(jnp.bfloat16)
    d_act = jnp.dot(cotangent, down_weight, preferred_element_type=jnp.float32)
    d_gate = (d_act * upper * sigma * (1.0 + gate * (1.0 - sigma))).astype(jnp.bfloat16)
    d_up = (d_act * gate * sigma).astype(jnp.bfloat16)
    grad_down = token_product(cotangent, act)
    grad_gate = token_product(ffn_normed, d_gate)
    grad_up = token_product(ffn_normed, d_up)
    d_normed_part = right_product(d_gate, gate_weight) + right_product(d_up, up_weight)
    grad_ffn_gain = jnp.sum(d_normed_part * resid * ffn_scale, axis=0)
    d_normed_part, _, _, _ = lax.optimization_barrier((d_normed_part, grad_down, grad_gate, grad_up))
    (d_resid,) = ring(
        [("norm", d_normed_part, own_rows(resid), ffn_gain[None], own_rows(cotangent))], 2
    )
    d_resid_low = d_resid.astype(jnp.bfloat16)
    d_gated = jnp.dot(d_resid_low, out_weight, preferred_element_type=jnp.float32)
    grad_out = token_product(d_resid_low, gated)
    d_chan_c = d_gated * conv_out
    d_conv = d_gated * chan_c
    tail_rows = from_behind(d_conv[:2], "seq", -1)
    later = jnp.concatenate([d_conv, tail_rows])
    next_one = later[1 : tok_rows + 1]
    next_two = later[2 : tok_rows + 2]
    near_next = near_ext[1 : tok_rows + 1, None]
    far_next = far_ext[2 : tok_rows + 2, None]
    d_mixed = kernel[0] * d_conv + kernel[1] * near_next * next_one + kernel[2] * far_next * next_two
    grad_conv = jnp.stack(
        [
            jnp.sum(d_conv * mixed, axis=0),
            jnp.sum(d_conv * near_own * prev_one, axis=0),
            jnp.sum(d_conv * far_own * prev_two, axis=0),
        ]
    )
    d_projected = jnp.stack([d_mixed * chan_x, d_chan_c, d_mixed * chan_b], axis=1).astype(
        jnp.bfloat16
    )
    grad_in = jnp.einsum("td,tkc->kdc", mix_normed, d_projected, preferred_element_type=jnp.float32)
    d_mix_part = jnp.einsum(
        "tkc,dkc->td", d_projected, in_weight, preferred_element_type=jnp.float32
    )
    grad_mix_gain = jnp.sum(d_mix_part * inputs * mix_scale, axis=0)
    small = jnp.concatenate(
        [
            grad_mix_gain.reshape(4, 256),
            grad_ffn_gain.reshape(4, 256),
            grad_conv,
            jnp.zeros((5, 256), jnp.float32),
        ]
    )
    result_part = right_product(act, down_weight)
    grad_tokens, result, gate_share, up_share, down_share, in_share, out_share, totals = finish_all(
        d_mix_part,
        own_rows(tokens),
        mix_gain[None],
        own_rows(d_resid),
        result_part,
        own_rows(resid),
        grad_gate,
        grad_up,
        grad_down,
        grad_in,
        grad_out,
        small,
    )
    return (
        result.astype(jnp.bfloat16),
        grad_tokens,
        totals[0:4].reshape(1024),
        in_share.transpose(1, 0, 2),
        totals[8:11],
        out_share,
        totals[4:8].reshape(1024),
        gate_share,
        up_share,
        down_share,
    )


def solution(mesh):
    placed = (
        P("seq", None),
        P(),
        P(),
        P(None, None, "head"),
        P(None, "head"),
        P(None, "head"),
        P(),
        P(None, "head"),
        P(None, "head"),
        P(None, "head"),
        P("seq", None),
    )
    return jax.shard_map(
        on_device,
        mesh=mesh,
        in_specs=placed,
        out_specs=(
            P("seq", None),
            P("seq", None),
            P(),
            P("seq", None, "head"),
            P(None, "head"),
            P("seq", "head"),
            P(),
            P("seq", "head"),
            P("seq", "head"),
            P("seq", "head"),
        ),
        check_vma=False,
    )
```

```python
import jax
import jax.numpy as jnp
from jax import lax
from jax.experimental import pallas as pl
from jax.experimental.pallas import tpu as pltpu
from jax.sharding import PartitionSpec as P

EPS = 1e-05
MESH = pl.DeviceIdType.MESH
HEADS = 4


def norm_back_rows(grad_normed, values, gain, extra):
    scale = lax.rsqrt(jnp.mean(values * values, axis=-1, keepdims=True) + EPS)
    weighted = grad_normed * gain
    inner = jnp.mean(weighted * values, axis=-1, keepdims=True)
    return extra + (scale * weighted - values * (scale * scale * scale) * inner)


def ring_kernel(kinds, *refs):
    jobs = len(kinds)
    at = 0
    ins = []
    for kind in kinds:
        n = 4 if kind == "norm" else 2
        ins.append(refs[at : at + n])
        at += n
    outs = refs[at : at + jobs]
    at += jobs
    scratch = [refs[at + 4 * j : at + 4 * j + 4] for j in range(jobs)]
    s_sem, r_sem = refs[at + 4 * jobs : at + 4 * jobs + 2]
    T = outs[0].shape[0]
    C = T // HEADS
    H = C // 2

    me = lax.axis_index("head")
    R = lax.rem(me + 1, HEADS)
    L = lax.rem(me + HEADS - 1, HEADS)
    O = lax.rem(me + 2, HEADS)
    barrier = pltpu.get_barrier_semaphore()
    for other in (R, L):
        pl.semaphore_signal(barrier, inc=1, device_id={"head": other}, device_id_type=MESH)
    pl.semaphore_wait(barrier, 2)

    def rows(k, half):
        return pl.ds(pl.multiple_of(k * C + half * H, H), H)

    def send(src, dst, job, i, dev):
        copy = pltpu.make_async_remote_copy(
            src_ref=src,
            dst_ref=dst,
            send_sem=s_sem.at[job, i],
            recv_sem=r_sem.at[job, i],
            device_id={"head": dev},
            device_id_type=MESH,
        )
        copy.start()
        return copy

    def finish(job, half, total):
        kind = kinds[job]
        mine = pl.ds(half * H, H)
        if kind == "norm":
            _, values, gain, extra = ins[job]
            total = norm_back_rows(
                total, values[mine, :].astype(jnp.float32), gain[...], extra[mine, :].astype(jnp.float32)
            )
        else:
            total = total + ins[job][1][mine, :].astype(jnp.float32)
        outs[job][rows(me, half), :] = total

    every = []
    live = []
    for j in range(jobs):
        p = ins[j][0]
        t1, t2, fl, fr = scratch[j]
        a0 = send(p.at[rows(O, 0)], t1.at[0], j, 0, R)
        a1 = send(p.at[rows(O, 1)], t2.at[0], j, 1, L)
        a2 = send(p.at[rows(R, 1)], fl.at[1], j, 2, R)
        a3 = send(p.at[rows(L, 0)], fr.at[0], j, 3, L)
        live.append((a0, a1, a2, a3))
        every += [a0, a1, a2, a3]
    second = []
    for j in range(jobs):
        p = ins[j][0]
        t1, t2, fl, fr = scratch[j]
        a0, a1, a2, a3 = live[j]
        a0.wait_recv()
        t1[1] = p[rows(R, 0), :] + t1[0]
        a4 = send(t1.at[1], fl.at[0], j, 4, R)
        a1.wait_recv()
        t2[1] = p[rows(L, 1), :] + t2[0]
        a5 = send(t2.at[1], fr.at[1], j, 5, L)
        second.append((a2, a3, a4, a5))
        every += [a4, a5]
    shares = []
    for j in range(jobs):
        p, o = ins[j][0], outs[j]
        t1, t2, fl, fr = scratch[j]
        a2, a3, a4, a5 = second[j]
        a3.wait_recv()
        a4.wait_recv()
        finish(j, 0, p[rows(me, 0), :] + fl[0] + fr[0])
        b0 = send(o.at[rows(me, 0)], o.at[rows(me, 0)], j, 6, R)
        c0 = send(o.at[rows(me, 0)], o.at[rows(me, 0)], j, 8, L)
        a2.wait_recv()
        a5.wait_recv()
        finish(j, 1, p[rows(me, 1), :] + fl[1] + fr[1])
        b1 = send(o.at[rows(me, 1)], o.at[rows(me, 1)], j, 7, R)
        c1 = send(o.at[rows(me, 1)], o.at[rows(me, 1)], j, 9, L)
        shares.append((b0, b1, c0, c1))
        every += [b0, b1, c0, c1]
    last = []
    for j in range(jobs):
        o = outs[j]
        b0, b1, c0, c1 = shares[j]
        b0.wait_recv()
        d0 = send(o.at[rows(L, 0)], o.at[rows(L, 0)], j, 10, R)
        c1.wait_recv()
        d1 = send(o.at[rows(R, 1)], o.at[rows(R, 1)], j, 11, L)
        last += [b1, c0, d0, d1]
        every += [d0, d1]
    for copy in last:
        copy.wait_recv()
    for copy in every:
        copy.wait_send()


def ring(jobs, cid):
    kinds = tuple(job[0] for job in jobs)
    arrays = [a for job in jobs for a in job[1:]]
    T, D = jobs[0][1].shape
    H = T // HEADS // 2
    n = len(jobs)
    outs = pl.pallas_call(
        lambda *refs: ring_kernel(kinds, *refs),
        out_shape=tuple(jax.ShapeDtypeStruct((T, D), jnp.float32) for _ in jobs),
        in_specs=[pl.BlockSpec(memory_space=pltpu.VMEM)] * len(arrays),
        out_specs=tuple(pl.BlockSpec(memory_space=pltpu.VMEM) for _ in jobs),
        scratch_shapes=[pltpu.VMEM((2, H, D), jnp.float32)] * (4 * n)
        + [pltpu.SemaphoreType.DMA((n, 12))] * 2,
        compiler_params=pltpu.CompilerParams(
            collective_id=cid, has_side_effects=True, vmem_limit_bytes=32 << 20
        ),
        cost_estimate=pl.CostEstimate(flops=1, bytes_accessed=1, transcendentals=0),
        name=f"ring{cid}",
    )(*arrays)
    return outs


class Comm:
    def __init__(self):
        seq = lax.axis_index("seq")
        self.me = lax.axis_index("head")
        self.core = lax.rem(seq, 2)
        self.z = lax.rem(lax.div(seq, 2), 4)
        self.x = lax.div(seq, 8)
        self.every = []
        self.steps = []

    def at_x(self, n):
        return {"seq": (ahead(self.x, n) * 4 + self.z) * 2 + self.core, "head": self.me}

    def at_z(self, n):
        return {"seq": (self.x * 4 + ahead(self.z, n)) * 2 + self.core, "head": self.me}

    def at_y(self, n):
        return {"seq": (self.x * 4 + self.z) * 2 + self.core, "head": ahead(self.me, n)}

    def twin(self, n=1):
        return {"seq": (self.x * 4 + self.z) * 2 + (1 - self.core), "head": self.me}

    def greet(self, devices):
        barrier = pltpu.get_barrier_semaphore()
        for device in devices:
            pl.semaphore_signal(barrier, inc=1, device_id=device, device_id_type=MESH)
        pl.semaphore_wait(barrier, len(devices))

    def send(self, src, dst, s_sem, r_sem, dev):
        copy = pltpu.make_async_remote_copy(
            src_ref=src, dst_ref=dst, send_sem=s_sem, recv_sem=r_sem, device_id=dev, device_id_type=MESH
        )
        copy.start()
        self.every.append(copy)
        return copy

    def when(self, time):
        def add(fn):
            self.steps.append((time, len(self.steps), fn))
            return fn

        return add

    def run(self):
        for _, _, fn in sorted(self.steps, key=lambda s: s[:2]):
            fn()
        for copy in self.every:
            copy.wait_send()


def ahead(k, n):
    return lax.rem(k + n, 4)


def add_up(dst, *srcs):
    n, r = dst.shape[:2]
    q = r // 8

    def body(i, carry):
        b, at = lax.div(i, q), pl.ds(pl.multiple_of(lax.rem(i, q) * 8, 8), 8)
        total = dst[b, at, :]
        for src in srcs:
            total = total + src[b, at, :]
        dst[b, at, :] = total
        return carry

    lax.fori_loop(0, n * q, body, 0)


def head_sum(cm, p, o, t, f, s_sem, r_sem, finish, times, closing):
    T = o.shape[0]
    C = T // 4
    H = C // 2
    R, L, O = ahead(cm.me, 1), ahead(cm.me, 3), ahead(cm.me, 2)
    me = cm.me
    c = {}

    def rows(k, half):
        return pl.ds(pl.multiple_of(k * C + half * H, H), H)

    def go(name, src, dst, i, n):
        c[name] = cm.send(src, dst, s_sem.at[i], r_sem.at[i], cm.at_y(n))

    @cm.when(times[0])
    def _():
        go("a0", p.at[rows(O, 0)], t.at[0], 0, 1)
        go("a1", p.at[rows(O, 1)], t.at[1], 1, 3)
        go("a2", p.at[rows(R, 1)], f.at[0, 1], 2, 1)
        go("a3", p.at[rows(L, 0)], f.at[1, 0], 3, 3)

    @cm.when(times[1])
    def _():
        c["a0"].wait_recv()
        t[0] = p[rows(R, 0), :] + t[0]
        go("a4", t.at[0], f.at[0, 0], 4, 1)
        c["a1"].wait_recv()
        t[1] = p[rows(L, 1), :] + t[1]
        go("a5", t.at[1], f.at[1, 1], 5, 3)

    @cm.when(times[2])
    def _():
        c["a3"].wait_recv()
        c["a4"].wait_recv()
        o[rows(me, 0), :] = finish(0, p[rows(me, 0), :] + f[0, 0] + f[1, 0])
        go("b0", o.at[rows(me, 0)], o.at[rows(me, 0)], 6, 1)
        go("c0", o.at[rows(me, 0)], o.at[rows(me, 0)], 8, 3)
        c["a2"].wait_recv()
        c["a5"].wait_recv()
        o[rows(me, 1), :] = finish(1, p[rows(me, 1), :] + f[0, 1] + f[1, 1])
        go("c1", o.at[rows(me, 1)], o.at[rows(me, 1)], 9, 3)
        go("b1", o.at[rows(me, 1)], o.at[rows(me, 1)], 7, 1)

    @cm.when(times[3])
    def _():
        c["b0"].wait_recv()
        go("d0", o.at[rows(L, 0)], o.at[rows(L, 0)], 10, 1)
        c["c1"].wait_recv()
        go("d1", o.at[rows(R, 1)], o.at[rows(R, 1)], 11, 3)

    @cm.when(900)
    def _():
        for name in ("b1", "c0", "d0", "d1"):
            c[name].wait_recv()
        closing()


def scatter_ring(cm, chunk, t, f, s_sem, r_sem, base, to, times, done):
    c = {}

    def go(name, src, dst, i, n):
        c[name] = cm.send(src, dst, s_sem.at[base + i], r_sem.at[base + i], to(n))

    @cm.when(times[0])
    def _():
        go("a0", chunk(2, 0), t.at[0], 0, 1)
        go("a1", chunk(2, 1), t.at[1], 1, 3)

    @cm.when(times[1])
    def _():
        go("a2", chunk(1, 1), f.at[0, 1], 2, 1)

    @cm.when(times[2])
    def _():
        go("a3", chunk(3, 0), f.at[1, 0], 3, 3)

    @cm.when(times[3])
    def _():
        c["a0"].wait_recv()
        add_up(t.at[0], chunk(1, 0))
        go("a4", t.at[0], f.at[0, 0], 4, 1)
        c["a1"].wait_recv()
        add_up(t.at[1], chunk(3, 1))
        go("a5", t.at[1], f.at[1, 1], 5, 3)

    @cm.when(times[4])
    def _():
        c["a3"].wait_recv()
        c["a4"].wait_recv()
        add_up(chunk(0, 0), f.at[0, 0], f.at[1, 0])
        c["a2"].wait_recv()
        c["a5"].wait_recv()
        add_up(chunk(0, 1), f.at[0, 1], f.at[1, 1])
        done()


def grad_scatter(cm, products, G, RC, wa, bufs, sems, times, done_a, done_b):
    tA, tB, fA, fB, t2A, t2B, f2A, f2B = bufs
    cs, cr, as_, ar, bs, br = sems
    W = G.shape[-1]
    quarter = products[0][0].shape[1] // 4
    got = {}

    def block(turn):
        k = ahead(cm.x, turn)
        for left, rights, at in products:
            right = jnp.concatenate([r[...] for r in rights], axis=1)
            w = right.shape[1]
            lhs = left[:, pl.ds(pl.multiple_of(k * quarter, quarter), quarter)]
            value = lax.dot_general(
                lhs, right, (((0,), (0,)), ((), ())), preferred_element_type=jnp.float32
            )
            G[k, :, :, :, pl.ds(at, w)] = value.reshape(4, 2, 32, w)
        got[turn] = cm.send(G.at[k, :, 1 - cm.core], RC.at[k], cs.at[turn], cr.at[turn], cm.twin())

    def settle(turn):
        k = ahead(cm.x, turn)
        got[turn].wait_recv()
        add_up(G.at[k, :, cm.core], RC.at[k])

    for i, turn in enumerate((2, 1, 3, 0)):
        cm.when(times["block"][i])(lambda turn=turn: block(turn))
        cm.when(times["settle"][i])(lambda turn=turn: settle(turn))

    cols_a, cols_b = pl.ds(0, wa), pl.ds(wa, W - wa)
    core = cm.core

    def a1(turn, half):
        return G.at[ahead(cm.x, turn), pl.ds(half * 2, 2), core, :, cols_a]

    def b1(turn, half):
        return G.at[pl.ds(half * 2, 2), ahead(cm.z, turn), core, :, cols_b]

    def a2(turn, half):
        return G.at[cm.x, pl.ds(ahead(cm.z, turn), 1), core, pl.ds(half * 16, 16), cols_a]

    def b2(turn, half):
        return G.at[pl.ds(ahead(cm.x, turn), 1), cm.z, core, pl.ds(half * 16, 16), cols_b]

    nothing = lambda: None
    scatter_ring(cm, a1, tA, fA, as_, ar, 0, cm.at_x, times["A"], nothing)
    scatter_ring(cm, b1, tB, fB, bs, br, 0, cm.at_z, times["B"], nothing)
    scatter_ring(cm, a2, t2A, f2A, as_, ar, 6, cm.at_z, times["A2"], done_a)
    scatter_ring(cm, b2, t2B, f2B, bs, br, 6, cm.at_x, times["B2"], done_b)


def small_sums(cm, small, sm, sr, s_sem, r_sem, times, done):
    axes = [(cm.at_z, cm.z), (cm.at_x, cm.x), (cm.at_y, cm.me)]
    first = {}

    @cm.when(times[0])
    def _():
        first["c"] = cm.send(small, sr.at[3, 0], s_sem.at[9], r_sem.at[9], cm.twin())

    @cm.when(times[1])
    def _():
        first["c"].wait_recv()
        sm[0] = small[...] + sr[3, 0]

    for a, (to, here) in enumerate(axes):
        copies = []

        def begin(a=a, to=to, here=here, copies=copies):
            sr[a, here] = sm[a]
            for n in (1, 2, 3):
                i = a * 3 + n - 1
                copies.append(cm.send(sm.at[a], sr.at[a, here], s_sem.at[i], r_sem.at[i], to(n)))

        def end(a=a, copies=copies):
            for copy in copies:
                copy.wait_recv()
            total = (sr[a, 0] + sr[a, 1]) + (sr[a, 2] + sr[a, 3])
            if a < 2:
                sm[a + 1] = total
            else:
                done(total[0:16], sm[2][16:24])

        cm.when(times[1] + 0.01)(begin) if a == 0 else cm.when(times[1 + a] + 0.01)(begin)
        cm.when(times[2 + a])(end)


def greet_all(cm):
    cm.greet([axis(n) for n in (1, 2, 3) for axis in (cm.at_x, cm.at_z, cm.at_y)] + [cm.twin()])


def middle_kernel(*refs):
    (dn, own_resid, gain, own_cot, normed, d_gate, d_up, act, cot, down) = refs[:10]
    (o_dres, o_res, o_gate, o_up, o_down) = refs[10:15]
    (rp, full, yt, yf, G, RC) = refs[15:21]
    bufs, (ys, yr), sems = refs[21:29], refs[29:31], refs[31:]
    H = own_resid.shape[0] // 2
    cm = Comm()
    greet_all(cm)

    def finish_dres(half, total):
        mine = pl.ds(half * H, H)
        return norm_back_rows(total, own_resid[mine, :], gain[...], own_cot[mine, :].astype(jnp.float32))

    def finish_result(half, total):
        return total + own_resid[pl.ds(half * H, H), :]

    def rounded():
        o_res[...] = full[...].astype(jnp.bfloat16)

    @cm.when(13)
    def _():
        n = act.shape[0] // 4

        def body(i, carry):
            rows = pl.ds(pl.multiple_of(i * n, n), n)
            rp[rows, :] = lax.dot_general(
                act[rows, :], down[...], (((1,), (1,)), ((), ())), preferred_element_type=jnp.float32
            )
            return carry

        lax.fori_loop(0, 4, body, 0)

    head_sum(cm, dn, o_dres, yt.at[0], yf.at[0], ys.at[0], yr.at[0], finish_dres, (0, 6.5, 17, 30), lambda: None)
    head_sum(cm, rp, full, yt.at[1], yf.at[1], ys.at[1], yr.at[1], finish_result, (16, 25, 35, 49), rounded)

    w = act.shape[1]
    wa = 1792

    def done_a():
        rows = G[cm.x, cm.z, cm.core, :, pl.ds(0, wa)]
        o_gate[...] = rows[:, :w]
        o_up[:, pl.ds(0, wa - w)] = rows[:, w:]

    def done_b():
        rows = G[cm.x, cm.z, cm.core, :, pl.ds(wa, 3 * w - wa)]
        o_up[:, pl.ds(wa - w, 2 * w - wa)] = rows[:, : 2 * w - wa]
        o_down[...] = rows[:, 2 * w - wa :]

    times = {
        "block": (0.1, 3, 6, 9),
        "settle": (3.3, 6.3, 9.3, 12),
        "A": (3.4, 6.4, 9.4, 14.5, 33),
        "B": (12.1, 12.2, 12.3, 22, 40),
        "A2": (33.1, 33.2, 33.3, 37, 42.5),
        "B2": (40.1, 40.2, 40.3, 44, 50),
    }
    products = [(normed, [d_gate], 0), (normed, [d_up], w), (cot, [act], 2 * w)]
    grad_scatter(cm, products, G, RC, wa, bufs, sems, times, done_a, done_b)
    cm.run()


def end_kernel(*refs):
    (dm, toks, gain, d_res, normed) = refs[:5]
    d_proj = refs[5:8]
    (d_low, gated, small) = refs[8:11]
    (o_tok, o_in, o_out, o_mix, o_ffn, o_conv) = refs[11:17]
    (yt, yf, G, RC) = refs[17:21]
    bufs = refs[21:29]
    sm, sr = refs[29:31]
    ys, yr = refs[31:33]
    sems = refs[33:39]
    ss, sr_sem = refs[39:]
    H = toks.shape[0] // 2
    cm = Comm()
    greet_all(cm)

    def finish_tokens(half, total):
        mine = pl.ds(half * H, H)
        return norm_back_rows(total, toks[mine, :].astype(jnp.float32), gain[...], d_res[mine, :])

    head_sum(cm, dm, o_tok, yt, yf, ys, yr, finish_tokens, (0, 6.5, 17, 26), lambda: None)

    wa = 512

    def done_a():
        rows = G[cm.x, cm.z, cm.core, :, pl.ds(0, wa)]
        o_in[0] = rows[:, :256]
        o_in[1] = rows[:, 256:]

    def done_b():
        rows = G[cm.x, cm.z, cm.core, :, pl.ds(wa, 512)]
        o_in[2] = rows[:, :256]
        o_out[...] = rows[:, 256:]

    times = {
        "block": (0.1, 1, 2, 3),
        "settle": (1.5, 2.5, 3.5, 4.5),
        "A": (1.6, 2.6, 3.6, 6, 14),
        "B": (4.6, 4.7, 4.8, 8.5, 16),
        "A2": (14.1, 14.2, 14.3, 17.2, 20),
        "B2": (16.1, 16.2, 16.3, 18.5, 21),
    }
    products = [(normed, d_proj, 0), (d_low, [gated], 768)]
    grad_scatter(cm, products, G, RC, wa, bufs, sems, times, done_a, done_b)

    def small_done(gains, rest):
        o_mix[...] = gains[0:8]
        o_ffn[...] = gains[8:16]
        for k in range(3):
            for h in range(2):
                o_conv[k : k + 1, pl.ds(128 * h, 128)] = rest[2 * k + h : 2 * k + h + 1]

    small_sums(cm, small, sm, sr, ss, sr_sem, (0.05, 5, 9, 15, 22), small_done)
    cm.run()


VMEM_SPEC = pl.BlockSpec(memory_space=pltpu.VMEM)


def call(kernel, name, cid, args, outs, scratch, limit):
    return pl.pallas_call(
        kernel,
        out_shape=outs,
        in_specs=[VMEM_SPEC] * len(args),
        out_specs=(VMEM_SPEC,) * len(outs),
        scratch_shapes=scratch,
        compiler_params=pltpu.CompilerParams(
            collective_id=cid, has_side_effects=True, vmem_limit_bytes=limit << 20
        ),
        cost_estimate=pl.CostEstimate(flops=1, bytes_accessed=1, transcendentals=0),
        name=name,
    )(*args)


def scatter_scratch(W, wa):
    f32 = jnp.float32
    wb = W - wa
    return [
        pltpu.VMEM((4, 4, 2, 32, W), f32),
        pltpu.VMEM((4, 4, 32, W), f32),
        pltpu.VMEM((2, 2, 32, wa), f32),
        pltpu.VMEM((2, 2, 32, wb), f32),
        pltpu.VMEM((2, 2, 2, 32, wa), f32),
        pltpu.VMEM((2, 2, 2, 32, wb), f32),
        pltpu.VMEM((2, 1, 16, wa), f32),
        pltpu.VMEM((2, 1, 16, wb), f32),
        pltpu.VMEM((2, 2, 1, 16, wa), f32),
        pltpu.VMEM((2, 2, 1, 16, wb), f32),
    ]


SCATTER_SEMS = [pltpu.SemaphoreType.DMA((n,)) for n in (4, 4, 12, 12, 12, 12)]


def middle(dn, own_resid, gain, own_cot, normed, d_gate, d_up, act, cot, down):
    T, D = dn.shape
    H = T // 8
    f32, shape, dma = jnp.float32, jax.ShapeDtypeStruct, pltpu.SemaphoreType.DMA
    w = act.shape[1]
    outs = (shape((T, D), f32), shape((T, D), jnp.bfloat16)) + (shape((32, w), f32),) * 3
    scratch = [
        pltpu.VMEM((T, D), f32),
        pltpu.VMEM((T, D), f32),
        pltpu.VMEM((2, 2, H, D), f32),
        pltpu.VMEM((2, 2, 2, H, D), f32),
        *scatter_scratch(3 * w, 1792),
        dma((2, 12)),
        dma((2, 12)),
        *SCATTER_SEMS,
    ]
    args = (dn, own_resid, gain, own_cot, normed, d_gate, d_up, act, cot, down)
    return call(middle_kernel, "middle", 5, args, outs, scratch, 56)


def end(dm, toks, gain, d_res, normed, d_proj, d_low, gated, small):
    T, D = dm.shape
    H = T // 8
    f32, shape, dma = jnp.float32, jax.ShapeDtypeStruct, pltpu.SemaphoreType.DMA
    outs = (
        shape((T, D), f32),
        shape((3, 32, 256), f32),
        shape((32, 256), f32),
        shape((8, 128), f32),
        shape((8, 128), f32),
        shape((3, 256), f32),
    )
    scratch = [
        pltpu.VMEM((2, H, D), f32),
        pltpu.VMEM((2, 2, H, D), f32),
        *scatter_scratch(1024, 512),
        pltpu.VMEM((3, 24, 128), f32),
        pltpu.VMEM((4, 4, 24, 128), f32),
        dma((12,)),
        dma((12,)),
        *SCATTER_SEMS,
        dma((10,)),
        dma((10,)),
    ]
    args = (dm, toks, gain, d_res, normed, *d_proj, d_low, gated, small)
    return call(end_kernel, "end", 7, args, outs, scratch, 40)


def place(*arrays):
    n = len(arrays)

    def kernel(*refs):
        copies = [pltpu.make_async_copy(refs[i], refs[n + i], refs[2 * n].at[i]) for i in range(n)]
        for copy in copies:
            copy.start()
        for copy in copies:
            copy.wait()

    anywhere = pl.BlockSpec(memory_space=pl.ANY)
    return pl.pallas_call(
        kernel,
        out_shape=tuple(jax.ShapeDtypeStruct(a.shape, a.dtype) for a in arrays),
        in_specs=[anywhere] * n,
        out_specs=(anywhere,) * n,
        scratch_shapes=[pltpu.SemaphoreType.DMA((n,))],
        name="place",
    )(*arrays)


def from_behind(block, axis, distance):
    devices = range(lax.axis_size(axis))
    route = [(i - distance, i) for i in devices if i - distance in devices]
    return lax.ppermute(block, axis, route)


def rms_scale(values):
    return lax.rsqrt(jnp.mean(values * values, axis=-1, keepdims=True) + EPS)


def right_product(left, right):
    return lax.dot_general(
        left, right, (((1,), (1,)), ((), ())), preferred_element_type=jnp.float32
    )


def on_device(
    tokens,
    segment_ids,
    mix_gain,
    in_weight,
    conv_weight,
    out_weight,
    ffn_gain,
    gate_weight,
    up_weight,
    down_weight,
    cotangent,
):
    tok_rows = tokens.shape[0]
    own = tok_rows // HEADS
    own_at = lax.axis_index("head") * own

    def own_rows(x):
        return lax.dynamic_slice_in_dim(x, own_at, own, 0)

    first_row = lax.axis_index("seq") * tok_rows
    padded_ids = jnp.concatenate(
        [jnp.full((2,), -1, jnp.int32), segment_ids, jnp.full((2,), -2, jnp.int32)]
    )
    id_window = lax.dynamic_slice_in_dim(padded_ids, first_row, tok_rows + 4)
    near_ext = (id_window[2 : tok_rows + 4] == id_window[1 : tok_rows + 3]).astype(jnp.float32)
    far_ext = (id_window[2 : tok_rows + 4] == id_window[0 : tok_rows + 2]).astype(jnp.float32)
    near_own = near_ext[:tok_rows, None]
    far_own = far_ext[:tok_rows, None]
    inputs = tokens.astype(jnp.float32)
    mix_scale = rms_scale(inputs)
    mix_normed = (inputs * mix_scale * mix_gain).astype(jnp.bfloat16)
    projected = jnp.einsum("td,dkc->tkc", mix_normed, in_weight, preferred_element_type=jnp.float32)
    chan_b = projected[:, 0]
    chan_c = projected[:, 1]
    chan_x = projected[:, 2]
    mixed = chan_b * chan_x
    edge_rows = from_behind(mixed[tok_rows - 2 :], "seq", 1)
    extended = jnp.concatenate([edge_rows, mixed])
    kernel = conv_weight.astype(jnp.float32)
    prev_one = extended[1 : tok_rows + 1]
    prev_two = extended[0:tok_rows]
    conv_out = kernel[0] * mixed + kernel[1] * near_own * prev_one + kernel[2] * far_own * prev_two
    gated = (chan_c * conv_out).astype(jnp.bfloat16)
    (resid,) = ring([("add", right_product(gated, out_weight), own_rows(tokens))], 1)
    ffn_scale = rms_scale(resid)
    ffn_normed = (resid * ffn_scale * ffn_gain).astype(jnp.bfloat16)
    gate = jnp.dot(ffn_normed, gate_weight, preferred_element_type=jnp.float32)
    upper = jnp.dot(ffn_normed, up_weight, preferred_element_type=jnp.float32)
    sigma = jax.nn.sigmoid(gate)
    act = (gate * sigma * upper).astype(jnp.bfloat16)
    d_act = jnp.dot(cotangent, down_weight, preferred_element_type=jnp.float32)
    d_gate = (d_act * upper * sigma * (1.0 + gate * (1.0 - sigma))).astype(jnp.bfloat16)
    d_up = (d_act * gate * sigma).astype(jnp.bfloat16)
    d_normed_part = right_product(d_gate, gate_weight) + right_product(d_up, up_weight)
    grad_ffn_gain = jnp.sum(d_normed_part * resid * ffn_scale, axis=0)
    d_resid, result, gate_share, up_share, down_share = middle(
        d_normed_part,
        own_rows(resid),
        ffn_gain[None],
        own_rows(cotangent),
        ffn_normed,
        d_gate,
        d_up,
        act,
        cotangent,
        down_weight,
    )
    d_resid_low = d_resid.astype(jnp.bfloat16)
    d_gated = jnp.dot(d_resid_low, out_weight, preferred_element_type=jnp.float32)
    d_chan_c = d_gated * conv_out
    d_conv = d_gated * chan_c
    tail_rows = from_behind(d_conv[:2], "seq", -1)
    later = jnp.concatenate([d_conv, tail_rows])
    next_one = later[1 : tok_rows + 1]
    next_two = later[2 : tok_rows + 2]
    near_next = near_ext[1 : tok_rows + 1, None]
    far_next = far_ext[2 : tok_rows + 2, None]
    d_mixed = kernel[0] * d_conv + kernel[1] * near_next * next_one + kernel[2] * far_next * next_two
    grad_conv = jnp.stack(
        [
            jnp.sum(d_conv * mixed, axis=0),
            jnp.sum(d_conv * near_own * prev_one, axis=0),
            jnp.sum(d_conv * far_own * prev_two, axis=0),
        ]
    )
    d_projected = [p.astype(jnp.bfloat16) for p in (d_mixed * chan_x, d_chan_c, d_mixed * chan_b)]
    d_mix_part = jnp.einsum(
        "tkc,dkc->td",
        jnp.stack(d_projected, axis=1),
        in_weight,
        preferred_element_type=jnp.float32,
    )
    grad_mix_gain = jnp.sum(d_mix_part * inputs * mix_scale, axis=0)
    small = jnp.concatenate(
        [
            grad_mix_gain.reshape(8, 128),
            grad_ffn_gain.reshape(8, 128),
            grad_conv.reshape(6, 128),
            jnp.zeros((2, 128), jnp.float32),
        ]
    )
    grad_tokens, in_share, out_share, mix_total, ffn_total, conv_total = end(
        d_mix_part,
        own_rows(tokens),
        mix_gain[None],
        own_rows(d_resid),
        mix_normed,
        d_projected,
        d_resid_low,
        gated,
        small,
    )
    (
        result,
        grad_tokens,
        mix_total,
        in_share,
        conv_total,
        out_share,
        ffn_total,
        gate_share,
        up_share,
        down_share,
    ) = place(
        result,
        grad_tokens,
        mix_total,
        in_share,
        conv_total,
        out_share,
        ffn_total,
        gate_share,
        up_share,
        down_share,
    )
    return (
        result,
        grad_tokens,
        mix_total.reshape(-1),
        in_share.transpose(1, 0, 2),
        conv_total,
        out_share,
        ffn_total.reshape(-1),
        gate_share,
        up_share,
        down_share,
    )


def solution(mesh):
    placed = (
        P("seq", None),
        P(),
        P(),
        P(None, None, "head"),
        P(None, "head"),
        P(None, "head"),
        P(),
        P(None, "head"),
        P(None, "head"),
        P(None, "head"),
        P("seq", None),
    )
    return jax.shard_map(
        on_device,
        mesh=mesh,
        in_specs=placed,
        out_specs=(
            P("seq", None),
            P("seq", None),
            P(),
            P("seq", None, "head"),
            P(None, "head"),
            P("seq", "head"),
            P(),
            P("seq", "head"),
            P("seq", "head"),
            P("seq", "head"),
        ),
        check_vma=False,
    )
```

```python
import jax
import jax.numpy as jnp
from jax import lax
from jax.experimental import pallas as pl
from jax.experimental.pallas import tpu as pltpu
from jax.sharding import PartitionSpec as P

EPS = 1e-05
MESH = pl.DeviceIdType.MESH
HEADS = 4


def norm_back_rows(grad_normed, values, gain, extra):
    scale = lax.rsqrt(jnp.mean(values * values, axis=-1, keepdims=True) + EPS)
    weighted = grad_normed * gain
    inner = jnp.mean(weighted * values, axis=-1, keepdims=True)
    return extra + (scale * weighted - values * (scale * scale * scale) * inner)


def ring_kernel(kinds, *refs):
    jobs = len(kinds)
    at = 0
    ins = []
    for kind in kinds:
        n = 4 if kind == "norm" else 2
        ins.append(refs[at : at + n])
        at += n
    outs = refs[at : at + jobs]
    at += jobs
    scratch = [refs[at + 4 * j : at + 4 * j + 4] for j in range(jobs)]
    s_sem, r_sem = refs[at + 4 * jobs : at + 4 * jobs + 2]
    T = outs[0].shape[0]
    C = T // HEADS
    H = C // 2

    me = lax.axis_index("head")
    R = lax.rem(me + 1, HEADS)
    L = lax.rem(me + HEADS - 1, HEADS)
    O = lax.rem(me + 2, HEADS)
    barrier = pltpu.get_barrier_semaphore()
    for other in (R, L):
        pl.semaphore_signal(barrier, inc=1, device_id={"head": other}, device_id_type=MESH)
    pl.semaphore_wait(barrier, 2)

    def rows(k, half):
        return pl.ds(pl.multiple_of(k * C + half * H, H), H)

    def send(src, dst, job, i, dev):
        copy = pltpu.make_async_remote_copy(
            src_ref=src,
            dst_ref=dst,
            send_sem=s_sem.at[job, i],
            recv_sem=r_sem.at[job, i],
            device_id={"head": dev},
            device_id_type=MESH,
        )
        copy.start()
        return copy

    def finish(job, half, total):
        kind = kinds[job]
        mine = pl.ds(half * H, H)
        if kind == "norm":
            _, values, gain, extra = ins[job]
            total = norm_back_rows(
                total, values[mine, :].astype(jnp.float32), gain[...], extra[mine, :].astype(jnp.float32)
            )
        else:
            total = total + ins[job][1][mine, :].astype(jnp.float32)
        outs[job][rows(me, half), :] = total

    every = []
    live = []
    for j in range(jobs):
        p = ins[j][0]
        t1, t2, fl, fr = scratch[j]
        a0 = send(p.at[rows(O, 0)], t1.at[0], j, 0, R)
        a1 = send(p.at[rows(O, 1)], t2.at[0], j, 1, L)
        a2 = send(p.at[rows(R, 1)], fl.at[1], j, 2, R)
        a3 = send(p.at[rows(L, 0)], fr.at[0], j, 3, L)
        live.append((a0, a1, a2, a3))
        every += [a0, a1, a2, a3]
    second = []
    for j in range(jobs):
        p = ins[j][0]
        t1, t2, fl, fr = scratch[j]
        a0, a1, a2, a3 = live[j]
        a0.wait_recv()
        t1[1] = p[rows(R, 0), :] + t1[0]
        a4 = send(t1.at[1], fl.at[0], j, 4, R)
        a1.wait_recv()
        t2[1] = p[rows(L, 1), :] + t2[0]
        a5 = send(t2.at[1], fr.at[1], j, 5, L)
        second.append((a2, a3, a4, a5))
        every += [a4, a5]
    shares = []
    for j in range(jobs):
        p, o = ins[j][0], outs[j]
        t1, t2, fl, fr = scratch[j]
        a2, a3, a4, a5 = second[j]
        a3.wait_recv()
        a4.wait_recv()
        finish(j, 0, p[rows(me, 0), :] + fl[0] + fr[0])
        b0 = send(o.at[rows(me, 0)], o.at[rows(me, 0)], j, 6, R)
        c0 = send(o.at[rows(me, 0)], o.at[rows(me, 0)], j, 8, L)
        a2.wait_recv()
        a5.wait_recv()
        finish(j, 1, p[rows(me, 1), :] + fl[1] + fr[1])
        b1 = send(o.at[rows(me, 1)], o.at[rows(me, 1)], j, 7, R)
        c1 = send(o.at[rows(me, 1)], o.at[rows(me, 1)], j, 9, L)
        shares.append((b0, b1, c0, c1))
        every += [b0, b1, c0, c1]
    last = []
    for j in range(jobs):
        o = outs[j]
        b0, b1, c0, c1 = shares[j]
        b0.wait_recv()
        d0 = send(o.at[rows(L, 0)], o.at[rows(L, 0)], j, 10, R)
        c1.wait_recv()
        d1 = send(o.at[rows(R, 1)], o.at[rows(R, 1)], j, 11, L)
        last += [b1, c0, d0, d1]
        every += [d0, d1]
    for copy in last:
        copy.wait_recv()
    for copy in every:
        copy.wait_send()


def ring(jobs, cid):
    kinds = tuple(job[0] for job in jobs)
    arrays = [a for job in jobs for a in job[1:]]
    T, D = jobs[0][1].shape
    H = T // HEADS // 2
    n = len(jobs)
    outs = pl.pallas_call(
        lambda *refs: ring_kernel(kinds, *refs),
        out_shape=tuple(jax.ShapeDtypeStruct((T, D), jnp.float32) for _ in jobs),
        in_specs=[pl.BlockSpec(memory_space=pltpu.VMEM)] * len(arrays),
        out_specs=tuple(pl.BlockSpec(memory_space=pltpu.VMEM) for _ in jobs),
        scratch_shapes=[pltpu.VMEM((2, H, D), jnp.float32)] * (4 * n)
        + [pltpu.SemaphoreType.DMA((n, 12))] * 2,
        compiler_params=pltpu.CompilerParams(
            collective_id=cid, has_side_effects=True, vmem_limit_bytes=32 << 20
        ),
        cost_estimate=pl.CostEstimate(flops=1, bytes_accessed=1, transcendentals=0),
        name=f"ring{cid}",
    )(*arrays)
    return outs


class Comm:
    def __init__(self):
        seq = lax.axis_index("seq")
        self.me = lax.axis_index("head")
        self.core = lax.rem(seq, 2)
        self.z = lax.rem(lax.div(seq, 2), 4)
        self.x = lax.div(seq, 8)
        self.every = []
        self.steps = []

    def at_x(self, n):
        return {"seq": (ahead(self.x, n) * 4 + self.z) * 2 + self.core, "head": self.me}

    def at_z(self, n):
        return {"seq": (self.x * 4 + ahead(self.z, n)) * 2 + self.core, "head": self.me}

    def at_y(self, n):
        return {"seq": (self.x * 4 + self.z) * 2 + self.core, "head": ahead(self.me, n)}

    def twin(self, n=1):
        return {"seq": (self.x * 4 + self.z) * 2 + (1 - self.core), "head": self.me}

    def greet(self, devices):
        barrier = pltpu.get_barrier_semaphore()
        for device in devices:
            pl.semaphore_signal(barrier, inc=1, device_id=device, device_id_type=MESH)
        pl.semaphore_wait(barrier, len(devices))

    def send(self, src, dst, s_sem, r_sem, dev):
        copy = pltpu.make_async_remote_copy(
            src_ref=src, dst_ref=dst, send_sem=s_sem, recv_sem=r_sem, device_id=dev, device_id_type=MESH
        )
        copy.start()
        self.every.append(copy)
        return copy

    def when(self, time):
        def add(fn):
            self.steps.append((time, len(self.steps), fn))
            return fn

        return add

    def run(self):
        for _, _, fn in sorted(self.steps, key=lambda s: s[:2]):
            fn()
        for copy in self.every:
            copy.wait_send()


def ahead(k, n):
    return lax.rem(k + n, 4)


def add_up(dst, *srcs):
    n, r = dst.shape[:2]
    q = r // 8

    def body(i, carry):
        b, at = lax.div(i, q), pl.ds(pl.multiple_of(lax.rem(i, q) * 8, 8), 8)
        total = dst[b, at, :]
        for src in srcs:
            total = total + src[b, at, :]
        dst[b, at, :] = total
        return carry

    lax.fori_loop(0, n * q, body, 0)


def head_sum(cm, p, o, t, f, s_sem, r_sem, finish, times, closing):
    T = o.shape[0]
    C = T // 4
    H = C // 2
    R, L, O = ahead(cm.me, 1), ahead(cm.me, 3), ahead(cm.me, 2)
    me = cm.me
    c = {}

    def rows(k, half):
        return pl.ds(pl.multiple_of(k * C + half * H, H), H)

    def go(name, src, dst, i, n):
        c[name] = cm.send(src, dst, s_sem.at[i], r_sem.at[i], cm.at_y(n))

    @cm.when(times[0])
    def _():
        go("a0", p.at[rows(O, 0)], t.at[0], 0, 1)
        go("a1", p.at[rows(O, 1)], t.at[1], 1, 3)
        go("a2", p.at[rows(R, 1)], f.at[0, 1], 2, 1)
        go("a3", p.at[rows(L, 0)], f.at[1, 0], 3, 3)

    @cm.when(times[1])
    def _():
        c["a0"].wait_recv()
        t[0] = p[rows(R, 0), :] + t[0]
        go("a4", t.at[0], f.at[0, 0], 4, 1)
        c["a1"].wait_recv()
        t[1] = p[rows(L, 1), :] + t[1]
        go("a5", t.at[1], f.at[1, 1], 5, 3)

    @cm.when(times[2])
    def _():
        c["a3"].wait_recv()
        c["a4"].wait_recv()
        o[rows(me, 0), :] = finish(0, p[rows(me, 0), :] + f[0, 0] + f[1, 0])
        go("b0", o.at[rows(me, 0)], o.at[rows(me, 0)], 6, 1)
        go("c0", o.at[rows(me, 0)], o.at[rows(me, 0)], 8, 3)
        c["a2"].wait_recv()
        c["a5"].wait_recv()
        o[rows(me, 1), :] = finish(1, p[rows(me, 1), :] + f[0, 1] + f[1, 1])
        go("c1", o.at[rows(me, 1)], o.at[rows(me, 1)], 9, 3)
        go("b1", o.at[rows(me, 1)], o.at[rows(me, 1)], 7, 1)

    @cm.when(times[3])
    def _():
        c["b0"].wait_recv()
        go("d0", o.at[rows(L, 0)], o.at[rows(L, 0)], 10, 1)
        c["c1"].wait_recv()
        go("d1", o.at[rows(R, 1)], o.at[rows(R, 1)], 11, 3)

    @cm.when(900)
    def _():
        for name in ("b1", "c0", "d0", "d1"):
            c[name].wait_recv()
        closing()


def scatter_ring(cm, chunk, t, f, s_sem, r_sem, base, to, times, done):
    c = {}

    def go(name, src, dst, i, n):
        c[name] = cm.send(src, dst, s_sem.at[base + i], r_sem.at[base + i], to(n))

    @cm.when(times[0])
    def _():
        go("a0", chunk(2, 0), t.at[0], 0, 1)
        go("a1", chunk(2, 1), t.at[1], 1, 3)

    @cm.when(times[1])
    def _():
        go("a2", chunk(1, 1), f.at[0, 1], 2, 1)

    @cm.when(times[2])
    def _():
        go("a3", chunk(3, 0), f.at[1, 0], 3, 3)

    @cm.when(times[3])
    def _():
        c["a0"].wait_recv()
        add_up(t.at[0], chunk(1, 0))
        go("a4", t.at[0], f.at[0, 0], 4, 1)
        c["a1"].wait_recv()
        add_up(t.at[1], chunk(3, 1))
        go("a5", t.at[1], f.at[1, 1], 5, 3)

    @cm.when(times[4])
    def _():
        c["a3"].wait_recv()
        c["a4"].wait_recv()
        add_up(chunk(0, 0), f.at[0, 0], f.at[1, 0])
        c["a2"].wait_recv()
        c["a5"].wait_recv()
        add_up(chunk(0, 1), f.at[0, 1], f.at[1, 1])
        done()


def grad_scatter(cm, products, G, RC, wa, bufs, sems, times, done_a, done_b):
    tA, tB, fA, fB, t2A, t2B, f2A, f2B = bufs
    cs, cr, as_, ar, bs, br = sems
    W = G.shape[-1]
    quarter = products[0][0].shape[1] // 4
    got = {}

    def block(turn):
        k = ahead(cm.x, turn)
        for left, rights, at in products:
            right = jnp.concatenate([r[...] for r in rights], axis=1)
            w = right.shape[1]
            lhs = left[:, pl.ds(pl.multiple_of(k * quarter, quarter), quarter)]
            value = lax.dot_general(
                lhs, right, (((0,), (0,)), ((), ())), preferred_element_type=jnp.float32
            )
            G[k, :, :, :, pl.ds(at, w)] = value.reshape(4, 2, 32, w)
        got[turn] = cm.send(G.at[k, :, 1 - cm.core], RC.at[k], cs.at[turn], cr.at[turn], cm.twin())

    def settle(turn):
        k = ahead(cm.x, turn)
        got[turn].wait_recv()
        add_up(G.at[k, :, cm.core], RC.at[k])

    for i, turn in enumerate((2, 1, 3, 0)):
        cm.when(times["block"][i])(lambda turn=turn: block(turn))
        cm.when(times["settle"][i])(lambda turn=turn: settle(turn))

    cols_a, cols_b = pl.ds(0, wa), pl.ds(wa, W - wa)
    core = cm.core

    def a1(turn, half):
        return G.at[ahead(cm.x, turn), pl.ds(half * 2, 2), core, :, cols_a]

    def b1(turn, half):
        return G.at[pl.ds(half * 2, 2), ahead(cm.z, turn), core, :, cols_b]

    def a2(turn, half):
        return G.at[cm.x, pl.ds(ahead(cm.z, turn), 1), core, pl.ds(half * 16, 16), cols_a]

    def b2(turn, half):
        return G.at[pl.ds(ahead(cm.x, turn), 1), cm.z, core, pl.ds(half * 16, 16), cols_b]

    nothing = lambda: None
    scatter_ring(cm, a1, tA, fA, as_, ar, 0, cm.at_x, times["A"], nothing)
    scatter_ring(cm, b1, tB, fB, bs, br, 0, cm.at_z, times["B"], nothing)
    scatter_ring(cm, a2, t2A, f2A, as_, ar, 6, cm.at_z, times["A2"], done_a)
    scatter_ring(cm, b2, t2B, f2B, bs, br, 6, cm.at_x, times["B2"], done_b)


def small_sums(cm, small, sm, sr, s_sem, r_sem, times, done):
    axes = [(cm.at_z, cm.z), (cm.at_x, cm.x), (cm.at_y, cm.me)]
    first = {}

    @cm.when(times[0])
    def _():
        first["c"] = cm.send(small, sr.at[3, 0], s_sem.at[9], r_sem.at[9], cm.twin())

    @cm.when(times[1])
    def _():
        first["c"].wait_recv()
        sm[0] = small[...] + sr[3, 0]

    for a, (to, here) in enumerate(axes):
        copies = []

        def begin(a=a, to=to, here=here, copies=copies):
            sr[a, here] = sm[a]
            for n in (1, 2, 3):
                i = a * 3 + n - 1
                copies.append(cm.send(sm.at[a], sr.at[a, here], s_sem.at[i], r_sem.at[i], to(n)))

        def end(a=a, copies=copies):
            for copy in copies:
                copy.wait_recv()
            total = (sr[a, 0] + sr[a, 1]) + (sr[a, 2] + sr[a, 3])
            if a < 2:
                sm[a + 1] = total
            else:
                done(total[0:16], sm[2][16:24])

        cm.when(times[1] + 0.01)(begin) if a == 0 else cm.when(times[1 + a] + 0.01)(begin)
        cm.when(times[2 + a])(end)


def greet_all(cm):
    cm.greet([axis(n) for n in (1, 2, 3) for axis in (cm.at_x, cm.at_z, cm.at_y)] + [cm.twin()])


def middle_kernel(*refs):
    (dn, own_resid, gain, own_cot, normed, d_gate, d_up, act, cot, down) = refs[:10]
    (o_dres, o_res, o_gate, o_up, o_down) = refs[10:15]
    (rp, full, yt, yf, G, RC) = refs[15:21]
    bufs, (ys, yr), sems = refs[21:29], refs[29:31], refs[31:]
    H = own_resid.shape[0] // 2
    cm = Comm()
    greet_all(cm)

    def finish_dres(half, total):
        mine = pl.ds(half * H, H)
        return norm_back_rows(total, own_resid[mine, :], gain[...], own_cot[mine, :].astype(jnp.float32))

    def finish_result(half, total):
        return total + own_resid[pl.ds(half * H, H), :]

    def rounded():
        o_res[...] = full[...].astype(jnp.bfloat16)

    @cm.when(0.02)
    def _():
        rp[...] = lax.dot_general(
            act[...], down[...], (((1,), (1,)), ((), ())), preferred_element_type=jnp.float32
        )

    head_sum(cm, dn, o_dres, yt.at[0], yf.at[0], ys.at[0], yr.at[0], finish_dres, (0, 7, 28, 43), lambda: None)
    head_sum(cm, rp, full, yt.at[1], yf.at[1], ys.at[1], yr.at[1], finish_result, (0.03, 18, 36, 56), rounded)

    w = act.shape[1]
    wa = 1792

    def done_a():
        rows = G[cm.x, cm.z, cm.core, :, pl.ds(0, wa)]
        o_gate[...] = rows[:, :w]
        o_up[:, pl.ds(0, wa - w)] = rows[:, w:]

    def done_b():
        rows = G[cm.x, cm.z, cm.core, :, pl.ds(wa, 3 * w - wa)]
        o_up[:, pl.ds(wa - w, 2 * w - wa)] = rows[:, : 2 * w - wa]
        o_down[...] = rows[:, 2 * w - wa :]

    times = {
        "block": (4, 5.5, 7.5, 9),
        "settle": (7.1, 8.5, 10, 12),
        "A": (7.2, 8.6, 10.1, 18.5, 42),
        "B": (12.1, 12.2, 12.3, 24, 45),
        "A2": (42.1, 42.2, 42.3, 46, 52),
        "B2": (45.1, 45.2, 45.3, 49, 55),
    }
    products = [(normed, [d_gate], 0), (normed, [d_up], w), (cot, [act], 2 * w)]
    grad_scatter(cm, products, G, RC, wa, bufs, sems, times, done_a, done_b)
    cm.run()


def end_kernel(*refs):
    (dm, toks, gain, d_res, normed) = refs[:5]
    d_proj = refs[5:8]
    (d_low, gated, small) = refs[8:11]
    (o_tok, o_in, o_out, o_mix, o_ffn, o_conv) = refs[11:17]
    (yt, yf, G, RC) = refs[17:21]
    bufs = refs[21:29]
    sm, sr = refs[29:31]
    ys, yr = refs[31:33]
    sems = refs[33:39]
    ss, sr_sem = refs[39:]
    H = toks.shape[0] // 2
    cm = Comm()
    greet_all(cm)

    def finish_tokens(half, total):
        mine = pl.ds(half * H, H)
        return norm_back_rows(total, toks[mine, :].astype(jnp.float32), gain[...], d_res[mine, :])

    head_sum(cm, dm, o_tok, yt, yf, ys, yr, finish_tokens, (0, 6.5, 17, 26), lambda: None)

    wa = 512

    def done_a():
        rows = G[cm.x, cm.z, cm.core, :, pl.ds(0, wa)]
        o_in[0] = rows[:, :256]
        o_in[1] = rows[:, 256:]

    def done_b():
        rows = G[cm.x, cm.z, cm.core, :, pl.ds(wa, 512)]
        o_in[2] = rows[:, :256]
        o_out[...] = rows[:, 256:]

    times = {
        "block": (0.1, 1, 2, 3),
        "settle": (1.5, 2.5, 3.5, 4.5),
        "A": (1.6, 2.6, 3.6, 6, 14),
        "B": (4.6, 4.7, 4.8, 8.5, 16),
        "A2": (14.1, 14.2, 14.3, 17.2, 20),
        "B2": (16.1, 16.2, 16.3, 18.5, 21),
    }
    products = [(normed, d_proj, 0), (d_low, [gated], 768)]
    grad_scatter(cm, products, G, RC, wa, bufs, sems, times, done_a, done_b)

    def small_done(gains, rest):
        o_mix[...] = gains[0:8]
        o_ffn[...] = gains[8:16]
        for k in range(3):
            for h in range(2):
                o_conv[k : k + 1, pl.ds(128 * h, 128)] = rest[2 * k + h : 2 * k + h + 1]

    small_sums(cm, small, sm, sr, ss, sr_sem, (0.05, 5, 9, 15, 22), small_done)
    cm.run()


VMEM_SPEC = pl.BlockSpec(memory_space=pltpu.VMEM)


def call(kernel, name, cid, args, outs, scratch, limit):
    return pl.pallas_call(
        kernel,
        out_shape=outs,
        in_specs=[VMEM_SPEC] * len(args),
        out_specs=(VMEM_SPEC,) * len(outs),
        scratch_shapes=scratch,
        compiler_params=pltpu.CompilerParams(
            collective_id=cid, has_side_effects=True, vmem_limit_bytes=limit << 20
        ),
        cost_estimate=pl.CostEstimate(flops=1, bytes_accessed=1, transcendentals=0),
        name=name,
    )(*args)


def scatter_scratch(W, wa):
    f32 = jnp.float32
    wb = W - wa
    return [
        pltpu.VMEM((4, 4, 2, 32, W), f32),
        pltpu.VMEM((4, 4, 32, W), f32),
        pltpu.VMEM((2, 2, 32, wa), f32),
        pltpu.VMEM((2, 2, 32, wb), f32),
        pltpu.VMEM((2, 2, 2, 32, wa), f32),
        pltpu.VMEM((2, 2, 2, 32, wb), f32),
        pltpu.VMEM((2, 1, 16, wa), f32),
        pltpu.VMEM((2, 1, 16, wb), f32),
        pltpu.VMEM((2, 2, 1, 16, wa), f32),
        pltpu.VMEM((2, 2, 1, 16, wb), f32),
    ]


SCATTER_SEMS = [pltpu.SemaphoreType.DMA((n,)) for n in (4, 4, 12, 12, 12, 12)]


def middle(dn, own_resid, gain, own_cot, normed, d_gate, d_up, act, cot, down):
    T, D = dn.shape
    H = T // 8
    f32, shape, dma = jnp.float32, jax.ShapeDtypeStruct, pltpu.SemaphoreType.DMA
    w = act.shape[1]
    outs = (shape((T, D), f32), shape((T, D), jnp.bfloat16)) + (shape((32, w), f32),) * 3
    scratch = [
        pltpu.VMEM((T, D), f32),
        pltpu.VMEM((T, D), f32),
        pltpu.VMEM((2, 2, H, D), f32),
        pltpu.VMEM((2, 2, 2, H, D), f32),
        *scatter_scratch(3 * w, 1792),
        dma((2, 12)),
        dma((2, 12)),
        *SCATTER_SEMS,
    ]
    args = (dn, own_resid, gain, own_cot, normed, d_gate, d_up, act, cot, down)
    return call(middle_kernel, "middle", 5, args, outs, scratch, 56)


def end(dm, toks, gain, d_res, normed, d_proj, d_low, gated, small):
    T, D = dm.shape
    H = T // 8
    f32, shape, dma = jnp.float32, jax.ShapeDtypeStruct, pltpu.SemaphoreType.DMA
    outs = (
        shape((T, D), f32),
        shape((3, 32, 256), f32),
        shape((32, 256), f32),
        shape((8, 128), f32),
        shape((8, 128), f32),
        shape((3, 256), f32),
    )
    scratch = [
        pltpu.VMEM((2, H, D), f32),
        pltpu.VMEM((2, 2, H, D), f32),
        *scatter_scratch(1024, 512),
        pltpu.VMEM((3, 24, 128), f32),
        pltpu.VMEM((4, 4, 24, 128), f32),
        dma((12,)),
        dma((12,)),
        *SCATTER_SEMS,
        dma((10,)),
        dma((10,)),
    ]
    args = (dm, toks, gain, d_res, normed, *d_proj, d_low, gated, small)
    return call(end_kernel, "end", 7, args, outs, scratch, 40)


def place(*arrays):
    n = len(arrays)

    def kernel(*refs):
        copies = [pltpu.make_async_copy(refs[i], refs[n + i], refs[2 * n].at[i]) for i in range(n)]
        for copy in copies:
            copy.start()
        for copy in copies:
            copy.wait()

    anywhere = pl.BlockSpec(memory_space=pl.ANY)
    return pl.pallas_call(
        kernel,
        out_shape=tuple(jax.ShapeDtypeStruct(a.shape, a.dtype) for a in arrays),
        in_specs=[VMEM_SPEC] * n,
        out_specs=(anywhere,) * n,
        scratch_shapes=[pltpu.SemaphoreType.DMA((n,))],
        name="place",
    )(*arrays)


def from_behind(block, axis, distance):
    devices = range(lax.axis_size(axis))
    route = [(i - distance, i) for i in devices if i - distance in devices]
    return lax.ppermute(block, axis, route)


def rms_scale(values):
    return lax.rsqrt(jnp.mean(values * values, axis=-1, keepdims=True) + EPS)


def right_product(left, right):
    return lax.dot_general(
        left, right, (((1,), (1,)), ((), ())), preferred_element_type=jnp.float32
    )


def on_device(
    tokens,
    segment_ids,
    mix_gain,
    in_weight,
    conv_weight,
    out_weight,
    ffn_gain,
    gate_weight,
    up_weight,
    down_weight,
    cotangent,
):
    tok_rows = tokens.shape[0]
    own = tok_rows // HEADS
    own_at = lax.axis_index("head") * own

    def own_rows(x):
        return lax.dynamic_slice_in_dim(x, own_at, own, 0)

    first_row = lax.axis_index("seq") * tok_rows
    padded_ids = jnp.concatenate(
        [jnp.full((2,), -1, jnp.int32), segment_ids, jnp.full((2,), -2, jnp.int32)]
    )
    id_window = lax.dynamic_slice_in_dim(padded_ids, first_row, tok_rows + 4)
    near_ext = (id_window[2 : tok_rows + 4] == id_window[1 : tok_rows + 3]).astype(jnp.float32)
    far_ext = (id_window[2 : tok_rows + 4] == id_window[0 : tok_rows + 2]).astype(jnp.float32)
    near_own = near_ext[:tok_rows, None]
    far_own = far_ext[:tok_rows, None]
    inputs = tokens.astype(jnp.float32)
    mix_scale = rms_scale(inputs)
    mix_normed = (inputs * mix_scale * mix_gain).astype(jnp.bfloat16)
    projected = jnp.einsum("td,dkc->tkc", mix_normed, in_weight, preferred_element_type=jnp.float32)
    chan_b = projected[:, 0]
    chan_c = projected[:, 1]
    chan_x = projected[:, 2]
    mixed = chan_b * chan_x
    edge_rows = from_behind(mixed[tok_rows - 2 :], "seq", 1)
    extended = jnp.concatenate([edge_rows, mixed])
    kernel = conv_weight.astype(jnp.float32)
    prev_one = extended[1 : tok_rows + 1]
    prev_two = extended[0:tok_rows]
    conv_out = kernel[0] * mixed + kernel[1] * near_own * prev_one + kernel[2] * far_own * prev_two
    gated = (chan_c * conv_out).astype(jnp.bfloat16)
    (resid,) = ring([("add", right_product(gated, out_weight), own_rows(tokens))], 1)
    ffn_scale = rms_scale(resid)
    ffn_normed = (resid * ffn_scale * ffn_gain).astype(jnp.bfloat16)
    gate = jnp.dot(ffn_normed, gate_weight, preferred_element_type=jnp.float32)
    upper = jnp.dot(ffn_normed, up_weight, preferred_element_type=jnp.float32)
    sigma = jax.nn.sigmoid(gate)
    act = (gate * sigma * upper).astype(jnp.bfloat16)
    d_act = jnp.dot(cotangent, down_weight, preferred_element_type=jnp.float32)
    d_gate = (d_act * upper * sigma * (1.0 + gate * (1.0 - sigma))).astype(jnp.bfloat16)
    d_up = (d_act * gate * sigma).astype(jnp.bfloat16)
    d_normed_part = right_product(d_gate, gate_weight) + right_product(d_up, up_weight)
    grad_ffn_gain = jnp.sum(d_normed_part * resid * ffn_scale, axis=0)
    d_resid, result, gate_share, up_share, down_share = middle(
        d_normed_part,
        own_rows(resid),
        ffn_gain[None],
        own_rows(cotangent),
        ffn_normed,
        d_gate,
        d_up,
        act,
        cotangent,
        down_weight,
    )
    d_resid_low = d_resid.astype(jnp.bfloat16)
    d_gated = jnp.dot(d_resid_low, out_weight, preferred_element_type=jnp.float32)
    d_chan_c = d_gated * conv_out
    d_conv = d_gated * chan_c
    tail_rows = from_behind(d_conv[:2], "seq", -1)
    later = jnp.concatenate([d_conv, tail_rows])
    next_one = later[1 : tok_rows + 1]
    next_two = later[2 : tok_rows + 2]
    near_next = near_ext[1 : tok_rows + 1, None]
    far_next = far_ext[2 : tok_rows + 2, None]
    d_mixed = kernel[0] * d_conv + kernel[1] * near_next * next_one + kernel[2] * far_next * next_two
    grad_conv = jnp.stack(
        [
            jnp.sum(d_conv * mixed, axis=0),
            jnp.sum(d_conv * near_own * prev_one, axis=0),
            jnp.sum(d_conv * far_own * prev_two, axis=0),
        ]
    )
    d_projected = [p.astype(jnp.bfloat16) for p in (d_mixed * chan_x, d_chan_c, d_mixed * chan_b)]
    d_mix_part = jnp.einsum(
        "tkc,dkc->td",
        jnp.stack(d_projected, axis=1),
        in_weight,
        preferred_element_type=jnp.float32,
    )
    grad_mix_gain = jnp.sum(d_mix_part * inputs * mix_scale, axis=0)
    small = jnp.concatenate(
        [
            grad_mix_gain.reshape(8, 128),
            grad_ffn_gain.reshape(8, 128),
            grad_conv.reshape(6, 128),
            jnp.zeros((2, 128), jnp.float32),
        ]
    )
    grad_tokens, in_share, out_share, mix_total, ffn_total, conv_total = end(
        d_mix_part,
        own_rows(tokens),
        mix_gain[None],
        own_rows(d_resid),
        mix_normed,
        d_projected,
        d_resid_low,
        gated,
        small,
    )
    (
        result,
        grad_tokens,
        mix_total,
        in_share,
        conv_total,
        out_share,
        ffn_total,
        gate_share,
        up_share,
        down_share,
    ) = place(
        result,
        grad_tokens,
        mix_total,
        in_share,
        conv_total,
        out_share,
        ffn_total,
        gate_share,
        up_share,
        down_share,
    )
    return (
        result,
        grad_tokens,
        mix_total.reshape(-1),
        in_share.transpose(1, 0, 2),
        conv_total,
        out_share,
        ffn_total.reshape(-1),
        gate_share,
        up_share,
        down_share,
    )


def solution(mesh):
    placed = (
        P("seq", None),
        P(),
        P(),
        P(None, None, "head"),
        P(None, "head"),
        P(None, "head"),
        P(),
        P(None, "head"),
        P(None, "head"),
        P(None, "head"),
        P("seq", None),
    )
    return jax.shard_map(
        on_device,
        mesh=mesh,
        in_specs=placed,
        out_specs=(
            P("seq", None),
            P("seq", None),
            P(),
            P("seq", None, "head"),
            P(None, "head"),
            P("seq", "head"),
            P(),
            P("seq", "head"),
            P("seq", "head"),
            P("seq", "head"),
        ),
        check_vma=False,
    )
```

```python
import jax
import jax.numpy as jnp
from jax import lax
from jax.experimental import pallas as pl
from jax.experimental.pallas import tpu as pltpu
from jax.sharding import PartitionSpec as P

EPS = 1e-05
MESH = pl.DeviceIdType.MESH
HEADS = 4


def norm_back_rows(grad_normed, values, gain, extra):
    scale = lax.rsqrt(jnp.mean(values * values, axis=-1, keepdims=True) + EPS)
    weighted = grad_normed * gain
    inner = jnp.mean(weighted * values, axis=-1, keepdims=True)
    return extra + (scale * weighted - values * (scale * scale * scale) * inner)


class Comm:
    def __init__(self):
        seq = lax.axis_index("seq")
        self.me = lax.axis_index("head")
        self.core = lax.rem(seq, 2)
        self.z = lax.rem(lax.div(seq, 2), 4)
        self.x = lax.div(seq, 8)
        self.every = []
        self.steps = []

    def at_x(self, n):
        return {"seq": (ahead(self.x, n) * 4 + self.z) * 2 + self.core, "head": self.me}

    def at_z(self, n):
        return {"seq": (self.x * 4 + ahead(self.z, n)) * 2 + self.core, "head": self.me}

    def at_y(self, n):
        return {"seq": (self.x * 4 + self.z) * 2 + self.core, "head": ahead(self.me, n)}

    def twin(self, n=1):
        return {"seq": (self.x * 4 + self.z) * 2 + (1 - self.core), "head": self.me}

    def greet(self, devices):
        barrier = pltpu.get_barrier_semaphore()
        for device in devices:
            pl.semaphore_signal(barrier, inc=1, device_id=device, device_id_type=MESH)
        pl.semaphore_wait(barrier, len(devices))

    def send(self, src, dst, s_sem, r_sem, dev):
        copy = pltpu.make_async_remote_copy(
            src_ref=src, dst_ref=dst, send_sem=s_sem, recv_sem=r_sem, device_id=dev, device_id_type=MESH
        )
        copy.start()
        self.every.append(copy)
        return copy

    def when(self, time):
        def add(fn):
            self.steps.append((time, len(self.steps), fn))
            return fn

        return add

    def run(self):
        for _, _, fn in sorted(self.steps, key=lambda s: s[:2]):
            fn()
        for copy in self.every:
            copy.wait_send()


def ahead(k, n):
    return lax.rem(k + n, 4)


def add_up(dst, *srcs):
    n, r = dst.shape[:2]
    q = r // 8

    def body(i, carry):
        b, at = lax.div(i, q), pl.ds(pl.multiple_of(lax.rem(i, q) * 8, 8), 8)
        total = dst[b, at, :]
        for src in srcs:
            total = total + src[b, at, :]
        dst[b, at, :] = total
        return carry

    lax.fori_loop(0, n * q, body, 0)


def head_sum(cm, p, o, t, f, s_sem, r_sem, finish, times, closing, share=True):
    T = p.shape[0]
    C = T // 4
    H = C // 2
    R, L, O = ahead(cm.me, 1), ahead(cm.me, 3), ahead(cm.me, 2)
    me = cm.me
    c = {}

    def rows(k, half):
        return pl.ds(pl.multiple_of(k * C + half * H, H), H)

    def go(name, src, dst, i, n):
        c[name] = cm.send(src, dst, s_sem.at[i], r_sem.at[i], cm.at_y(n))

    @cm.when(times[0])
    def _():
        go("a0", p.at[rows(O, 0)], t.at[0], 0, 1)
        go("a1", p.at[rows(O, 1)], t.at[1], 1, 3)
        go("a2", p.at[rows(R, 1)], f.at[0, 1], 2, 1)
        go("a3", p.at[rows(L, 0)], f.at[1, 0], 3, 3)

    @cm.when(times[1])
    def _():
        c["a0"].wait_recv()
        t[0] = p[rows(R, 0), :] + t[0]
        go("a4", t.at[0], f.at[0, 0], 4, 1)
        c["a1"].wait_recv()
        t[1] = p[rows(L, 1), :] + t[1]
        go("a5", t.at[1], f.at[1, 1], 5, 3)

    @cm.when(times[2])
    def _():
        c["a3"].wait_recv()
        c["a4"].wait_recv()
        first = finish(0, p[rows(me, 0), :] + f[0, 0] + f[1, 0])
        if not share:
            c["a2"].wait_recv()
            c["a5"].wait_recv()
            o[0:H, :] = first
            o[H:C, :] = finish(1, p[rows(me, 1), :] + f[0, 1] + f[1, 1])
            return
        o[rows(me, 0), :] = first
        go("b0", o.at[rows(me, 0)], o.at[rows(me, 0)], 6, 1)
        go("c0", o.at[rows(me, 0)], o.at[rows(me, 0)], 8, 3)
        c["a2"].wait_recv()
        c["a5"].wait_recv()
        o[rows(me, 1), :] = finish(1, p[rows(me, 1), :] + f[0, 1] + f[1, 1])
        go("c1", o.at[rows(me, 1)], o.at[rows(me, 1)], 9, 3)
        go("b1", o.at[rows(me, 1)], o.at[rows(me, 1)], 7, 1)

    if not share:
        return

    @cm.when(times[3])
    def _():
        c["b0"].wait_recv()
        go("d0", o.at[rows(L, 0)], o.at[rows(L, 0)], 10, 1)
        c["c1"].wait_recv()
        go("d1", o.at[rows(R, 1)], o.at[rows(R, 1)], 11, 3)

    @cm.when(900)
    def _():
        for name in ("b1", "c0", "d0", "d1"):
            c[name].wait_recv()
        closing()


def scatter_ring(cm, chunk, t, f, s_sem, r_sem, base, to, times, done):
    c = {}

    def go(name, src, dst, i, n):
        c[name] = cm.send(src, dst, s_sem.at[base + i], r_sem.at[base + i], to(n))

    @cm.when(times[0])
    def _():
        go("a0", chunk(2, 0), t.at[0], 0, 1)
        go("a1", chunk(2, 1), t.at[1], 1, 3)

    @cm.when(times[1])
    def _():
        go("a2", chunk(1, 1), f.at[0, 1], 2, 1)

    @cm.when(times[2])
    def _():
        go("a3", chunk(3, 0), f.at[1, 0], 3, 3)

    @cm.when(times[3])
    def _():
        c["a0"].wait_recv()
        add_up(t.at[0], chunk(1, 0))
        go("a4", t.at[0], f.at[0, 0], 4, 1)
        c["a1"].wait_recv()
        add_up(t.at[1], chunk(3, 1))
        go("a5", t.at[1], f.at[1, 1], 5, 3)

    @cm.when(times[4])
    def _():
        c["a3"].wait_recv()
        c["a4"].wait_recv()
        add_up(chunk(0, 0), f.at[0, 0], f.at[1, 0])
        c["a2"].wait_recv()
        c["a5"].wait_recv()
        add_up(chunk(0, 1), f.at[0, 1], f.at[1, 1])
        done()


def grad_scatter(cm, products, G, RC, wa, bufs, sems, times, done_a, done_b):
    tA, tB, fA, fB, t2A, t2B, f2A, f2B = bufs
    cs, cr, as_, ar, bs, br = sems
    W = G.shape[-1]
    quarter = products[0][0].shape[1] // 4
    got = {}

    def block(turn):
        k = ahead(cm.x, turn)
        for left, rights, at in products:
            right = jnp.concatenate([r[...] for r in rights], axis=1)
            w = right.shape[1]
            lhs = left[:, pl.ds(pl.multiple_of(k * quarter, quarter), quarter)]
            value = lax.dot_general(
                lhs, right, (((0,), (0,)), ((), ())), preferred_element_type=jnp.float32
            )
            G[k, :, :, :, pl.ds(at, w)] = value.reshape(4, 2, 32, w)
        got[turn] = cm.send(G.at[k, :, 1 - cm.core], RC.at[k], cs.at[turn], cr.at[turn], cm.twin())

    def settle(turn):
        k = ahead(cm.x, turn)
        got[turn].wait_recv()
        add_up(G.at[k, :, cm.core], RC.at[k])

    for i, turn in enumerate((2, 1, 3, 0)):
        cm.when(times["block"][i])(lambda turn=turn: block(turn))
        cm.when(times["settle"][i])(lambda turn=turn: settle(turn))

    cols_a, cols_b = pl.ds(0, wa), pl.ds(wa, W - wa)
    core = cm.core

    def a1(turn, half):
        return G.at[ahead(cm.x, turn), pl.ds(half * 2, 2), core, :, cols_a]

    def b1(turn, half):
        return G.at[pl.ds(half * 2, 2), ahead(cm.z, turn), core, :, cols_b]

    def a2(turn, half):
        return G.at[cm.x, pl.ds(ahead(cm.z, turn), 1), core, pl.ds(half * 16, 16), cols_a]

    def b2(turn, half):
        return G.at[pl.ds(ahead(cm.x, turn), 1), cm.z, core, pl.ds(half * 16, 16), cols_b]

    nothing = lambda: None
    scatter_ring(cm, a1, tA, fA, as_, ar, 0, cm.at_x, times["A"], nothing)
    scatter_ring(cm, b1, tB, fB, bs, br, 0, cm.at_z, times["B"], nothing)
    scatter_ring(cm, a2, t2A, f2A, as_, ar, 6, cm.at_z, times["A2"], done_a)
    scatter_ring(cm, b2, t2B, f2B, bs, br, 6, cm.at_x, times["B2"], done_b)


def small_sums(cm, small, sm, sr, s_sem, r_sem, times, done):
    axes = [(cm.at_z, cm.z), (cm.at_x, cm.x), (cm.at_y, cm.me)]
    first = {}

    @cm.when(times[0])
    def _():
        first["c"] = cm.send(small, sr.at[3, 0], s_sem.at[9], r_sem.at[9], cm.twin())

    @cm.when(times[1])
    def _():
        first["c"].wait_recv()
        sm[0] = small[...] + sr[3, 0]

    for a, (to, here) in enumerate(axes):
        copies = []

        def begin(a=a, to=to, here=here, copies=copies):
            sr[a, here] = sm[a]
            for n in (1, 2, 3):
                i = a * 3 + n - 1
                copies.append(cm.send(sm.at[a], sr.at[a, here], s_sem.at[i], r_sem.at[i], to(n)))

        def end(a=a, copies=copies):
            for copy in copies:
                copy.wait_recv()
            total = (sr[a, 0] + sr[a, 1]) + (sr[a, 2] + sr[a, 3])
            if a < 2:
                sm[a + 1] = total
            else:
                done(total[0:16], sm[2][16:24])

        cm.when(times[1] + 0.01)(begin) if a == 0 else cm.when(times[1 + a] + 0.01)(begin)
        cm.when(times[2 + a])(end)


def greet_all(cm):
    cm.greet([axis(n) for n in (1, 2, 3) for axis in (cm.at_x, cm.at_z, cm.at_y)] + [cm.twin()])


def front_kernel(gated, ow, tokens, o_resid, o_full, o_own, GF, WF, ys, yr, ws, wr):
    cm = Comm()
    x, z, c, me = cm.x, cm.z, cm.core, cm.me
    R, L, O = ahead(me, 1), ahead(me, 3), ahead(me, 2)
    cm.greet([cm.at_x(1), cm.at_x(3), cm.at_z(1), cm.at_z(3), cm.at_y(1), cm.at_y(2), cm.at_y(3), cm.twin()])
    T = gated.shape[0]
    N = T // 2
    piece = ((x * 4 + z) * 2 + c) * 32
    h = {}

    def weight(name, ref, i, dev):
        h[name] = cm.send(ref, ref, ws.at[i], wr.at[i], dev)

    def gate(name, ref, i, n):
        h[name] = cm.send(ref, ref, ys.at[i], yr.at[i], cm.at_y(n))

    low, high = pl.ds(0, 2), pl.ds(2, 2)
    WF[x, z, c, me] = ow[pl.ds(pl.multiple_of(piece, 32), 32), :].astype(jnp.float32)
    for n in (1, 2, 3):
        weight(("y", n), WF.at[x, z, c, me], n - 1, cm.at_y(n))
    GF[me] = gated[...].astype(jnp.float32)
    first, second = pl.ds(0, N), pl.ds(N, N)
    gate("r0", GF.at[me, first], 0, 1)
    gate("l1", GF.at[me, second], 1, 3)
    gate("r1", GF.at[me, second], 2, 1)
    gate("l0", GF.at[me, first], 3, 3)
    for n in (1, 2, 3):
        h["y", n].wait_recv()
    weight("ax1", WF.at[x, z, c, low], 3, cm.at_x(1))
    weight("ax3", WF.at[x, z, c, low], 4, cm.at_x(3))
    weight("bz1", WF.at[x, z, c, high], 5, cm.at_z(1))
    weight("bz3", WF.at[x, z, c, high], 6, cm.at_z(3))
    o_resid[...] = tokens[...].astype(jnp.float32) + lax.dot_general(
        gated[...], ow[...], (((1,), (1,)), ((), ())), preferred_element_type=jnp.float32
    )
    xl, xr, zl, zr = ahead(x, 3), ahead(x, 1), ahead(z, 3), ahead(z, 1)
    h["ax1"].wait_recv()
    weight("ax1f", WF.at[xl, z, c, 0], 7, cm.at_x(1))
    h["ax3"].wait_recv()
    weight("ax3f", WF.at[xr, z, c, 1], 8, cm.at_x(3))
    h["bz1"].wait_recv()
    weight("bz1f", WF.at[x, zl, c, 2], 9, cm.at_z(1))
    h["bz3"].wait_recv()
    weight("bz3f", WF.at[x, zr, c, 3], 10, cm.at_z(3))
    h["ax1f"].wait_recv()
    h["ax3f"].wait_recv()
    weight("az1", WF.at[:, z, c, low], 11, cm.at_z(1))
    weight("az3", WF.at[:, z, c, low], 12, cm.at_z(3))
    h["bz1f"].wait_recv()
    h["bz3f"].wait_recv()
    weight("bx1", WF.at[x, :, c, high], 13, cm.at_x(1))
    weight("bx3", WF.at[x, :, c, high], 14, cm.at_x(3))
    h["r0"].wait_recv()
    gate("r0f", GF.at[L, first], 4, 1)
    h["l1"].wait_recv()
    gate("l1f", GF.at[R, second], 5, 3)
    h["az1"].wait_recv()
    weight("az1f", WF.at[:, zl, c, 0], 15, cm.at_z(1))
    h["az3"].wait_recv()
    weight("az3f", WF.at[:, zr, c, 1], 16, cm.at_z(3))
    h["bx1"].wait_recv()
    weight("bx1f", WF.at[xl, :, c, 2], 17, cm.at_x(1))
    h["bx3"].wait_recv()
    weight("bx3f", WF.at[xr, :, c, 3], 18, cm.at_x(3))
    for name in ("az1f", "az3f", "bx1f", "bx3f"):
        h[name].wait_recv()
    weight("twin", WF.at[:, :, c], 19, cm.twin())
    h["r1"].wait_recv()
    h["l0"].wait_recv()
    h["twin"].wait_recv()
    for k in range(4):
        o_full[k] = WF[:, :, :, k].reshape(1024, 256).astype(jnp.bfloat16)
    mine = pl.ds(pl.multiple_of(me * (T // 4), T // 4), T // 4)

    def add(k):
        low_gated = GF[k].astype(jnp.bfloat16)
        o_resid[...] += lax.dot_general(
            low_gated, o_full[k], (((1,), (1,)), ((), ())), preferred_element_type=jnp.float32
        )

    add(L)
    add(R)
    h["r0f"].wait_recv()
    h["l1f"].wait_recv()
    add(O)
    for k in range(4):
        o_own[:, 256 * k : 256 * (k + 1)] = GF[k, mine, :].astype(jnp.bfloat16)
    cm.run()


def middle_kernel(*refs):
    (dn, own_resid, gain, own_cot, normed, d_gate, d_up, act, cot, down, ow) = refs[:11]
    (o_dres, o_dgated, o_res, o_gate, o_up, o_down) = refs[11:17]
    (rp, full, turned, relay, yt, yf, G, RC) = refs[17:25]
    bufs, (ys, yr), sems, (xs, xr) = refs[25:33], refs[33:35], refs[35:41], refs[41:]
    H = own_resid.shape[0] // 2
    cm = Comm()
    greet_all(cm)

    def finish_dres(half, total):
        mine = pl.ds(half * H, H)
        return norm_back_rows(total, own_resid[mine, :], gain[...], own_cot[mine, :].astype(jnp.float32))

    def finish_result(half, total):
        return total + own_resid[pl.ds(half * H, H), :]

    def rounded():
        o_res[...] = full[...].astype(jnp.bfloat16)

    @cm.when(0.02)
    def _():
        rp[...] = lax.dot_general(
            act[...], down[...], (((1,), (1,)), ((), ())), preferred_element_type=jnp.float32
        )

    head_sum(cm, dn, o_dres, yt.at[0], yf.at[0], ys.at[0], yr.at[0], finish_dres, (0, 7, 20, 0), lambda: None, False)
    head_sum(cm, rp, full, yt.at[1], yf.at[1], ys.at[1], yr.at[1], finish_result, (7.05, 19, 33, 44), rounded)

    C = 2 * H
    R, L = ahead(cm.me, 1), ahead(cm.me, 3)
    c = {}

    def rows(k, half=None):
        if half is None:
            return pl.ds(pl.multiple_of(k * C, C), C)
        return pl.ds(pl.multiple_of(k * C + half * H, H), H)

    def go(name, src, dst, i, n):
        c[name] = cm.send(src, dst, xs.at[i], xr.at[i], cm.at_y(n))

    @cm.when(20.1)
    def _():
        low = o_dres[...].astype(jnp.bfloat16)
        for turn in (2, 1, 3):
            turned[turn - 1] = jnp.dot(low, ow[ahead(cm.me, turn)], preferred_element_type=jnp.float32)
            if turn == 2:
                go("e0", turned.at[1, pl.ds(0, H)], relay.at[0], 0, 1)
                go("e1", turned.at[1, pl.ds(H, H)], relay.at[1], 1, 3)
            else:
                go(("d", turn), turned.at[turn - 1], o_dgated.at[rows(cm.me)], 1 + turn, turn)
        o_dgated[rows(cm.me), :] = jnp.dot(low, ow[cm.me], preferred_element_type=jnp.float32)

    @cm.when(25)
    def _():
        c["e0"].wait_recv()
        go("f0", relay.at[0], o_dgated.at[rows(L, 0)], 5, 1)
        c["e1"].wait_recv()
        go("f1", relay.at[1], o_dgated.at[rows(R, 1)], 6, 3)

    @cm.when(901)
    def _():
        for name in (("d", 1), ("d", 3), "f0", "f1"):
            c[name].wait_recv()

    w = act.shape[1]
    wa = 1792

    def done_a():
        rows = G[cm.x, cm.z, cm.core, :, pl.ds(0, wa)]
        o_gate[...] = rows[:, :w]
        o_up[:, pl.ds(0, wa - w)] = rows[:, w:]

    def done_b():
        rows = G[cm.x, cm.z, cm.core, :, pl.ds(wa, 3 * w - wa)]
        o_up[:, pl.ds(wa - w, 2 * w - wa)] = rows[:, : 2 * w - wa]
        o_down[...] = rows[:, 2 * w - wa :]

    times = {
        "block": (4, 5.5, 7.5, 9),
        "settle": (7.1, 8.5, 10, 12),
        "A": (7.2, 8.6, 10.1, 18.5, 42),
        "B": (12.1, 12.2, 12.3, 24, 45),
        "A2": (42.1, 42.2, 42.3, 46, 52),
        "B2": (45.1, 45.2, 45.3, 49, 55),
    }
    products = [(normed, [d_gate], 0), (normed, [d_up], w), (cot, [act], 2 * w)]
    grad_scatter(cm, products, G, RC, wa, bufs, sems, times, done_a, done_b)
    cm.run()


def end_kernel(*refs):
    (dm, toks, gain, d_res, normed) = refs[:5]
    d_proj = refs[5:8]
    (d_low, gated, small) = refs[8:11]
    (o_tok, o_in, o_out, o_mix, o_ffn, o_conv) = refs[11:17]
    (yt, yf, G, RC) = refs[17:21]
    bufs = refs[21:29]
    sm, sr = refs[29:31]
    ys, yr = refs[31:33]
    sems = refs[33:39]
    ss, sr_sem = refs[39:41]
    mine, theirs, hs, hr = refs[41:]
    H = toks.shape[0] // 2
    cm = Comm()
    greet_all(cm)

    def finish_tokens(half, total):
        mine = pl.ds(half * H, H)
        return norm_back_rows(total, toks[mine, :].astype(jnp.float32), gain[...], d_res[mine, :])

    head_sum(cm, dm, o_tok, yt, yf, ys, yr, finish_tokens, (0, 6.5, 17, 26), lambda: None)

    wa = 768
    heads = []

    def done_a():
        rows = G[cm.x, cm.z, cm.core, :, pl.ds(0, wa)]
        for k in range(3):
            o_in[k] = rows[:, 256 * k : 256 * (k + 1)]

    def done_b():
        rows = G[cm.x, cm.z, cm.core, :, pl.ds(wa, 1024)]
        for k in range(4):
            mine[k] = rows[:, 256 * k : 256 * (k + 1)]
        for n in (1, 2, 3):
            heads.append(
                cm.send(mine.at[ahead(cm.me, n)], theirs.at[n - 1], hs.at[n - 1], hr.at[n - 1], cm.at_y(n))
            )

    @cm.when(950)
    def _():
        for copy in heads:
            copy.wait_recv()
        o_out[...] = (mine[cm.me] + theirs[0]) + (theirs[1] + theirs[2])

    times = {
        "block": (0.1, 1, 2, 3),
        "settle": (2, 3, 4, 5),
        "A": (2.1, 3.1, 4.1, 7.5, 19),
        "B": (5.1, 5.2, 5.3, 12, 23),
        "A2": (19.1, 19.2, 19.3, 21.5, 25.5),
        "B2": (23.1, 23.2, 23.3, 25.7, 28),
    }
    products = [(normed, d_proj, 0), (d_low, [gated], 768)]
    grad_scatter(cm, products, G, RC, wa, bufs, sems, times, done_a, done_b)

    def small_done(gains, rest):
        o_mix[...] = gains[0:8]
        o_ffn[...] = gains[8:16]
        for k in range(3):
            for h in range(2):
                o_conv[k : k + 1, pl.ds(128 * h, 128)] = rest[2 * k + h : 2 * k + h + 1]

    small_sums(cm, small, sm, sr, ss, sr_sem, (0.05, 5, 9, 15, 22), small_done)
    cm.run()


VMEM_SPEC = pl.BlockSpec(memory_space=pltpu.VMEM)


def call(kernel, name, cid, args, outs, scratch, limit):
    return pl.pallas_call(
        kernel,
        out_shape=outs,
        in_specs=[VMEM_SPEC] * len(args),
        out_specs=(VMEM_SPEC,) * len(outs),
        scratch_shapes=scratch,
        compiler_params=pltpu.CompilerParams(
            collective_id=cid, has_side_effects=True, vmem_limit_bytes=limit << 20
        ),
        cost_estimate=pl.CostEstimate(flops=1, bytes_accessed=1, transcendentals=0),
        name=name,
    )(*args)


def scatter_scratch(W, wa):
    f32 = jnp.float32
    wb = W - wa
    return [
        pltpu.VMEM((4, 4, 2, 32, W), f32),
        pltpu.VMEM((4, 4, 32, W), f32),
        pltpu.VMEM((2, 2, 32, wa), f32),
        pltpu.VMEM((2, 2, 32, wb), f32),
        pltpu.VMEM((2, 2, 2, 32, wa), f32),
        pltpu.VMEM((2, 2, 2, 32, wb), f32),
        pltpu.VMEM((2, 1, 16, wa), f32),
        pltpu.VMEM((2, 1, 16, wb), f32),
        pltpu.VMEM((2, 2, 1, 16, wa), f32),
        pltpu.VMEM((2, 2, 1, 16, wb), f32),
    ]


SCATTER_SEMS = [pltpu.SemaphoreType.DMA((n,)) for n in (4, 4, 12, 12, 12, 12)]


def front(gated, ow, tokens):
    T, D = tokens.shape
    f32, shape, dma = jnp.float32, jax.ShapeDtypeStruct, pltpu.SemaphoreType.DMA
    outs = (
        shape((T, D), f32),
        shape((4, *ow.shape), jnp.bfloat16),
        shape((T // 4, D), jnp.bfloat16),
    )
    scratch = [
        pltpu.VMEM((4, *gated.shape), f32),
        pltpu.VMEM((4, 4, 2, 4, 32, ow.shape[1]), f32),
        dma((6,)),
        dma((6,)),
        dma((20,)),
        dma((20,)),
    ]
    return call(front_kernel, "front", 3, (gated, ow, tokens), outs, scratch, 24)


def middle(dn, own_resid, gain, own_cot, normed, d_gate, d_up, act, cot, down, ow):
    T, D = dn.shape
    H = T // 8
    f32, shape, dma = jnp.float32, jax.ShapeDtypeStruct, pltpu.SemaphoreType.DMA
    w = act.shape[1]
    outs = (shape((T // 4, D), f32), shape((T, 256), f32), shape((T, D), jnp.bfloat16)) + (shape((32, w), f32),) * 3
    scratch = [
        pltpu.VMEM((T, D), f32),
        pltpu.VMEM((T, D), f32),
        pltpu.VMEM((3, 2 * H, 256), f32),
        pltpu.VMEM((2, H, 256), f32),
        pltpu.VMEM((2, 2, H, D), f32),
        pltpu.VMEM((2, 2, 2, H, D), f32),
        *scatter_scratch(3 * w, 1792),
        dma((2, 12)),
        dma((2, 12)),
        *SCATTER_SEMS,
        dma((7,)),
        dma((7,)),
    ]
    args = (dn, own_resid, gain, own_cot, normed, d_gate, d_up, act, cot, down, ow)
    return call(middle_kernel, "middle", 5, args, outs, scratch, 56)


def end(dm, toks, gain, d_res, normed, d_proj, d_low, gated, small):
    T, D = dm.shape
    H = T // 8
    f32, shape, dma = jnp.float32, jax.ShapeDtypeStruct, pltpu.SemaphoreType.DMA
    outs = (
        shape((T, D), f32),
        shape((3, 32, 256), f32),
        shape((32, 256), f32),
        shape((8, 128), f32),
        shape((8, 128), f32),
        shape((3, 256), f32),
    )
    scratch = [
        pltpu.VMEM((2, H, D), f32),
        pltpu.VMEM((2, 2, H, D), f32),
        *scatter_scratch(1792, 768),
        pltpu.VMEM((3, 24, 128), f32),
        pltpu.VMEM((4, 4, 24, 128), f32),
        dma((12,)),
        dma((12,)),
        *SCATTER_SEMS,
        dma((10,)),
        dma((10,)),
        pltpu.VMEM((4, 32, 256), f32),
        pltpu.VMEM((3, 32, 256), f32),
        dma((3,)),
        dma((3,)),
    ]
    args = (dm, toks, gain, d_res, normed, *d_proj, d_low, gated, small)
    return call(end_kernel, "end", 7, args, outs, scratch, 40)


def place(*arrays):
    n = len(arrays)

    def kernel(*refs):
        copies = [pltpu.make_async_copy(refs[i], refs[n + i], refs[2 * n].at[i]) for i in range(n)]
        for copy in copies:
            copy.start()
        for copy in copies:
            copy.wait()

    anywhere = pl.BlockSpec(memory_space=pl.ANY)
    return pl.pallas_call(
        kernel,
        out_shape=tuple(jax.ShapeDtypeStruct(a.shape, a.dtype) for a in arrays),
        in_specs=[VMEM_SPEC] * n,
        out_specs=(anywhere,) * n,
        scratch_shapes=[pltpu.SemaphoreType.DMA((n,))],
        name="place",
    )(*arrays)


def from_behind(block, axis, distance):
    devices = range(lax.axis_size(axis))
    route = [(i - distance, i) for i in devices if i - distance in devices]
    return lax.ppermute(block, axis, route)


def rms_scale(values):
    return lax.rsqrt(jnp.mean(values * values, axis=-1, keepdims=True) + EPS)


def right_product(left, right):
    return lax.dot_general(
        left, right, (((1,), (1,)), ((), ())), preferred_element_type=jnp.float32
    )


def on_device(
    tokens,
    segment_ids,
    mix_gain,
    in_weight,
    conv_weight,
    out_weight,
    ffn_gain,
    gate_weight,
    up_weight,
    down_weight,
    cotangent,
):
    tok_rows = tokens.shape[0]
    own = tok_rows // HEADS
    own_at = lax.axis_index("head") * own

    def own_rows(x):
        return lax.dynamic_slice_in_dim(x, own_at, own, 0)

    first_row = lax.axis_index("seq") * tok_rows
    padded_ids = jnp.concatenate(
        [jnp.full((2,), -1, jnp.int32), segment_ids, jnp.full((2,), -2, jnp.int32)]
    )
    id_window = lax.dynamic_slice_in_dim(padded_ids, first_row, tok_rows + 4)
    near_ext = (id_window[2 : tok_rows + 4] == id_window[1 : tok_rows + 3]).astype(jnp.float32)
    far_ext = (id_window[2 : tok_rows + 4] == id_window[0 : tok_rows + 2]).astype(jnp.float32)
    near_own = near_ext[:tok_rows, None]
    far_own = far_ext[:tok_rows, None]
    inputs = tokens.astype(jnp.float32)
    mix_scale = rms_scale(inputs)
    mix_normed = (inputs * mix_scale * mix_gain).astype(jnp.bfloat16)
    projected = jnp.einsum("td,dkc->tkc", mix_normed, in_weight, preferred_element_type=jnp.float32)
    chan_b = projected[:, 0]
    chan_c = projected[:, 1]
    chan_x = projected[:, 2]
    mixed = chan_b * chan_x
    edge_rows = from_behind(mixed[tok_rows - 2 :], "seq", 1)
    extended = jnp.concatenate([edge_rows, mixed])
    kernel = conv_weight.astype(jnp.float32)
    prev_one = extended[1 : tok_rows + 1]
    prev_two = extended[0:tok_rows]
    conv_out = kernel[0] * mixed + kernel[1] * near_own * prev_one + kernel[2] * far_own * prev_two
    gated = (chan_c * conv_out).astype(jnp.bfloat16)
    resid, out_full, gated_rows = front(gated, out_weight, tokens)
    ffn_scale = rms_scale(resid)
    ffn_normed = (resid * ffn_scale * ffn_gain).astype(jnp.bfloat16)
    gate = jnp.dot(ffn_normed, gate_weight, preferred_element_type=jnp.float32)
    upper = jnp.dot(ffn_normed, up_weight, preferred_element_type=jnp.float32)
    sigma = jax.nn.sigmoid(gate)
    act = (gate * sigma * upper).astype(jnp.bfloat16)
    d_act = jnp.dot(cotangent, down_weight, preferred_element_type=jnp.float32)
    d_gate = (d_act * upper * sigma * (1.0 + gate * (1.0 - sigma))).astype(jnp.bfloat16)
    d_up = (d_act * gate * sigma).astype(jnp.bfloat16)
    d_normed_part = right_product(d_gate, gate_weight) + right_product(d_up, up_weight)
    grad_ffn_gain = jnp.sum(d_normed_part * resid * ffn_scale, axis=0)
    d_resid, d_gated, result, gate_share, up_share, down_share = middle(
        d_normed_part,
        own_rows(resid),
        ffn_gain[None],
        own_rows(cotangent),
        ffn_normed,
        d_gate,
        d_up,
        act,
        cotangent,
        down_weight,
        out_full,
    )
    d_chan_c = d_gated * conv_out
    d_conv = d_gated * chan_c
    tail_rows = from_behind(d_conv[:2], "seq", -1)
    later = jnp.concatenate([d_conv, tail_rows])
    next_one = later[1 : tok_rows + 1]
    next_two = later[2 : tok_rows + 2]
    near_next = near_ext[1 : tok_rows + 1, None]
    far_next = far_ext[2 : tok_rows + 2, None]
    d_mixed = kernel[0] * d_conv + kernel[1] * near_next * next_one + kernel[2] * far_next * next_two
    grad_conv = jnp.stack(
        [
            jnp.sum(d_conv * mixed, axis=0),
            jnp.sum(d_conv * near_own * prev_one, axis=0),
            jnp.sum(d_conv * far_own * prev_two, axis=0),
        ]
    )
    d_projected = [p.astype(jnp.bfloat16) for p in (d_mixed * chan_x, d_chan_c, d_mixed * chan_b)]
    d_mix_part = jnp.einsum(
        "tkc,dkc->td",
        jnp.stack(d_projected, axis=1),
        in_weight,
        preferred_element_type=jnp.float32,
    )
    grad_mix_gain = jnp.sum(d_mix_part * inputs * mix_scale, axis=0)
    small = jnp.concatenate(
        [
            grad_mix_gain.reshape(8, 128),
            grad_ffn_gain.reshape(8, 128),
            grad_conv.reshape(6, 128),
            jnp.zeros((2, 128), jnp.float32),
        ]
    )
    grad_tokens, in_share, out_share, mix_total, ffn_total, conv_total = end(
        d_mix_part,
        own_rows(tokens),
        mix_gain[None],
        d_resid,
        mix_normed,
        d_projected,
        d_resid.astype(jnp.bfloat16),
        gated_rows,
        small,
    )
    (
        result,
        grad_tokens,
        mix_total,
        in_share,
        conv_total,
        out_share,
        ffn_total,
        gate_share,
        up_share,
        down_share,
    ) = place(
        result,
        grad_tokens,
        mix_total,
        in_share,
        conv_total,
        out_share,
        ffn_total,
        gate_share,
        up_share,
        down_share,
    )
    return (
        result,
        grad_tokens,
        mix_total.reshape(-1),
        in_share.transpose(1, 0, 2),
        conv_total,
        out_share,
        ffn_total.reshape(-1),
        gate_share,
        up_share,
        down_share,
    )


def solution(mesh):
    placed = (
        P("seq", None),
        P(),
        P(),
        P(None, None, "head"),
        P(None, "head"),
        P(None, "head"),
        P(),
        P(None, "head"),
        P(None, "head"),
        P(None, "head"),
        P("seq", None),
    )
    return jax.shard_map(
        on_device,
        mesh=mesh,
        in_specs=placed,
        out_specs=(
            P("seq", None),
            P("seq", None),
            P(),
            P("seq", None, "head"),
            P(None, "head"),
            P("seq", "head"),
            P(),
            P("seq", "head"),
            P("seq", "head"),
            P("seq", "head"),
        ),
        check_vma=False,
    )
```

```python
import jax
import jax.numpy as jnp
from jax import lax
from jax.experimental import pallas as pl
from jax.experimental.pallas import tpu as pltpu
from jax.sharding import PartitionSpec as P

EPS = 1e-05
MESH = pl.DeviceIdType.MESH


def norm_back_rows(grad_normed, values, gain, extra):
    scale = lax.rsqrt(jnp.mean(values * values, axis=-1, keepdims=True) + EPS)
    weighted = grad_normed * gain
    inner = jnp.mean(weighted * values, axis=-1, keepdims=True)
    grad_values = extra + (scale * weighted - values * (scale * scale * scale) * inner)
    return grad_values, jnp.sum(grad_normed * values * scale, axis=0, keepdims=True)


class Comm:
    def __init__(self):
        seq = lax.axis_index("seq")
        self.me = lax.axis_index("head")
        self.core = lax.rem(seq, 2)
        self.z = lax.rem(lax.div(seq, 2), 4)
        self.x = lax.div(seq, 8)
        self.every = []
        self.steps = []

    def at_x(self, n):
        return {"seq": (ahead(self.x, n) * 4 + self.z) * 2 + self.core, "head": self.me}

    def at_z(self, n):
        return {"seq": (self.x * 4 + ahead(self.z, n)) * 2 + self.core, "head": self.me}

    def at_y(self, n):
        return {"seq": (self.x * 4 + self.z) * 2 + self.core, "head": ahead(self.me, n)}

    def twin(self, n=1):
        return {"seq": (self.x * 4 + self.z) * 2 + (1 - self.core), "head": self.me}

    def greet(self, devices):
        barrier = pltpu.get_barrier_semaphore()
        for device in devices:
            pl.semaphore_signal(barrier, inc=1, device_id=device, device_id_type=MESH)
        pl.semaphore_wait(barrier, len(devices))

    def send(self, src, dst, s_sem, r_sem, dev):
        copy = pltpu.make_async_remote_copy(
            src_ref=src, dst_ref=dst, send_sem=s_sem, recv_sem=r_sem, device_id=dev, device_id_type=MESH
        )
        copy.start()
        self.every.append(copy)
        return copy

    def when(self, time):
        def add(fn):
            self.steps.append((time, len(self.steps), fn))
            return fn

        return add

    def run(self):
        for _, _, fn in sorted(self.steps, key=lambda s: s[:2]):
            fn()
        for copy in self.every:
            copy.wait_send()


def ahead(k, n):
    return lax.rem(k + n, 4)


def add_up(dst, *srcs):
    n, r = dst.shape[:2]
    q = r // 8

    def body(i, carry):
        b, at = lax.div(i, q), pl.ds(pl.multiple_of(lax.rem(i, q) * 8, 8), 8)
        total = dst[b, at, :]
        for src in srcs:
            total = total + src[b, at, :]
        dst[b, at, :] = total
        return carry

    lax.fori_loop(0, n * q, body, 0)


def head_sum(cm, p, o, t, f, s_sem, r_sem, finish, times, closing, share=True):
    T = p.shape[0]
    C = T // 4
    H = C // 2
    R, L, O = ahead(cm.me, 1), ahead(cm.me, 3), ahead(cm.me, 2)
    me = cm.me
    c = {}

    def rows(k, half):
        return pl.ds(pl.multiple_of(k * C + half * H, H), H)

    def go(name, src, dst, i, n):
        c[name] = cm.send(src, dst, s_sem.at[i], r_sem.at[i], cm.at_y(n))

    @cm.when(times[0])
    def _():
        go("a0", p.at[rows(O, 0)], t.at[0], 0, 1)
        go("a1", p.at[rows(O, 1)], t.at[1], 1, 3)
        go("a2", p.at[rows(R, 1)], f.at[0, 1], 2, 1)
        go("a3", p.at[rows(L, 0)], f.at[1, 0], 3, 3)

    @cm.when(times[1])
    def _():
        c["a0"].wait_recv()
        t[0] = p[rows(R, 0), :] + t[0]
        go("a4", t.at[0], f.at[0, 0], 4, 1)
        c["a1"].wait_recv()
        t[1] = p[rows(L, 1), :] + t[1]
        go("a5", t.at[1], f.at[1, 1], 5, 3)

    @cm.when(times[2])
    def _():
        c["a3"].wait_recv()
        c["a4"].wait_recv()
        first = finish(0, p[rows(me, 0), :] + f[0, 0] + f[1, 0])
        if not share:
            c["a2"].wait_recv()
            c["a5"].wait_recv()
            o[0:H, :] = first
            o[H:C, :] = finish(1, p[rows(me, 1), :] + f[0, 1] + f[1, 1])
            return
        o[rows(me, 0), :] = first
        go("b0", o.at[rows(me, 0)], o.at[rows(me, 0)], 6, 1)
        go("c0", o.at[rows(me, 0)], o.at[rows(me, 0)], 8, 3)
        c["a2"].wait_recv()
        c["a5"].wait_recv()
        o[rows(me, 1), :] = finish(1, p[rows(me, 1), :] + f[0, 1] + f[1, 1])
        go("c1", o.at[rows(me, 1)], o.at[rows(me, 1)], 9, 3)
        go("b1", o.at[rows(me, 1)], o.at[rows(me, 1)], 7, 1)

    if not share:
        return

    @cm.when(times[3])
    def _():
        c["b0"].wait_recv()
        go("d0", o.at[rows(L, 0)], o.at[rows(L, 0)], 10, 1)
        c["c1"].wait_recv()
        go("d1", o.at[rows(R, 1)], o.at[rows(R, 1)], 11, 3)

    @cm.when(900)
    def _():
        for name in ("b1", "c0", "d0", "d1"):
            c[name].wait_recv()
        closing()


def scatter_ring(cm, chunk, t, f, s_sem, r_sem, base, to, times, done):
    c = {}

    def go(name, src, dst, i, n):
        c[name] = cm.send(src, dst, s_sem.at[base + i], r_sem.at[base + i], to(n))

    @cm.when(times[0])
    def _():
        go("a0", chunk(2, 0), t.at[0], 0, 1)
        go("a1", chunk(2, 1), t.at[1], 1, 3)

    @cm.when(times[1])
    def _():
        go("a2", chunk(1, 1), f.at[0, 1], 2, 1)

    @cm.when(times[2])
    def _():
        go("a3", chunk(3, 0), f.at[1, 0], 3, 3)

    @cm.when(times[3])
    def _():
        c["a0"].wait_recv()
        add_up(t.at[0], chunk(1, 0))
        go("a4", t.at[0], f.at[0, 0], 4, 1)
        c["a1"].wait_recv()
        add_up(t.at[1], chunk(3, 1))
        go("a5", t.at[1], f.at[1, 1], 5, 3)

    @cm.when(times[4])
    def _():
        c["a3"].wait_recv()
        c["a4"].wait_recv()
        add_up(chunk(0, 0), f.at[0, 0], f.at[1, 0])
        c["a2"].wait_recv()
        c["a5"].wait_recv()
        add_up(chunk(0, 1), f.at[0, 1], f.at[1, 1])
        done()


def grad_scatter(cm, products, G, RC, wa, bufs, sems, times, done_a, done_b):
    tA, tB, fA, fB, t2A, t2B, f2A, f2B = bufs
    cs, cr, as_, ar, bs, br = sems
    W = G.shape[-1]
    quarter = products[0][0].shape[1] // 4
    got = {}

    def block(turn):
        k = ahead(cm.x, turn)
        for left, rights, at in products:
            right = jnp.concatenate([r[...] for r in rights], axis=1)
            w = right.shape[1]
            lhs = left[:, pl.ds(pl.multiple_of(k * quarter, quarter), quarter)]
            value = lax.dot_general(
                lhs, right, (((0,), (0,)), ((), ())), preferred_element_type=jnp.float32
            )
            G[k, :, :, :, pl.ds(at, w)] = value.reshape(4, 2, 32, w)
        got[turn] = cm.send(G.at[k, :, 1 - cm.core], RC.at[k], cs.at[turn], cr.at[turn], cm.twin())

    def settle(turn):
        k = ahead(cm.x, turn)
        got[turn].wait_recv()
        add_up(G.at[k, :, cm.core], RC.at[k])

    for i, turn in enumerate((2, 1, 3, 0)):
        cm.when(times["block"][i])(lambda turn=turn: block(turn))
        cm.when(times["settle"][i])(lambda turn=turn: settle(turn))

    cols_a, cols_b = pl.ds(0, wa), pl.ds(wa, W - wa)
    core = cm.core

    def a1(turn, half):
        return G.at[ahead(cm.x, turn), pl.ds(half * 2, 2), core, :, cols_a]

    def b1(turn, half):
        return G.at[pl.ds(half * 2, 2), ahead(cm.z, turn), core, :, cols_b]

    def a2(turn, half):
        return G.at[cm.x, pl.ds(ahead(cm.z, turn), 1), core, pl.ds(half * 16, 16), cols_a]

    def b2(turn, half):
        return G.at[pl.ds(ahead(cm.x, turn), 1), cm.z, core, pl.ds(half * 16, 16), cols_b]

    nothing = lambda: None
    scatter_ring(cm, a1, tA, fA, as_, ar, 0, cm.at_x, times["A"], nothing)
    scatter_ring(cm, b1, tB, fB, bs, br, 0, cm.at_z, times["B"], nothing)
    scatter_ring(cm, a2, t2A, f2A, as_, ar, 6, cm.at_z, times["A2"], done_a)
    scatter_ring(cm, b2, t2B, f2B, bs, br, 6, cm.at_x, times["B2"], done_b)


def small_sums(cm, small, sm, sr, s_sem, r_sem, times, done):
    axes = [(cm.at_z, cm.z), (cm.at_x, cm.x), (cm.at_y, cm.me)]
    first = {}

    @cm.when(times[0])
    def _():
        first["c"] = cm.send(small, sr.at[3, 0], s_sem.at[9], r_sem.at[9], cm.twin())

    @cm.when(times[1])
    def _():
        first["c"].wait_recv()
        sm[0] = small[...] + sr[3, 0]

    for a, (to, here) in enumerate(axes):
        copies = []

        def begin(a=a, to=to, here=here, copies=copies):
            sr[a, here] = sm[a]
            for n in (1, 2, 3):
                i = a * 3 + n - 1
                copies.append(cm.send(sm.at[a], sr.at[a, here], s_sem.at[i], r_sem.at[i], to(n)))

        def end(a=a, copies=copies):
            for copy in copies:
                copy.wait_recv()
            total = (sr[a, 0] + sr[a, 1]) + (sr[a, 2] + sr[a, 3])
            if a < 2:
                sm[a + 1] = total
            else:
                done(total[0:16], sm[2][16:24])

        cm.when(times[1] + 0.01)(begin) if a == 0 else cm.when(times[1 + a] + 0.01)(begin)
        cm.when(times[2 + a])(end)


def greet_all(cm):
    cm.greet([axis(n) for n in (1, 2, 3) for axis in (cm.at_x, cm.at_z, cm.at_y)] + [cm.twin()])


def front_kernel(
    gated, ow, tokens, cot, down, gain, o_normed, o_full, o_own, o_dact, o_resid, o_cot, o_tok, resid, GF, WF, ys, yr, ws, wr
):
    cm = Comm()
    x, z, c, me = cm.x, cm.z, cm.core, cm.me
    R, L, O = ahead(me, 1), ahead(me, 3), ahead(me, 2)
    cm.greet([cm.at_x(1), cm.at_x(3), cm.at_z(1), cm.at_z(3), cm.at_y(1), cm.at_y(2), cm.at_y(3), cm.twin()])
    T = gated.shape[0]
    N = T // 2
    piece = ((x * 4 + z) * 2 + c) * 32
    h = {}

    def weight(name, ref, i, dev):
        h[name] = cm.send(ref, ref, ws.at[i], wr.at[i], dev)

    def gate(name, ref, i, n):
        h[name] = cm.send(ref, ref, ys.at[i], yr.at[i], cm.at_y(n))

    low, high = pl.ds(0, 2), pl.ds(2, 2)
    WF[x, z, c, me] = ow[pl.ds(pl.multiple_of(piece, 32), 32), :].astype(jnp.float32)
    for n in (1, 2, 3):
        weight(("y", n), WF.at[x, z, c, me], n - 1, cm.at_y(n))
    GF[me] = gated[...].astype(jnp.float32)
    first, second = pl.ds(0, N), pl.ds(N, N)
    gate("r0", GF.at[me, first], 0, 1)
    gate("l1", GF.at[me, second], 1, 3)
    gate("r1", GF.at[me, second], 2, 1)
    gate("l0", GF.at[me, first], 3, 3)
    for n in (1, 2, 3):
        h["y", n].wait_recv()
    weight("ax1", WF.at[x, z, c, low], 3, cm.at_x(1))
    weight("ax3", WF.at[x, z, c, low], 4, cm.at_x(3))
    weight("bz1", WF.at[x, z, c, high], 5, cm.at_z(1))
    weight("bz3", WF.at[x, z, c, high], 6, cm.at_z(3))
    resid[...] = tokens[...].astype(jnp.float32) + lax.dot_general(
        gated[...], ow[...], (((1,), (1,)), ((), ())), preferred_element_type=jnp.float32
    )
    mine = pl.ds(pl.multiple_of(me * (T // 4), T // 4), T // 4)
    o_cot[...] = cot[mine, :]
    o_tok[...] = tokens[mine, :]
    xl, xr, zl, zr = ahead(x, 3), ahead(x, 1), ahead(z, 3), ahead(z, 1)
    h["ax1"].wait_recv()
    weight("ax1f", WF.at[xl, z, c, 0], 7, cm.at_x(1))
    h["ax3"].wait_recv()
    weight("ax3f", WF.at[xr, z, c, 1], 8, cm.at_x(3))
    h["bz1"].wait_recv()
    weight("bz1f", WF.at[x, zl, c, 2], 9, cm.at_z(1))
    h["bz3"].wait_recv()
    weight("bz3f", WF.at[x, zr, c, 3], 10, cm.at_z(3))
    h["ax1f"].wait_recv()
    h["ax3f"].wait_recv()
    weight("az1", WF.at[:, z, c, low], 11, cm.at_z(1))
    weight("az3", WF.at[:, z, c, low], 12, cm.at_z(3))
    h["bz1f"].wait_recv()
    h["bz3f"].wait_recv()
    weight("bx1", WF.at[x, :, c, high], 13, cm.at_x(1))
    weight("bx3", WF.at[x, :, c, high], 14, cm.at_x(3))
    o_dact[...] = jnp.dot(cot[...], down[...], preferred_element_type=jnp.float32)
    h["r0"].wait_recv()
    gate("r0f", GF.at[L, first], 4, 1)
    h["l1"].wait_recv()
    gate("l1f", GF.at[R, second], 5, 3)
    h["az1"].wait_recv()
    weight("az1f", WF.at[:, zl, c, 0], 15, cm.at_z(1))
    h["az3"].wait_recv()
    weight("az3f", WF.at[:, zr, c, 1], 16, cm.at_z(3))
    h["bx1"].wait_recv()
    weight("bx1f", WF.at[xl, :, c, 2], 17, cm.at_x(1))
    h["bx3"].wait_recv()
    weight("bx3f", WF.at[xr, :, c, 3], 18, cm.at_x(3))
    for name in ("az1f", "az3f", "bx1f", "bx3f"):
        h[name].wait_recv()
    weight("twin", WF.at[:, :, c], 19, cm.twin())
    h["r1"].wait_recv()
    h["l0"].wait_recv()
    h["twin"].wait_recv()
    for k in range(4):
        o_full[k] = WF[:, :, :, k].reshape(1024, 256).astype(jnp.bfloat16)

    def add(k):
        low_gated = GF[k].astype(jnp.bfloat16)
        resid[...] += lax.dot_general(
            low_gated, o_full[k], (((1,), (1,)), ((), ())), preferred_element_type=jnp.float32
        )

    add(L)
    add(R)
    h["r0f"].wait_recv()
    h["l1f"].wait_recv()
    add(O)
    for k in range(4):
        o_own[:, 256 * k : 256 * (k + 1)] = GF[k, mine, :].astype(jnp.bfloat16)
    o_resid[...] = resid[mine, :]

    def body(i, carry):
        rows = pl.ds(pl.multiple_of(i * 32, 32), 32)
        values = resid[rows, :]
        scale = lax.rsqrt(jnp.mean(values * values, axis=-1, keepdims=True) + EPS)
        o_normed[rows, :] = (values * scale * gain[...]).astype(jnp.bfloat16)
        return carry

    lax.fori_loop(0, T // 32, body, 0)
    cm.run()


def middle_kernel(*refs):
    (dn, own_resid, gain, own_cot, normed, d_gate, d_up, act, cot, down, ow) = refs[:11]
    (o_dres, o_dlow, o_gain, o_dgated, o_res, o_gate, o_up, o_down) = refs[11:19]
    (rp, full, turned, relay, yt, yf, G, RC) = refs[19:27]
    bufs, (ys, yr), sems, (xs, xr) = refs[27:35], refs[35:37], refs[37:43], refs[43:]
    H = own_resid.shape[0] // 2
    cm = Comm()
    greet_all(cm)

    def finish_dres(half, total):
        mine = pl.ds(half * H, H)
        rows, gains = norm_back_rows(
            total, own_resid[mine, :], gain[...], own_cot[mine, :].astype(jnp.float32)
        )
        o_gain[...] = gains if half == 0 else o_gain[...] + gains
        return rows

    def finish_result(half, total):
        return total + own_resid[pl.ds(half * H, H), :]

    def rounded():
        o_res[...] = full[...].astype(jnp.bfloat16)

    @cm.when(0.02)
    def _():
        rp[...] = lax.dot_general(
            act[...], down[...], (((1,), (1,)), ((), ())), preferred_element_type=jnp.float32
        )

    head_sum(cm, dn, o_dres, yt.at[0], yf.at[0], ys.at[0], yr.at[0], finish_dres, (0, 7, 20, 0), lambda: None, False)
    head_sum(cm, rp, full, yt.at[1], yf.at[1], ys.at[1], yr.at[1], finish_result, (7.05, 19, 33, 44), rounded)

    C = 2 * H
    R, L = ahead(cm.me, 1), ahead(cm.me, 3)
    c = {}

    def rows(k, half=None):
        if half is None:
            return pl.ds(pl.multiple_of(k * C, C), C)
        return pl.ds(pl.multiple_of(k * C + half * H, H), H)

    def go(name, src, dst, i, n):
        c[name] = cm.send(src, dst, xs.at[i], xr.at[i], cm.at_y(n))

    @cm.when(20.1)
    def _():
        low = o_dres[...].astype(jnp.bfloat16)
        o_dlow[...] = low
        for turn in (2, 1, 3):
            turned[turn - 1] = jnp.dot(low, ow[ahead(cm.me, turn)], preferred_element_type=jnp.float32)
            if turn == 2:
                go("e0", turned.at[1, pl.ds(0, H)], relay.at[0], 0, 1)
                go("e1", turned.at[1, pl.ds(H, H)], relay.at[1], 1, 3)
            else:
                go(("d", turn), turned.at[turn - 1], o_dgated.at[rows(cm.me)], 1 + turn, turn)
        o_dgated[rows(cm.me), :] = jnp.dot(low, ow[cm.me], preferred_element_type=jnp.float32)

    @cm.when(25)
    def _():
        c["e0"].wait_recv()
        go("f0", relay.at[0], o_dgated.at[rows(L, 0)], 5, 1)
        c["e1"].wait_recv()
        go("f1", relay.at[1], o_dgated.at[rows(R, 1)], 6, 3)

    @cm.when(901)
    def _():
        for name in (("d", 1), ("d", 3), "f0", "f1"):
            c[name].wait_recv()

    w = act.shape[1]
    wa = 1792

    def done_a():
        rows = G[cm.x, cm.z, cm.core, :, pl.ds(0, wa)]
        o_gate[...] = rows[:, :w]
        o_up[:, pl.ds(0, wa - w)] = rows[:, w:]

    def done_b():
        rows = G[cm.x, cm.z, cm.core, :, pl.ds(wa, 3 * w - wa)]
        o_up[:, pl.ds(wa - w, 2 * w - wa)] = rows[:, : 2 * w - wa]
        o_down[...] = rows[:, 2 * w - wa :]

    times = {
        "block": (4, 5.5, 7.5, 9),
        "settle": (7.1, 8.5, 10, 12),
        "A": (7.2, 8.6, 10.1, 18.5, 42),
        "B": (12.1, 12.2, 12.3, 24, 45),
        "A2": (42.1, 42.2, 42.3, 46, 52),
        "B2": (45.1, 45.2, 45.3, 49, 55),
    }
    products = [(normed, [d_gate], 0), (normed, [d_up], w), (cot, [act], 2 * w)]
    grad_scatter(cm, products, G, RC, wa, bufs, sems, times, done_a, done_b)
    cm.run()


def end_kernel(*refs):
    (dm, toks, gain, d_res, normed) = refs[:5]
    d_proj = refs[5:8]
    (d_low, gated, small) = refs[8:11]
    (o_tok, o_in, o_out, o_mix, o_ffn, o_conv) = refs[11:17]
    (yt, yf, G, RC) = refs[17:21]
    bufs = refs[21:29]
    sm, sr = refs[29:31]
    ys, yr = refs[31:33]
    sems = refs[33:39]
    ss, sr_sem = refs[39:41]
    mine, theirs, hs, hr = refs[41:]
    H = toks.shape[0] // 2
    cm = Comm()
    greet_all(cm)

    def finish_tokens(half, total):
        mine = pl.ds(half * H, H)
        return norm_back_rows(total, toks[mine, :].astype(jnp.float32), gain[...], d_res[mine, :])[0]

    head_sum(cm, dm, o_tok, yt, yf, ys, yr, finish_tokens, (0, 6.5, 17, 26), lambda: None)

    wa = 768
    heads = []

    def done_a():
        rows = G[cm.x, cm.z, cm.core, :, pl.ds(0, wa)]
        for k in range(3):
            o_in[k] = rows[:, 256 * k : 256 * (k + 1)]

    def done_b():
        rows = G[cm.x, cm.z, cm.core, :, pl.ds(wa, 1024)]
        for k in range(4):
            mine[k] = rows[:, 256 * k : 256 * (k + 1)]
        for n in (1, 2, 3):
            heads.append(
                cm.send(mine.at[ahead(cm.me, n)], theirs.at[n - 1], hs.at[n - 1], hr.at[n - 1], cm.at_y(n))
            )

    @cm.when(950)
    def _():
        for copy in heads:
            copy.wait_recv()
        o_out[...] = (mine[cm.me] + theirs[0]) + (theirs[1] + theirs[2])

    times = {
        "block": (0.1, 1, 2, 3),
        "settle": (2, 3, 4, 5),
        "A": (2.1, 3.1, 4.1, 7.5, 19),
        "B": (5.1, 5.2, 5.3, 12, 23),
        "A2": (19.1, 19.2, 19.3, 21.5, 25.5),
        "B2": (23.1, 23.2, 23.3, 25.7, 28),
    }
    products = [(normed, d_proj, 0), (d_low, [gated], 768)]
    grad_scatter(cm, products, G, RC, wa, bufs, sems, times, done_a, done_b)

    def small_done(gains, rest):
        o_mix[...] = gains[0:8]
        o_ffn[...] = gains[8:16]
        for k in range(3):
            for h in range(2):
                o_conv[k : k + 1, pl.ds(128 * h, 128)] = rest[2 * k + h : 2 * k + h + 1]

    small_sums(cm, small, sm, sr, ss, sr_sem, (0.05, 5, 9, 15, 22), small_done)
    cm.run()


VMEM_SPEC = pl.BlockSpec(memory_space=pltpu.VMEM)


def call(kernel, name, cid, args, outs, scratch, limit):
    return pl.pallas_call(
        kernel,
        out_shape=outs,
        in_specs=[VMEM_SPEC] * len(args),
        out_specs=(VMEM_SPEC,) * len(outs),
        scratch_shapes=scratch,
        compiler_params=pltpu.CompilerParams(
            collective_id=cid, has_side_effects=True, vmem_limit_bytes=limit << 20
        ),
        cost_estimate=pl.CostEstimate(flops=1, bytes_accessed=1, transcendentals=0),
        name=name,
    )(*args)


def scatter_scratch(W, wa):
    f32 = jnp.float32
    wb = W - wa
    return [
        pltpu.VMEM((4, 4, 2, 32, W), f32),
        pltpu.VMEM((4, 4, 32, W), f32),
        pltpu.VMEM((2, 2, 32, wa), f32),
        pltpu.VMEM((2, 2, 32, wb), f32),
        pltpu.VMEM((2, 2, 2, 32, wa), f32),
        pltpu.VMEM((2, 2, 2, 32, wb), f32),
        pltpu.VMEM((2, 1, 16, wa), f32),
        pltpu.VMEM((2, 1, 16, wb), f32),
        pltpu.VMEM((2, 2, 1, 16, wa), f32),
        pltpu.VMEM((2, 2, 1, 16, wb), f32),
    ]


SCATTER_SEMS = [pltpu.SemaphoreType.DMA((n,)) for n in (4, 4, 12, 12, 12, 12)]


def front(gated, ow, tokens, cot, down, gain):
    T, D = tokens.shape
    f32, bf16, shape, dma = jnp.float32, jnp.bfloat16, jax.ShapeDtypeStruct, pltpu.SemaphoreType.DMA
    outs = (
        shape((T, D), bf16),
        shape((4, *ow.shape), bf16),
        shape((T // 4, D), bf16),
        shape((T, down.shape[1]), f32),
        shape((T // 4, D), f32),
        shape((T // 4, D), bf16),
        shape((T // 4, D), bf16),
    )
    scratch = [
        pltpu.VMEM((T, D), f32),
        pltpu.VMEM((4, *gated.shape), f32),
        pltpu.VMEM((4, 4, 2, 4, 32, ow.shape[1]), f32),
        dma((6,)),
        dma((6,)),
        dma((20,)),
        dma((20,)),
    ]
    return call(front_kernel, "front", 3, (gated, ow, tokens, cot, down, gain), outs, scratch, 24)


def middle(dn, own_resid, gain, own_cot, normed, d_gate, d_up, act, cot, down, ow):
    T, D = dn.shape
    H = T // 8
    f32, shape, dma = jnp.float32, jax.ShapeDtypeStruct, pltpu.SemaphoreType.DMA
    w = act.shape[1]
    outs = (
        shape((T // 4, D), f32),
        shape((T // 4, D), jnp.bfloat16),
        shape((1, D), f32),
        shape((T, 256), f32),
        shape((T, D), jnp.bfloat16),
    ) + (shape((32, w), f32),) * 3
    scratch = [
        pltpu.VMEM((T, D), f32),
        pltpu.VMEM((T, D), f32),
        pltpu.VMEM((3, 2 * H, 256), f32),
        pltpu.VMEM((2, H, 256), f32),
        pltpu.VMEM((2, 2, H, D), f32),
        pltpu.VMEM((2, 2, 2, H, D), f32),
        *scatter_scratch(3 * w, 1792),
        dma((2, 12)),
        dma((2, 12)),
        *SCATTER_SEMS,
        dma((7,)),
        dma((7,)),
    ]
    args = (dn, own_resid, gain, own_cot, normed, d_gate, d_up, act, cot, down, ow)
    return call(middle_kernel, "middle", 5, args, outs, scratch, 42)


def end(dm, toks, gain, d_res, normed, d_proj, d_low, gated, small):
    T, D = dm.shape
    H = T // 8
    f32, shape, dma = jnp.float32, jax.ShapeDtypeStruct, pltpu.SemaphoreType.DMA
    outs = (
        shape((T, D), f32),
        shape((3, 32, 256), f32),
        shape((32, 256), f32),
        shape((8, 128), f32),
        shape((8, 128), f32),
        shape((3, 256), f32),
    )
    scratch = [
        pltpu.VMEM((2, H, D), f32),
        pltpu.VMEM((2, 2, H, D), f32),
        *scatter_scratch(1792, 768),
        pltpu.VMEM((3, 24, 128), f32),
        pltpu.VMEM((4, 4, 24, 128), f32),
        dma((12,)),
        dma((12,)),
        *SCATTER_SEMS,
        dma((10,)),
        dma((10,)),
        pltpu.VMEM((4, 32, 256), f32),
        pltpu.VMEM((3, 32, 256), f32),
        dma((3,)),
        dma((3,)),
    ]
    args = (dm, toks, gain, d_res, normed, *d_proj, d_low, gated, small)
    return call(end_kernel, "end", 7, args, outs, scratch, 24)


def place(*arrays):
    n = len(arrays)

    def kernel(*refs):
        copies = [pltpu.make_async_copy(refs[i], refs[n + i], refs[2 * n].at[i]) for i in range(n)]
        for copy in copies:
            copy.start()
        for copy in copies:
            copy.wait()

    anywhere = pl.BlockSpec(memory_space=pl.ANY)
    return pl.pallas_call(
        kernel,
        out_shape=tuple(jax.ShapeDtypeStruct(a.shape, a.dtype) for a in arrays),
        in_specs=[VMEM_SPEC] * n,
        out_specs=(anywhere,) * n,
        scratch_shapes=[pltpu.SemaphoreType.DMA((n,))],
        compiler_params=pltpu.CompilerParams(vmem_limit_bytes=2 << 20),
        name="place",
    )(*arrays)


def from_behind(block, axis, distance):
    devices = range(lax.axis_size(axis))
    route = [(i - distance, i) for i in devices if i - distance in devices]
    return lax.ppermute(block, axis, route)


def rms_scale(values):
    return lax.rsqrt(jnp.mean(values * values, axis=-1, keepdims=True) + EPS)


def right_product(left, right):
    return lax.dot_general(
        left, right, (((1,), (1,)), ((), ())), preferred_element_type=jnp.float32
    )


def on_device(
    tokens,
    segment_ids,
    mix_gain,
    in_weight,
    conv_weight,
    out_weight,
    ffn_gain,
    gate_weight,
    up_weight,
    down_weight,
    cotangent,
):
    tok_rows = tokens.shape[0]
    first_row = lax.axis_index("seq") * tok_rows
    padded_ids = jnp.concatenate(
        [jnp.full((2,), -1, jnp.int32), segment_ids, jnp.full((2,), -2, jnp.int32)]
    )
    id_window = lax.dynamic_slice_in_dim(padded_ids, first_row, tok_rows + 4)
    near_ext = (id_window[2 : tok_rows + 4] == id_window[1 : tok_rows + 3]).astype(jnp.float32)
    far_ext = (id_window[2 : tok_rows + 4] == id_window[0 : tok_rows + 2]).astype(jnp.float32)
    near_own = near_ext[:tok_rows, None]
    far_own = far_ext[:tok_rows, None]
    inputs = tokens.astype(jnp.float32)
    mix_scale = rms_scale(inputs)
    mix_normed = (inputs * mix_scale * mix_gain).astype(jnp.bfloat16)
    projected = jnp.einsum("td,dkc->tkc", mix_normed, in_weight, preferred_element_type=jnp.float32)
    chan_b = projected[:, 0]
    chan_c = projected[:, 1]
    chan_x = projected[:, 2]
    mixed = chan_b * chan_x
    edge_rows = from_behind(mixed[tok_rows - 2 :], "seq", 1)
    extended = jnp.concatenate([edge_rows, mixed])
    kernel = conv_weight.astype(jnp.float32)
    prev_one = extended[1 : tok_rows + 1]
    prev_two = extended[0:tok_rows]
    conv_out = kernel[0] * mixed + kernel[1] * near_own * prev_one + kernel[2] * far_own * prev_two
    gated = (chan_c * conv_out).astype(jnp.bfloat16)
    ffn_normed, out_full, gated_rows, d_act, own_resid, own_cot, own_tok = front(
        gated, out_weight, tokens, cotangent, down_weight, ffn_gain[None]
    )
    gate = jnp.dot(ffn_normed, gate_weight, preferred_element_type=jnp.float32)
    upper = jnp.dot(ffn_normed, up_weight, preferred_element_type=jnp.float32)
    sigma = jax.nn.sigmoid(gate)
    act = (gate * sigma * upper).astype(jnp.bfloat16)
    d_gate = (d_act * upper * sigma * (1.0 + gate * (1.0 - sigma))).astype(jnp.bfloat16)
    d_up = (d_act * gate * sigma).astype(jnp.bfloat16)
    d_normed_part = right_product(d_gate, gate_weight) + right_product(d_up, up_weight)
    d_resid, d_resid_low, grad_ffn_gain, d_gated, result, gate_share, up_share, down_share = middle(
        d_normed_part,
        own_resid,
        ffn_gain[None],
        own_cot,
        ffn_normed,
        d_gate,
        d_up,
        act,
        cotangent,
        down_weight,
        out_full,
    )
    d_chan_c = d_gated * conv_out
    d_conv = d_gated * chan_c
    tail_rows = from_behind(d_conv[:2], "seq", -1)
    later = jnp.concatenate([d_conv, tail_rows])
    next_one = later[1 : tok_rows + 1]
    next_two = later[2 : tok_rows + 2]
    near_next = near_ext[1 : tok_rows + 1, None]
    far_next = far_ext[2 : tok_rows + 2, None]
    d_mixed = kernel[0] * d_conv + kernel[1] * near_next * next_one + kernel[2] * far_next * next_two
    grad_conv = jnp.stack(
        [
            jnp.sum(d_conv * mixed, axis=0),
            jnp.sum(d_conv * near_own * prev_one, axis=0),
            jnp.sum(d_conv * far_own * prev_two, axis=0),
        ]
    )
    d_projected = [p.astype(jnp.bfloat16) for p in (d_mixed * chan_x, d_chan_c, d_mixed * chan_b)]
    d_mix_part = jnp.einsum(
        "tkc,dkc->td",
        jnp.stack(d_projected, axis=1),
        in_weight,
        preferred_element_type=jnp.float32,
    )
    grad_mix_gain = jnp.sum(d_mix_part * inputs * mix_scale, axis=0)
    small = jnp.concatenate(
        [
            grad_mix_gain.reshape(8, 128),
            grad_ffn_gain.reshape(8, 128),
            grad_conv.reshape(6, 128),
            jnp.zeros((2, 128), jnp.float32),
        ]
    )
    grad_tokens, in_share, out_share, mix_total, ffn_total, conv_total = end(
        d_mix_part,
        own_tok,
        mix_gain[None],
        d_resid,
        mix_normed,
        d_projected,
        d_resid_low,
        gated_rows,
        small,
    )
    (
        result,
        grad_tokens,
        mix_total,
        in_share,
        conv_total,
        out_share,
        ffn_total,
        gate_share,
        up_share,
        down_share,
    ) = place(
        result,
        grad_tokens,
        mix_total,
        in_share,
        conv_total,
        out_share,
        ffn_total,
        gate_share,
        up_share,
        down_share,
    )
    return (
        result,
        grad_tokens,
        mix_total.reshape(-1),
        in_share.transpose(1, 0, 2),
        conv_total,
        out_share,
        ffn_total.reshape(-1),
        gate_share,
        up_share,
        down_share,
    )


def solution(mesh):
    placed = (
        P("seq", None),
        P(),
        P(),
        P(None, None, "head"),
        P(None, "head"),
        P(None, "head"),
        P(),
        P(None, "head"),
        P(None, "head"),
        P(None, "head"),
        P("seq", None),
    )
    return jax.shard_map(
        on_device,
        mesh=mesh,
        in_specs=placed,
        out_specs=(
            P("seq", None),
            P("seq", None),
            P(),
            P("seq", None, "head"),
            P(None, "head"),
            P("seq", "head"),
            P(),
            P("seq", "head"),
            P("seq", "head"),
            P("seq", "head"),
        ),
        check_vma=False,
    )
```

```python
import jax
import jax.numpy as jnp
from jax import lax
from jax.experimental import pallas as pl
from jax.experimental.pallas import tpu as pltpu
from jax.sharding import PartitionSpec as P

EPS = 1e-05
MESH = pl.DeviceIdType.MESH


def norm_back_rows(grad_normed, values, gain, extra):
    scale = lax.rsqrt(jnp.mean(values * values, axis=-1, keepdims=True) + EPS)
    weighted = grad_normed * gain
    inner = jnp.mean(weighted * values, axis=-1, keepdims=True)
    grad_values = extra + (scale * weighted - values * (scale * scale * scale) * inner)
    return grad_values, jnp.sum(grad_normed * values * scale, axis=0, keepdims=True)


class Comm:
    def __init__(self):
        seq = lax.axis_index("seq")
        self.me = lax.axis_index("head")
        self.core = lax.rem(seq, 2)
        self.z = lax.rem(lax.div(seq, 2), 4)
        self.x = lax.div(seq, 8)
        self.every = []
        self.steps = []

    def at_x(self, n):
        return {"seq": (ahead(self.x, n) * 4 + self.z) * 2 + self.core, "head": self.me}

    def at_z(self, n):
        return {"seq": (self.x * 4 + ahead(self.z, n)) * 2 + self.core, "head": self.me}

    def at_y(self, n):
        return {"seq": (self.x * 4 + self.z) * 2 + self.core, "head": ahead(self.me, n)}

    def twin(self, n=1):
        return {"seq": (self.x * 4 + self.z) * 2 + (1 - self.core), "head": self.me}

    def along(self, n):
        return {"seq": lax.rem((self.x * 4 + self.z) * 2 + self.core + n, 32), "head": self.me}

    def greet(self, devices):
        barrier = pltpu.get_barrier_semaphore()
        for device in devices:
            pl.semaphore_signal(barrier, inc=1, device_id=device, device_id_type=MESH)
        pl.semaphore_wait(barrier, len(devices))

    def send(self, src, dst, s_sem, r_sem, dev):
        copy = pltpu.make_async_remote_copy(
            src_ref=src, dst_ref=dst, send_sem=s_sem, recv_sem=r_sem, device_id=dev, device_id_type=MESH
        )
        copy.start()
        self.every.append(copy)
        return copy

    def when(self, time):
        def add(fn):
            self.steps.append((time, len(self.steps), fn))
            return fn

        return add

    def run(self):
        for _, _, fn in sorted(self.steps, key=lambda s: s[:2]):
            fn()
        for copy in self.every:
            copy.wait_send()


def ahead(k, n):
    return lax.rem(k + n, 4)


def add_up(dst, *srcs):
    n, r = dst.shape[:2]
    q = r // 8

    def body(i, carry):
        b, at = lax.div(i, q), pl.ds(pl.multiple_of(lax.rem(i, q) * 8, 8), 8)
        total = dst[b, at, :]
        for src in srcs:
            total = total + src[b, at, :]
        dst[b, at, :] = total
        return carry

    lax.fori_loop(0, n * q, body, 0)


def head_sum(cm, p, o, t, f, s_sem, r_sem, finish, times, closing, share=True):
    T = p.shape[0]
    C = T // 4
    H = C // 2
    R, L, O = ahead(cm.me, 1), ahead(cm.me, 3), ahead(cm.me, 2)
    me = cm.me
    c = {}

    def rows(k, half):
        return pl.ds(pl.multiple_of(k * C + half * H, H), H)

    def go(name, src, dst, i, n):
        c[name] = cm.send(src, dst, s_sem.at[i], r_sem.at[i], cm.at_y(n))

    @cm.when(times[0])
    def _():
        go("a0", p.at[rows(O, 0)], t.at[0], 0, 1)
        go("a1", p.at[rows(O, 1)], t.at[1], 1, 3)
        go("a2", p.at[rows(R, 1)], f.at[0, 1], 2, 1)
        go("a3", p.at[rows(L, 0)], f.at[1, 0], 3, 3)

    @cm.when(times[1])
    def _():
        c["a0"].wait_recv()
        t[0] = p[rows(R, 0), :] + t[0]
        go("a4", t.at[0], f.at[0, 0], 4, 1)
        c["a1"].wait_recv()
        t[1] = p[rows(L, 1), :] + t[1]
        go("a5", t.at[1], f.at[1, 1], 5, 3)

    @cm.when(times[2])
    def _():
        c["a3"].wait_recv()
        c["a4"].wait_recv()
        first = finish(0, p[rows(me, 0), :] + f[0, 0] + f[1, 0])
        if not share:
            c["a2"].wait_recv()
            c["a5"].wait_recv()
            o[0:H, :] = first
            o[H:C, :] = finish(1, p[rows(me, 1), :] + f[0, 1] + f[1, 1])
            return
        o[rows(me, 0), :] = first
        go("b0", o.at[rows(me, 0)], o.at[rows(me, 0)], 6, 1)
        go("c0", o.at[rows(me, 0)], o.at[rows(me, 0)], 8, 3)
        c["a2"].wait_recv()
        c["a5"].wait_recv()
        o[rows(me, 1), :] = finish(1, p[rows(me, 1), :] + f[0, 1] + f[1, 1])
        go("c1", o.at[rows(me, 1)], o.at[rows(me, 1)], 9, 3)
        go("b1", o.at[rows(me, 1)], o.at[rows(me, 1)], 7, 1)

    if not share:
        return

    @cm.when(times[3])
    def _():
        c["b0"].wait_recv()
        go("d0", o.at[rows(L, 0)], o.at[rows(L, 0)], 10, 1)
        c["c1"].wait_recv()
        go("d1", o.at[rows(R, 1)], o.at[rows(R, 1)], 11, 3)

    @cm.when(900)
    def _():
        for name in ("b1", "c0", "d0", "d1"):
            c[name].wait_recv()
        closing()


def scatter_ring(cm, chunk, t, f, s_sem, r_sem, base, to, times, done):
    c = {}

    def go(name, src, dst, i, n):
        c[name] = cm.send(src, dst, s_sem.at[base + i], r_sem.at[base + i], to(n))

    @cm.when(times[0])
    def _():
        go("a0", chunk(2, 0), t.at[0], 0, 1)
        go("a1", chunk(2, 1), t.at[1], 1, 3)

    @cm.when(times[1])
    def _():
        go("a2", chunk(1, 1), f.at[0, 1], 2, 1)

    @cm.when(times[2])
    def _():
        go("a3", chunk(3, 0), f.at[1, 0], 3, 3)

    @cm.when(times[3])
    def _():
        c["a0"].wait_recv()
        add_up(t.at[0], chunk(1, 0))
        go("a4", t.at[0], f.at[0, 0], 4, 1)
        c["a1"].wait_recv()
        add_up(t.at[1], chunk(3, 1))
        go("a5", t.at[1], f.at[1, 1], 5, 3)

    @cm.when(times[4])
    def _():
        c["a3"].wait_recv()
        c["a4"].wait_recv()
        add_up(chunk(0, 0), f.at[0, 0], f.at[1, 0])
        c["a2"].wait_recv()
        c["a5"].wait_recv()
        add_up(chunk(0, 1), f.at[0, 1], f.at[1, 1])
        done()


def grad_scatter(cm, products, G, RC, wa, bufs, sems, times, done_a, done_b):
    tA, tB, fA, fB, t2A, t2B, f2A, f2B = bufs
    cs, cr, as_, ar, bs, br = sems
    W = G.shape[-1]
    quarter = products[0][0].shape[1] // 4
    got = {}

    def block(turn):
        k = ahead(cm.x, turn)
        for left, rights, at in products:
            right = jnp.concatenate([r[...] for r in rights], axis=1)
            w = right.shape[1]
            lhs = left[:, pl.ds(pl.multiple_of(k * quarter, quarter), quarter)]
            value = lax.dot_general(
                lhs, right, (((0,), (0,)), ((), ())), preferred_element_type=jnp.float32
            )
            G[k, :, :, :, pl.ds(at, w)] = value.reshape(4, 2, 32, w)
        got[turn] = cm.send(G.at[k, :, 1 - cm.core], RC.at[k], cs.at[turn], cr.at[turn], cm.twin())

    def settle(turn):
        k = ahead(cm.x, turn)
        got[turn].wait_recv()
        add_up(G.at[k, :, cm.core], RC.at[k])

    for i, turn in enumerate((2, 1, 3, 0)):
        cm.when(times["block"][i])(lambda turn=turn: block(turn))
        cm.when(times["settle"][i])(lambda turn=turn: settle(turn))

    cols_a, cols_b = pl.ds(0, wa), pl.ds(wa, W - wa)
    core = cm.core

    def a1(turn, half):
        return G.at[ahead(cm.x, turn), pl.ds(half * 2, 2), core, :, cols_a]

    def b1(turn, half):
        return G.at[pl.ds(half * 2, 2), ahead(cm.z, turn), core, :, cols_b]

    def a2(turn, half):
        return G.at[cm.x, pl.ds(ahead(cm.z, turn), 1), core, pl.ds(half * 16, 16), cols_a]

    def b2(turn, half):
        return G.at[pl.ds(ahead(cm.x, turn), 1), cm.z, core, pl.ds(half * 16, 16), cols_b]

    nothing = lambda: None
    scatter_ring(cm, a1, tA, fA, as_, ar, 0, cm.at_x, times["A"], nothing)
    scatter_ring(cm, b1, tB, fB, bs, br, 0, cm.at_z, times["B"], nothing)
    scatter_ring(cm, a2, t2A, f2A, as_, ar, 6, cm.at_z, times["A2"], done_a)
    scatter_ring(cm, b2, t2B, f2B, bs, br, 6, cm.at_x, times["B2"], done_b)


def small_sums(cm, small, sm, sr, s_sem, r_sem, times, done):
    axes = [(cm.at_z, cm.z), (cm.at_x, cm.x), (cm.at_y, cm.me)]
    first = {}

    @cm.when(times[0])
    def _():
        first["c"] = cm.send(small, sr.at[3, 0], s_sem.at[9], r_sem.at[9], cm.twin())

    @cm.when(times[1])
    def _():
        first["c"].wait_recv()
        sm[0] = small[...] + sr[3, 0]

    for a, (to, here) in enumerate(axes):
        copies = []

        def begin(a=a, to=to, here=here, copies=copies):
            sr[a, here] = sm[a]
            for n in (1, 2, 3):
                i = a * 3 + n - 1
                copies.append(cm.send(sm.at[a], sr.at[a, here], s_sem.at[i], r_sem.at[i], to(n)))

        def end(a=a, copies=copies):
            for copy in copies:
                copy.wait_recv()
            total = (sr[a, 0] + sr[a, 1]) + (sr[a, 2] + sr[a, 3])
            if a < 2:
                sm[a + 1] = total
            else:
                done(total[0:16], sm[2][16:24])

        cm.when(times[1] + 0.01)(begin) if a == 0 else cm.when(times[1 + a] + 0.01)(begin)
        cm.when(times[2 + a])(end)


def greet_all(cm, more):
    cm.greet([axis(n) for n in (1, 2, 3) for axis in (cm.at_x, cm.at_z, cm.at_y)] + [cm.twin()] + more)


def front_kernel(
    gated, ow, tokens, cot, down, gain, o_normed, o_full, o_own, o_dact, o_resid, o_cot, o_tok, resid, GF, WF, ys, yr, ws, wr
):
    cm = Comm()
    x, z, c, me = cm.x, cm.z, cm.core, cm.me
    R, L, O = ahead(me, 1), ahead(me, 3), ahead(me, 2)
    cm.greet([cm.at_x(1), cm.at_x(3), cm.at_z(1), cm.at_z(3), cm.at_y(1), cm.at_y(2), cm.at_y(3), cm.twin()])
    T = gated.shape[0]
    N = T // 2
    piece = ((x * 4 + z) * 2 + c) * 32
    h = {}

    def weight(name, ref, i, dev):
        h[name] = cm.send(ref, ref, ws.at[i], wr.at[i], dev)

    def gate(name, ref, i, n):
        h[name] = cm.send(ref, ref, ys.at[i], yr.at[i], cm.at_y(n))

    low, high = pl.ds(0, 2), pl.ds(2, 2)
    WF[x, z, c, me] = ow[pl.ds(pl.multiple_of(piece, 32), 32), :].astype(jnp.float32)
    for n in (1, 2, 3):
        weight(("y", n), WF.at[x, z, c, me], n - 1, cm.at_y(n))
    GF[me] = gated[...].astype(jnp.float32)
    first, second = pl.ds(0, N), pl.ds(N, N)
    gate("r0", GF.at[me, first], 0, 1)
    gate("l1", GF.at[me, second], 1, 3)
    gate("r1", GF.at[me, second], 2, 1)
    gate("l0", GF.at[me, first], 3, 3)
    for n in (1, 2, 3):
        h["y", n].wait_recv()
    weight("ax1", WF.at[x, z, c, low], 3, cm.at_x(1))
    weight("ax3", WF.at[x, z, c, low], 4, cm.at_x(3))
    weight("bz1", WF.at[x, z, c, high], 5, cm.at_z(1))
    weight("bz3", WF.at[x, z, c, high], 6, cm.at_z(3))
    resid[...] = tokens[...].astype(jnp.float32) + lax.dot_general(
        gated[...], ow[...], (((1,), (1,)), ((), ())), preferred_element_type=jnp.float32
    )
    mine = pl.ds(pl.multiple_of(me * (T // 4), T // 4), T // 4)
    o_cot[...] = cot[mine, :]
    o_tok[...] = tokens[mine, :]
    xl, xr, zl, zr = ahead(x, 3), ahead(x, 1), ahead(z, 3), ahead(z, 1)
    h["ax1"].wait_recv()
    weight("ax1f", WF.at[xl, z, c, 0], 7, cm.at_x(1))
    h["ax3"].wait_recv()
    weight("ax3f", WF.at[xr, z, c, 1], 8, cm.at_x(3))
    h["bz1"].wait_recv()
    weight("bz1f", WF.at[x, zl, c, 2], 9, cm.at_z(1))
    h["bz3"].wait_recv()
    weight("bz3f", WF.at[x, zr, c, 3], 10, cm.at_z(3))
    h["ax1f"].wait_recv()
    h["ax3f"].wait_recv()
    weight("az1", WF.at[:, z, c, low], 11, cm.at_z(1))
    weight("az3", WF.at[:, z, c, low], 12, cm.at_z(3))
    h["bz1f"].wait_recv()
    h["bz3f"].wait_recv()
    weight("bx1", WF.at[x, :, c, high], 13, cm.at_x(1))
    weight("bx3", WF.at[x, :, c, high], 14, cm.at_x(3))
    o_dact[...] = jnp.dot(cot[...], down[...], preferred_element_type=jnp.float32)
    h["r0"].wait_recv()
    gate("r0f", GF.at[L, first], 4, 1)
    h["l1"].wait_recv()
    gate("l1f", GF.at[R, second], 5, 3)
    h["az1"].wait_recv()
    weight("az1f", WF.at[:, zl, c, 0], 15, cm.at_z(1))
    h["az3"].wait_recv()
    weight("az3f", WF.at[:, zr, c, 1], 16, cm.at_z(3))
    h["bx1"].wait_recv()
    weight("bx1f", WF.at[xl, :, c, 2], 17, cm.at_x(1))
    h["bx3"].wait_recv()
    weight("bx3f", WF.at[xr, :, c, 3], 18, cm.at_x(3))
    for name in ("az1f", "az3f", "bx1f", "bx3f"):
        h[name].wait_recv()
    weight("twin", WF.at[:, :, c], 19, cm.twin())
    h["r1"].wait_recv()
    h["l0"].wait_recv()
    h["twin"].wait_recv()
    for k in range(4):
        o_full[k] = WF[:, :, :, k].reshape(1024, 256).astype(jnp.bfloat16)

    def add(k):
        low_gated = GF[k].astype(jnp.bfloat16)
        resid[...] += lax.dot_general(
            low_gated, o_full[k], (((1,), (1,)), ((), ())), preferred_element_type=jnp.float32
        )

    add(L)
    add(R)
    h["r0f"].wait_recv()
    h["l1f"].wait_recv()
    add(O)
    for k in range(4):
        o_own[:, 256 * k : 256 * (k + 1)] = GF[k, mine, :].astype(jnp.bfloat16)
    o_resid[...] = resid[mine, :]

    def body(i, carry):
        rows = pl.ds(pl.multiple_of(i * 32, 32), 32)
        values = resid[rows, :]
        scale = lax.rsqrt(jnp.mean(values * values, axis=-1, keepdims=True) + EPS)
        o_normed[rows, :] = (values * scale * gain[...]).astype(jnp.bfloat16)
        return carry

    lax.fori_loop(0, T // 32, body, 0)
    cm.run()


def middle_kernel(*refs):
    (dn, own_resid, gain, own_cot, normed, d_gate, d_up, act, down, ow) = refs[:10]
    (proj, mixed, conv_out, marks, taps, in_w) = refs[10:16]
    (o_dres, o_dlow, o_gain, o_res, o_gate, o_up, o_dproj, o_dm, o_taps) = refs[16:25]
    (rp, full, turned, relay, dgated, DC, yt, yf, G, RC) = refs[25:35]
    bufs, (ys, yr), sems, (xs, xr), (hs, hr) = refs[35:43], refs[43:45], refs[45:51], refs[51:53], refs[53:]
    H = own_resid.shape[0] // 2
    T = 8 * H
    cm = Comm()
    greet_all(cm, [cm.along(1), cm.along(31)])

    def finish_dres(half, total):
        mine = pl.ds(half * H, H)
        rows, gains = norm_back_rows(
            total, own_resid[mine, :], gain[...], own_cot[mine, :].astype(jnp.float32)
        )
        o_gain[...] = gains if half == 0 else o_gain[...] + gains
        return rows

    def finish_result(half, total):
        return total + own_resid[pl.ds(half * H, H), :]

    def rounded():
        o_res[...] = full[...].astype(jnp.bfloat16)

    @cm.when(0.02)
    def _():
        rp[...] = lax.dot_general(
            act[...], down[...], (((1,), (1,)), ((), ())), preferred_element_type=jnp.float32
        )

    head_sum(cm, dn, o_dres, yt.at[0], yf.at[0], ys.at[0], yr.at[0], finish_dres, (0, 7, 18, 0), lambda: None, False)
    head_sum(cm, rp, full, yt.at[1], yf.at[1], ys.at[1], yr.at[1], finish_result, (7.05, 25, 44, 56), rounded)

    C = 2 * H
    R, L = ahead(cm.me, 1), ahead(cm.me, 3)
    c = {}

    def rows(k, half=None):
        if half is None:
            return pl.ds(pl.multiple_of(k * C, C), C)
        return pl.ds(pl.multiple_of(k * C + half * H, H), H)

    def go(name, src, dst, i, n):
        c[name] = cm.send(src, dst, xs.at[i], xr.at[i], cm.at_y(n))

    @cm.when(18.1)
    def _():
        low = o_dres[...].astype(jnp.bfloat16)
        o_dlow[...] = low
        for turn in (2, 1, 3):
            turned[turn - 1] = jnp.dot(low, ow[ahead(cm.me, turn)], preferred_element_type=jnp.float32)
            if turn == 2:
                go("e0", turned.at[1, pl.ds(0, H)], relay.at[0], 0, 1)
                go("e1", turned.at[1, pl.ds(H, H)], relay.at[1], 1, 3)
            else:
                go(("d", turn), turned.at[turn - 1], dgated.at[rows(cm.me)], 1 + turn, turn)
        dgated[rows(cm.me), :] = jnp.dot(low, ow[cm.me], preferred_element_type=jnp.float32)

    @cm.when(32)
    def _():
        c["e0"].wait_recv()
        go("f0", relay.at[0], dgated.at[rows(L, 0)], 5, 1)
        c["e1"].wait_recv()
        go("f1", relay.at[1], dgated.at[rows(R, 1)], 6, 3)

    N = 64

    @cm.when(38)
    def _():
        for name in (("d", 1), ("d", 3), "f0", "f1"):
            c[name].wait_recv()
        for i in range(T // N):
            at = pl.ds(i * N, N)
            dg = dgated[at, :]
            o_dproj[1, at, :] = (dg * conv_out[at, :]).astype(jnp.bfloat16)
            DC[at, :] = dg * proj[1, at, :]
        c["halo"] = cm.send(DC.at[pl.ds(0, 8)], DC.at[pl.ds(T, 8)], hs.at[0], hr.at[0], cm.along(31))

    @cm.when(41)
    def _():
        c["halo"].wait_recv()
        w0, w1, w2 = taps[0:1, :], taps[1:2, :], taps[2:3, :]
        sums = [jnp.zeros((1, 256), jnp.float32)] * 3
        for i in range(T // N):
            at = pl.ds(i * N, N)
            near, far = marks[at, 0:1], marks[at, 1:2]
            near_next, far_next = marks[at, 2:3], marks[at, 3:4]
            dc = DC[at, :]
            d_mixed = w0 * dc + w1 * near_next * DC[pl.ds(i * N + 1, N), :] + w2 * far_next * DC[pl.ds(i * N + 2, N), :]
            o_dproj[0, at, :] = (d_mixed * proj[2, at, :]).astype(jnp.bfloat16)
            o_dproj[2, at, :] = (d_mixed * proj[0, at, :]).astype(jnp.bfloat16)
            terms = (
                dc * mixed[pl.ds(i * N + 8, N), :],
                dc * near * mixed[pl.ds(i * N + 7, N), :],
                dc * far * mixed[pl.ds(i * N + 6, N), :],
            )
            sums = [s + jnp.sum(t, axis=0, keepdims=True) for s, t in zip(sums, terms)]
        for k in range(3):
            o_taps[k : k + 1, :] = sums[k]

    @cm.when(45)
    def _():
        right = jnp.concatenate([in_w[0], in_w[1], in_w[2]], axis=1)
        for i in range(4):
            at = pl.ds(i * C, C)
            left = jnp.concatenate([o_dproj[0, at, :], o_dproj[1, at, :], o_dproj[2, at, :]], axis=1)
            o_dm[at, :] = lax.dot_general(
                left, right, (((1,), (1,)), ((), ())), preferred_element_type=jnp.float32
            )

    w = act.shape[1]

    def done_a():
        o_gate[...] = G[cm.x, cm.z, cm.core, :, pl.ds(0, w)]

    def done_b():
        o_up[...] = G[cm.x, cm.z, cm.core, :, pl.ds(w, w)]

    times = {
        "block": (4, 5.2, 7.2, 8.4),
        "settle": (6.8, 8, 9.5, 11),
        "A": (6.9, 8.1, 9.6, 15, 32),
        "B": (11.1, 11.2, 11.3, 20, 36),
        "A2": (32.1, 32.2, 32.3, 36.1, 41.1),
        "B2": (36.2, 36.3, 36.4, 41.2, 46),
    }
    products = [(normed, [d_gate], 0), (normed, [d_up], w)]
    grad_scatter(cm, products, G, RC, w, bufs, sems, times, done_a, done_b)
    cm.run()


def end_kernel(*refs):
    (dm, toks, gain, d_res, normed, d_proj, d_low, gated, act, cot, ffn_gains, taps) = refs[:12]
    (o_tok, o_in, o_out, o_down, o_mix, o_ffn, o_conv) = refs[12:19]
    (yt, yf, G, RC) = refs[19:23]
    bufs = refs[23:31]
    small, sm, sr = refs[31:34]
    ys, yr = refs[34:36]
    sems = refs[36:42]
    ss, sr_sem = refs[42:44]
    mine, theirs, hs, hr = refs[44:]
    H = toks.shape[0] // 2
    cm = Comm()
    greet_all(cm, [])

    def finish_tokens(half, total):
        at = pl.ds(half * H, H)
        rows, gains = norm_back_rows(total, toks[at, :].astype(jnp.float32), gain[...], d_res[at, :])
        for k in range(8):
            part = gains[:, 128 * k : 128 * (k + 1)]
            small[k : k + 1, :] = part if half == 0 else small[k : k + 1, :] + part
        return rows

    @cm.when(0.05)
    def _():
        small[16:24, :] = jnp.zeros((8, 128), jnp.float32)
        for k in range(8):
            small[8 + k : 9 + k, :] = ffn_gains[:, 128 * k : 128 * (k + 1)]
        for k in range(3):
            for h in range(2):
                small[16 + 2 * k + h : 17 + 2 * k + h, :] = taps[k : k + 1, 128 * h : 128 * (h + 1)]

    head_sum(cm, dm, o_tok, yt, yf, ys, yr, finish_tokens, (0, 7, 19, 26), lambda: None)

    w = act.shape[1]
    wa = w + 256
    heads = []

    def done_a():
        rows = G[cm.x, cm.z, cm.core, :, pl.ds(0, wa)]
        o_down[...] = rows[:, :w]
        o_in[0] = rows[:, w:]

    def done_b():
        rows = G[cm.x, cm.z, cm.core, :, pl.ds(wa, 1536)]
        o_in[1] = rows[:, :256]
        o_in[2] = rows[:, 256:512]
        for k in range(4):
            mine[k] = rows[:, 512 + 256 * k : 768 + 256 * k]
        for n in (1, 2, 3):
            heads.append(
                cm.send(mine.at[ahead(cm.me, n)], theirs.at[n - 1], hs.at[n - 1], hr.at[n - 1], cm.at_y(n))
            )

    @cm.when(950)
    def _():
        for copy in heads:
            copy.wait_recv()
        o_out[...] = (mine[cm.me] + theirs[0]) + (theirs[1] + theirs[2])

    times = {
        "block": (0.1, 1.5, 3, 4.5),
        "settle": (2.9, 4.4, 5.9, 7.1),
        "A": (3, 4.5, 6, 13.5, 32),
        "B": (7.2, 7.3, 7.4, 17.5, 36.5),
        "A2": (32.1, 32.2, 32.3, 36, 39.5),
        "B2": (36.6, 36.7, 36.8, 40.5, 44),
    }
    products = [(cot, [act], 0), (normed, [d_proj.at[k] for k in range(3)], w), (d_low, [gated], w + 768)]
    grad_scatter(cm, products, G, RC, wa, bufs, sems, times, done_a, done_b)

    def small_done(gains, rest):
        o_mix[...] = gains[0:8]
        o_ffn[...] = gains[8:16]
        for k in range(3):
            for h in range(2):
                o_conv[k : k + 1, pl.ds(128 * h, 128)] = rest[2 * k + h : 2 * k + h + 1]

    small_sums(cm, small, sm, sr, ss, sr_sem, (19.1, 23, 27, 33, 38), small_done)
    cm.run()


VMEM_SPEC = pl.BlockSpec(memory_space=pltpu.VMEM)


def call(kernel, name, cid, args, outs, scratch, limit):
    return pl.pallas_call(
        kernel,
        out_shape=outs,
        in_specs=[VMEM_SPEC] * len(args),
        out_specs=(VMEM_SPEC,) * len(outs),
        scratch_shapes=scratch,
        compiler_params=pltpu.CompilerParams(
            collective_id=cid, has_side_effects=True, vmem_limit_bytes=limit << 20
        ),
        cost_estimate=pl.CostEstimate(flops=1, bytes_accessed=1, transcendentals=0),
        name=name,
    )(*args)


def scatter_scratch(W, wa):
    f32 = jnp.float32
    wb = W - wa
    return [
        pltpu.VMEM((4, 4, 2, 32, W), f32),
        pltpu.VMEM((4, 4, 32, W), f32),
        pltpu.VMEM((2, 2, 32, wa), f32),
        pltpu.VMEM((2, 2, 32, wb), f32),
        pltpu.VMEM((2, 2, 2, 32, wa), f32),
        pltpu.VMEM((2, 2, 2, 32, wb), f32),
        pltpu.VMEM((2, 1, 16, wa), f32),
        pltpu.VMEM((2, 1, 16, wb), f32),
        pltpu.VMEM((2, 2, 1, 16, wa), f32),
        pltpu.VMEM((2, 2, 1, 16, wb), f32),
    ]


SCATTER_SEMS = [pltpu.SemaphoreType.DMA((n,)) for n in (4, 4, 12, 12, 12, 12)]


def front(gated, ow, tokens, cot, down, gain):
    T, D = tokens.shape
    f32, bf16, shape, dma = jnp.float32, jnp.bfloat16, jax.ShapeDtypeStruct, pltpu.SemaphoreType.DMA
    outs = (
        shape((T, D), bf16),
        shape((4, *ow.shape), bf16),
        shape((T // 4, D), bf16),
        shape((T, down.shape[1]), f32),
        shape((T // 4, D), f32),
        shape((T // 4, D), bf16),
        shape((T // 4, D), bf16),
    )
    scratch = [
        pltpu.VMEM((T, D), f32),
        pltpu.VMEM((4, *gated.shape), f32),
        pltpu.VMEM((4, 4, 2, 4, 32, ow.shape[1]), f32),
        dma((6,)),
        dma((6,)),
        dma((20,)),
        dma((20,)),
    ]
    return call(front_kernel, "front", 3, (gated, ow, tokens, cot, down, gain), outs, scratch, 24)


def middle(*args):
    dn, act, proj = args[0], args[7], args[10]
    T, D = dn.shape
    H = T // 8
    f32, bf16, shape, dma = jnp.float32, jnp.bfloat16, jax.ShapeDtypeStruct, pltpu.SemaphoreType.DMA
    w = act.shape[1]
    outs = (
        shape((T // 4, D), f32),
        shape((T // 4, D), bf16),
        shape((1, D), f32),
        shape((T, D), bf16),
        shape((32, w), f32),
        shape((32, w), f32),
        shape(proj.shape, bf16),
        shape((T, D), f32),
        shape((3, 256), f32),
    )
    scratch = [
        pltpu.VMEM((T, D), f32),
        pltpu.VMEM((T, D), f32),
        pltpu.VMEM((3, 2 * H, 256), f32),
        pltpu.VMEM((2, H, 256), f32),
        pltpu.VMEM((T, 256), f32),
        pltpu.VMEM((T + 8, 256), f32),
        pltpu.VMEM((2, 2, H, D), f32),
        pltpu.VMEM((2, 2, 2, H, D), f32),
        *scatter_scratch(2 * w, w),
        dma((2, 12)),
        dma((2, 12)),
        *SCATTER_SEMS,
        dma((7,)),
        dma((7,)),
        dma((1,)),
        dma((1,)),
    ]
    return call(middle_kernel, "middle", 5, args, outs, scratch, 38)


def end(*args):
    dm, act = args[0], args[8]
    T, D = dm.shape
    H = T // 8
    f32, shape, dma = jnp.float32, jax.ShapeDtypeStruct, pltpu.SemaphoreType.DMA
    w = act.shape[1]
    outs = (
        shape((T, D), f32),
        shape((3, 32, 256), f32),
        shape((32, 256), f32),
        shape((32, w), f32),
        shape((8, 128), f32),
        shape((8, 128), f32),
        shape((3, 256), f32),
    )
    scratch = [
        pltpu.VMEM((2, H, D), f32),
        pltpu.VMEM((2, 2, H, D), f32),
        *scatter_scratch(w + 1792, w + 256),
        pltpu.VMEM((24, 128), f32),
        pltpu.VMEM((3, 24, 128), f32),
        pltpu.VMEM((4, 4, 24, 128), f32),
        dma((12,)),
        dma((12,)),
        *SCATTER_SEMS,
        dma((10,)),
        dma((10,)),
        pltpu.VMEM((4, 32, 256), f32),
        pltpu.VMEM((3, 32, 256), f32),
        dma((3,)),
        dma((3,)),
    ]
    return call(end_kernel, "end", 7, args, outs, scratch, 36)


def place(*arrays):
    n = len(arrays)

    def kernel(*refs):
        copies = [pltpu.make_async_copy(refs[i], refs[n + i], refs[2 * n].at[i]) for i in range(n)]
        for copy in copies:
            copy.start()
        for copy in copies:
            copy.wait()

    anywhere = pl.BlockSpec(memory_space=pl.ANY)
    return pl.pallas_call(
        kernel,
        out_shape=tuple(jax.ShapeDtypeStruct(a.shape, a.dtype) for a in arrays),
        in_specs=[VMEM_SPEC] * n,
        out_specs=(anywhere,) * n,
        scratch_shapes=[pltpu.SemaphoreType.DMA((n,))],
        compiler_params=pltpu.CompilerParams(vmem_limit_bytes=2 << 20),
        name="place",
    )(*arrays)


def from_behind(block, axis, distance):
    devices = range(lax.axis_size(axis))
    route = [(i - distance, i) for i in devices if i - distance in devices]
    return lax.ppermute(block, axis, route)


def rms_scale(values):
    return lax.rsqrt(jnp.mean(values * values, axis=-1, keepdims=True) + EPS)


def right_product(left, right):
    return lax.dot_general(
        left, right, (((1,), (1,)), ((), ())), preferred_element_type=jnp.float32
    )


def on_device(
    tokens,
    segment_ids,
    mix_gain,
    in_weight,
    conv_weight,
    out_weight,
    ffn_gain,
    gate_weight,
    up_weight,
    down_weight,
    cotangent,
):
    tok_rows = tokens.shape[0]
    first_row = lax.axis_index("seq") * tok_rows
    padded_ids = jnp.concatenate(
        [jnp.full((2,), -1, jnp.int32), segment_ids, jnp.full((2,), -2, jnp.int32)]
    )
    id_window = lax.dynamic_slice_in_dim(padded_ids, first_row, tok_rows + 4)
    near_ext = (id_window[2 : tok_rows + 4] == id_window[1 : tok_rows + 3]).astype(jnp.float32)
    far_ext = (id_window[2 : tok_rows + 4] == id_window[0 : tok_rows + 2]).astype(jnp.float32)
    near_own = near_ext[:tok_rows, None]
    far_own = far_ext[:tok_rows, None]
    inputs = tokens.astype(jnp.float32)
    mix_scale = rms_scale(inputs)
    mix_normed = (inputs * mix_scale * mix_gain).astype(jnp.bfloat16)
    projected = jnp.einsum("td,dkc->tkc", mix_normed, in_weight, preferred_element_type=jnp.float32)
    chan_b = projected[:, 0]
    chan_c = projected[:, 1]
    chan_x = projected[:, 2]
    mixed = chan_b * chan_x
    edge_rows = from_behind(mixed[tok_rows - 2 :], "seq", 1)
    extended = jnp.concatenate([edge_rows, mixed])
    kernel = conv_weight.astype(jnp.float32)
    prev_one = extended[1 : tok_rows + 1]
    prev_two = extended[0:tok_rows]
    conv_out = kernel[0] * mixed + kernel[1] * near_own * prev_one + kernel[2] * far_own * prev_two
    gated = (chan_c * conv_out).astype(jnp.bfloat16)
    ffn_normed, out_full, gated_rows, d_act, own_resid, own_cot, own_tok = front(
        gated, out_weight, tokens, cotangent, down_weight, ffn_gain[None]
    )
    gate = jnp.dot(ffn_normed, gate_weight, preferred_element_type=jnp.float32)
    upper = jnp.dot(ffn_normed, up_weight, preferred_element_type=jnp.float32)
    sigma = jax.nn.sigmoid(gate)
    act = (gate * sigma * upper).astype(jnp.bfloat16)
    d_gate = (d_act * upper * sigma * (1.0 + gate * (1.0 - sigma))).astype(jnp.bfloat16)
    d_up = (d_act * gate * sigma).astype(jnp.bfloat16)
    d_normed_part = right_product(d_gate, gate_weight) + right_product(d_up, up_weight)
    marks = jnp.stack(
        [near_own[:, 0], far_own[:, 0], near_ext[1 : tok_rows + 1], far_ext[2 : tok_rows + 2]], axis=1
    )
    d_resid, d_resid_low, grad_ffn_gain, result, gate_share, up_share, d_projected, d_mix_part, grad_conv = middle(
        d_normed_part,
        own_resid,
        ffn_gain[None],
        own_cot,
        ffn_normed,
        d_gate,
        d_up,
        act,
        down_weight,
        out_full,
        projected.transpose(1, 0, 2),
        jnp.concatenate([jnp.zeros((6, mixed.shape[1]), jnp.float32), extended]),
        conv_out,
        marks,
        kernel,
        in_weight.transpose(1, 0, 2),
    )
    grad_tokens, in_share, out_share, down_share, mix_total, ffn_total, conv_total = end(
        d_mix_part,
        own_tok,
        mix_gain[None],
        d_resid,
        mix_normed,
        d_projected,
        d_resid_low,
        gated_rows,
        act,
        cotangent,
        grad_ffn_gain,
        grad_conv,
    )
    (
        result,
        grad_tokens,
        mix_total,
        in_share,
        conv_total,
        out_share,
        ffn_total,
        gate_share,
        up_share,
        down_share,
    ) = place(
        result,
        grad_tokens,
        mix_total,
        in_share,
        conv_total,
        out_share,
        ffn_total,
        gate_share,
        up_share,
        down_share,
    )
    return (
        result,
        grad_tokens,
        mix_total.reshape(-1),
        in_share.transpose(1, 0, 2),
        conv_total,
        out_share,
        ffn_total.reshape(-1),
        gate_share,
        up_share,
        down_share,
    )


def solution(mesh):
    placed = (
        P("seq", None),
        P(),
        P(),
        P(None, None, "head"),
        P(None, "head"),
        P(None, "head"),
        P(),
        P(None, "head"),
        P(None, "head"),
        P(None, "head"),
        P("seq", None),
    )
    return jax.shard_map(
        on_device,
        mesh=mesh,
        in_specs=placed,
        out_specs=(
            P("seq", None),
            P("seq", None),
            P(),
            P("seq", None, "head"),
            P(None, "head"),
            P("seq", "head"),
            P(),
            P("seq", "head"),
            P("seq", "head"),
            P("seq", "head"),
        ),
        check_vma=False,
    )
```

```python
import jax
import jax.numpy as jnp
from jax import lax
from jax.experimental import pallas as pl
from jax.experimental.pallas import tpu as pltpu
from jax.sharding import PartitionSpec as P

EPS = 1e-05
MESH = pl.DeviceIdType.MESH


def norm_back_rows(grad_normed, values, gain, extra):
    scale = lax.rsqrt(jnp.mean(values * values, axis=-1, keepdims=True) + EPS)
    weighted = grad_normed * gain
    inner = jnp.mean(weighted * values, axis=-1, keepdims=True)
    grad_values = extra + (scale * weighted - values * (scale * scale * scale) * inner)
    return grad_values, jnp.sum(grad_normed * values * scale, axis=0, keepdims=True)


class Comm:
    def __init__(self):
        seq = lax.axis_index("seq")
        self.me = lax.axis_index("head")
        self.core = lax.rem(seq, 2)
        self.z = lax.rem(lax.div(seq, 2), 4)
        self.x = lax.div(seq, 8)
        self.every = []
        self.steps = []

    def at_x(self, n):
        return {"seq": (ahead(self.x, n) * 4 + self.z) * 2 + self.core, "head": self.me}

    def at_z(self, n):
        return {"seq": (self.x * 4 + ahead(self.z, n)) * 2 + self.core, "head": self.me}

    def at_y(self, n):
        return {"seq": (self.x * 4 + self.z) * 2 + self.core, "head": ahead(self.me, n)}

    def twin(self, n=1):
        return {"seq": (self.x * 4 + self.z) * 2 + (1 - self.core), "head": self.me}

    def along(self, n):
        return {"seq": lax.rem((self.x * 4 + self.z) * 2 + self.core + n, 32), "head": self.me}

    def greet(self, devices):
        barrier = pltpu.get_barrier_semaphore()
        for device in devices:
            pl.semaphore_signal(barrier, inc=1, device_id=device, device_id_type=MESH)
        pl.semaphore_wait(barrier, len(devices))

    def send(self, src, dst, s_sem, r_sem, dev):
        copy = pltpu.make_async_remote_copy(
            src_ref=src, dst_ref=dst, send_sem=s_sem, recv_sem=r_sem, device_id=dev, device_id_type=MESH
        )
        copy.start()
        self.every.append(copy)
        return copy

    def when(self, time):
        def add(fn):
            self.steps.append((time, len(self.steps), fn))
            return fn

        return add

    def run(self):
        for _, _, fn in sorted(self.steps, key=lambda s: s[:2]):
            fn()
        for copy in self.every:
            copy.wait_send()


def ahead(k, n):
    return lax.rem(k + n, 4)


def add_up(dst, *srcs):
    n, r = dst.shape[:2]
    q = r // 8

    def body(i, carry):
        b, at = lax.div(i, q), pl.ds(pl.multiple_of(lax.rem(i, q) * 8, 8), 8)
        total = dst[b, at, :]
        for src in srcs:
            total = total + src[b, at, :]
        dst[b, at, :] = total
        return carry

    lax.fori_loop(0, n * q, body, 0)


def head_sum(cm, p, o, t, f, s_sem, r_sem, finish, times, closing, share=True):
    T = p.shape[0]
    C = T // 4
    H = C // 2
    R, L, O = ahead(cm.me, 1), ahead(cm.me, 3), ahead(cm.me, 2)
    me = cm.me
    c = {}

    def rows(k, half):
        return pl.ds(pl.multiple_of(k * C + half * H, H), H)

    def go(name, src, dst, i, n):
        c[name] = cm.send(src, dst, s_sem.at[i], r_sem.at[i], cm.at_y(n))

    @cm.when(times[0])
    def _():
        go("a0", p.at[rows(O, 0)], t.at[0], 0, 1)
        go("a1", p.at[rows(O, 1)], t.at[1], 1, 3)
        go("a2", p.at[rows(R, 1)], f.at[0, 1], 2, 1)
        go("a3", p.at[rows(L, 0)], f.at[1, 0], 3, 3)

    @cm.when(times[1])
    def _():
        c["a0"].wait_recv()
        t[0] = p[rows(R, 0), :] + t[0]
        go("a4", t.at[0], f.at[0, 0], 4, 1)
        c["a1"].wait_recv()
        t[1] = p[rows(L, 1), :] + t[1]
        go("a5", t.at[1], f.at[1, 1], 5, 3)

    @cm.when(times[2])
    def _():
        c["a3"].wait_recv()
        c["a4"].wait_recv()
        first = finish(0, p[rows(me, 0), :] + f[0, 0] + f[1, 0])
        if not share:
            c["a2"].wait_recv()
            c["a5"].wait_recv()
            o[0:H, :] = first
            o[H:C, :] = finish(1, p[rows(me, 1), :] + f[0, 1] + f[1, 1])
            return
        o[rows(me, 0), :] = first
        go("b0", o.at[rows(me, 0)], o.at[rows(me, 0)], 6, 1)
        go("c0", o.at[rows(me, 0)], o.at[rows(me, 0)], 8, 3)
        c["a2"].wait_recv()
        c["a5"].wait_recv()
        o[rows(me, 1), :] = finish(1, p[rows(me, 1), :] + f[0, 1] + f[1, 1])
        go("c1", o.at[rows(me, 1)], o.at[rows(me, 1)], 9, 3)
        go("b1", o.at[rows(me, 1)], o.at[rows(me, 1)], 7, 1)

    if not share:
        return

    @cm.when(times[3])
    def _():
        c["b0"].wait_recv()
        go("d0", o.at[rows(L, 0)], o.at[rows(L, 0)], 10, 1)
        c["c1"].wait_recv()
        go("d1", o.at[rows(R, 1)], o.at[rows(R, 1)], 11, 3)

    @cm.when(900)
    def _():
        for name in ("b1", "c0", "d0", "d1"):
            c[name].wait_recv()
        closing()


def scatter_ring(cm, chunk, t, f, s_sem, r_sem, base, to, times, done):
    c = {}

    def go(name, src, dst, i, n):
        c[name] = cm.send(src, dst, s_sem.at[base + i], r_sem.at[base + i], to(n))

    @cm.when(times[0])
    def _():
        go("a0", chunk(2, 0), t.at[0], 0, 1)
        go("a1", chunk(2, 1), t.at[1], 1, 3)

    @cm.when(times[1])
    def _():
        go("a2", chunk(1, 1), f.at[0, 1], 2, 1)

    @cm.when(times[2])
    def _():
        go("a3", chunk(3, 0), f.at[1, 0], 3, 3)

    @cm.when(times[3])
    def _():
        c["a0"].wait_recv()
        add_up(t.at[0], chunk(1, 0))
        go("a4", t.at[0], f.at[0, 0], 4, 1)
        c["a1"].wait_recv()
        add_up(t.at[1], chunk(3, 1))
        go("a5", t.at[1], f.at[1, 1], 5, 3)

    @cm.when(times[4])
    def _():
        c["a3"].wait_recv()
        c["a4"].wait_recv()
        add_up(chunk(0, 0), f.at[0, 0], f.at[1, 0])
        c["a2"].wait_recv()
        c["a5"].wait_recv()
        add_up(chunk(0, 1), f.at[0, 1], f.at[1, 1])
        done()


def grad_scatter(cm, products, G, RC, wa, bufs, sems, times, done_a, done_b):
    tA, tB, fA, fB, t2A, t2B, f2A, f2B = bufs
    cs, cr, as_, ar, bs, br = sems
    W = G.shape[-1]
    quarter = products[0][0].shape[1] // 4
    got = {}

    def block(turn):
        k = ahead(cm.x, turn)
        for left, rights, at in products:
            right = jnp.concatenate([r[...] for r in rights], axis=1)
            w = right.shape[1]
            lhs = left[:, pl.ds(pl.multiple_of(k * quarter, quarter), quarter)]
            value = lax.dot_general(
                lhs, right, (((0,), (0,)), ((), ())), preferred_element_type=jnp.float32
            )
            G[k, :, :, :, pl.ds(at, w)] = value.reshape(4, 2, 32, w)
        got[turn] = cm.send(G.at[k, :, 1 - cm.core], RC.at[k], cs.at[turn], cr.at[turn], cm.twin())

    def settle(turn):
        k = ahead(cm.x, turn)
        got[turn].wait_recv()
        add_up(G.at[k, :, cm.core], RC.at[k])

    for i, turn in enumerate((2, 1, 3, 0)):
        cm.when(times["block"][i])(lambda turn=turn: block(turn))
        cm.when(times["settle"][i])(lambda turn=turn: settle(turn))

    cols_a, cols_b = pl.ds(0, wa), pl.ds(wa, W - wa)
    core = cm.core

    def a1(turn, half):
        return G.at[ahead(cm.x, turn), pl.ds(half * 2, 2), core, :, cols_a]

    def b1(turn, half):
        return G.at[pl.ds(half * 2, 2), ahead(cm.z, turn), core, :, cols_b]

    def a2(turn, half):
        return G.at[cm.x, pl.ds(ahead(cm.z, turn), 1), core, pl.ds(half * 16, 16), cols_a]

    def b2(turn, half):
        return G.at[pl.ds(ahead(cm.x, turn), 1), cm.z, core, pl.ds(half * 16, 16), cols_b]

    nothing = lambda: None
    scatter_ring(cm, a1, tA, fA, as_, ar, 0, cm.at_x, times["A"], nothing)
    scatter_ring(cm, b1, tB, fB, bs, br, 0, cm.at_z, times["B"], nothing)
    scatter_ring(cm, a2, t2A, f2A, as_, ar, 6, cm.at_z, times["A2"], done_a)
    scatter_ring(cm, b2, t2B, f2B, bs, br, 6, cm.at_x, times["B2"], done_b)


def small_sums(cm, small, sm, sr, s_sem, r_sem, times, done):
    axes = [(cm.at_z, cm.z), (cm.at_x, cm.x), (cm.at_y, cm.me)]
    first = {}

    @cm.when(times[0])
    def _():
        first["c"] = cm.send(small, sr.at[3, 0], s_sem.at[9], r_sem.at[9], cm.twin())

    @cm.when(times[1])
    def _():
        first["c"].wait_recv()
        sm[0] = small[...] + sr[3, 0]

    for a, (to, here) in enumerate(axes):
        copies = []

        def begin(a=a, to=to, here=here, copies=copies):
            sr[a, here] = sm[a]
            for n in (1, 2, 3):
                i = a * 3 + n - 1
                copies.append(cm.send(sm.at[a], sr.at[a, here], s_sem.at[i], r_sem.at[i], to(n)))

        def end(a=a, copies=copies):
            for copy in copies:
                copy.wait_recv()
            total = (sr[a, 0] + sr[a, 1]) + (sr[a, 2] + sr[a, 3])
            if a < 2:
                sm[a + 1] = total
            else:
                done(total[0:16], sm[2][16:24])

        cm.when(times[1] + 0.01)(begin) if a == 0 else cm.when(times[1 + a] + 0.01)(begin)
        cm.when(times[2 + a])(end)


def greet_all(cm, more):
    cm.greet([axis(n) for n in (1, 2, 3) for axis in (cm.at_x, cm.at_z, cm.at_y)] + [cm.twin()] + more)


def front_kernel(
    gated, ow, tokens, cot, down, gain, o_normed, o_full, o_own, o_dact, o_resid, o_cot, o_tok, resid, GF, WF, ys, yr, ws, wr
):
    cm = Comm()
    x, z, c, me = cm.x, cm.z, cm.core, cm.me
    R, L, O = ahead(me, 1), ahead(me, 3), ahead(me, 2)
    cm.greet([cm.at_x(1), cm.at_x(3), cm.at_z(1), cm.at_z(3), cm.at_y(1), cm.at_y(2), cm.at_y(3), cm.twin()])
    T = gated.shape[0]
    N = T // 2
    piece = ((x * 4 + z) * 2 + c) * 32
    h = {}

    def weight(name, ref, i, dev):
        h[name] = cm.send(ref, ref, ws.at[i], wr.at[i], dev)

    def gate(name, ref, i, n):
        h[name] = cm.send(ref, ref, ys.at[i], yr.at[i], cm.at_y(n))

    low, high = pl.ds(0, 2), pl.ds(2, 2)
    WF[x, z, c, me] = ow[pl.ds(pl.multiple_of(piece, 32), 32), :].astype(jnp.float32)
    for n in (1, 2, 3):
        weight(("y", n), WF.at[x, z, c, me], n - 1, cm.at_y(n))
    GF[me] = gated[...].astype(jnp.float32)
    first, second = pl.ds(0, N), pl.ds(N, N)
    gate("r0", GF.at[me, first], 0, 1)
    gate("l1", GF.at[me, second], 1, 3)
    gate("r1", GF.at[me, second], 2, 1)
    gate("l0", GF.at[me, first], 3, 3)
    for n in (1, 2, 3):
        h["y", n].wait_recv()
    weight("ax1", WF.at[x, z, c, low], 3, cm.at_x(1))
    weight("ax3", WF.at[x, z, c, low], 4, cm.at_x(3))
    weight("bz1", WF.at[x, z, c, high], 5, cm.at_z(1))
    weight("bz3", WF.at[x, z, c, high], 6, cm.at_z(3))
    resid[...] = tokens[...].astype(jnp.float32) + lax.dot_general(
        gated[...], ow[...], (((1,), (1,)), ((), ())), preferred_element_type=jnp.float32
    )
    mine = pl.ds(pl.multiple_of(me * (T // 4), T // 4), T // 4)
    o_cot[...] = cot[mine, :]
    o_tok[...] = tokens[mine, :]
    xl, xr, zl, zr = ahead(x, 3), ahead(x, 1), ahead(z, 3), ahead(z, 1)
    h["ax1"].wait_recv()
    weight("ax1f", WF.at[xl, z, c, 0], 7, cm.at_x(1))
    h["ax3"].wait_recv()
    weight("ax3f", WF.at[xr, z, c, 1], 8, cm.at_x(3))
    h["bz1"].wait_recv()
    weight("bz1f", WF.at[x, zl, c, 2], 9, cm.at_z(1))
    h["bz3"].wait_recv()
    weight("bz3f", WF.at[x, zr, c, 3], 10, cm.at_z(3))
    h["ax1f"].wait_recv()
    h["ax3f"].wait_recv()
    weight("az1", WF.at[:, z, c, low], 11, cm.at_z(1))
    weight("az3", WF.at[:, z, c, low], 12, cm.at_z(3))
    h["bz1f"].wait_recv()
    h["bz3f"].wait_recv()
    weight("bx1", WF.at[x, :, c, high], 13, cm.at_x(1))
    weight("bx3", WF.at[x, :, c, high], 14, cm.at_x(3))
    o_dact[...] = jnp.dot(cot[...], down[...], preferred_element_type=jnp.float32)
    h["r0"].wait_recv()
    gate("r0f", GF.at[L, first], 4, 1)
    h["l1"].wait_recv()
    gate("l1f", GF.at[R, second], 5, 3)
    h["az1"].wait_recv()
    weight("az1f", WF.at[:, zl, c, 0], 15, cm.at_z(1))
    h["az3"].wait_recv()
    weight("az3f", WF.at[:, zr, c, 1], 16, cm.at_z(3))
    h["bx1"].wait_recv()
    weight("bx1f", WF.at[xl, :, c, 2], 17, cm.at_x(1))
    h["bx3"].wait_recv()
    weight("bx3f", WF.at[xr, :, c, 3], 18, cm.at_x(3))
    for name in ("az1f", "az3f", "bx1f", "bx3f"):
        h[name].wait_recv()
    weight("twin", WF.at[:, :, c], 19, cm.twin())
    h["r1"].wait_recv()
    h["l0"].wait_recv()
    h["twin"].wait_recv()
    for k in range(4):
        o_full[k] = WF[:, :, :, k].reshape(1024, 256).astype(jnp.bfloat16)

    def add(k):
        low_gated = GF[k].astype(jnp.bfloat16)
        resid[...] += lax.dot_general(
            low_gated, o_full[k], (((1,), (1,)), ((), ())), preferred_element_type=jnp.float32
        )

    add(L)
    add(R)
    h["r0f"].wait_recv()
    h["l1f"].wait_recv()
    add(O)
    for k in range(4):
        o_own[:, 256 * k : 256 * (k + 1)] = GF[k, mine, :].astype(jnp.bfloat16)
    o_resid[...] = resid[mine, :]

    def body(i, carry):
        rows = pl.ds(pl.multiple_of(i * 32, 32), 32)
        values = resid[rows, :]
        scale = lax.rsqrt(jnp.mean(values * values, axis=-1, keepdims=True) + EPS)
        o_normed[rows, :] = (values * scale * gain[...]).astype(jnp.bfloat16)
        return carry

    lax.fori_loop(0, T // 32, body, 0)
    cm.run()


EARLY = 256


def middle_kernel(*refs):
    (dn, own_resid, gain, own_cot, normed, d_gate, d_up, act, down, ow) = refs[:10]
    (proj, mixed, conv_out, marks, taps, in_w, toks, cot) = refs[10:18]
    (o_dres, o_dlow, o_gain, o_res, o_gate, o_up, o_down, o_dproj, o_dm, o_taps, o_mix) = refs[18:29]
    (rp, full, turned, relay, dgated, DC, yt, yf, G, RC) = refs[29:39]
    bufs, (ys, yr), sems, (xs, xr), (hs, hr) = refs[39:47], refs[47:49], refs[49:55], refs[55:57], refs[57:]
    H = own_resid.shape[0] // 2
    T = 8 * H
    cm = Comm()
    greet_all(cm, [cm.along(1), cm.along(31)])

    def finish_dres(half, total):
        mine = pl.ds(half * H, H)
        rows, gains = norm_back_rows(
            total, own_resid[mine, :], gain[...], own_cot[mine, :].astype(jnp.float32)
        )
        o_gain[...] = gains if half == 0 else o_gain[...] + gains
        return rows

    def finish_result(half, total):
        return total + own_resid[pl.ds(half * H, H), :]

    def rounded():
        o_res[...] = full[...].astype(jnp.bfloat16)

    @cm.when(0.02)
    def _():
        rp[...] = lax.dot_general(
            act[...], down[...], (((1,), (1,)), ((), ())), preferred_element_type=jnp.float32
        )

    head_sum(cm, dn, o_dres, yt.at[0], yf.at[0], ys.at[0], yr.at[0], finish_dres, (0, 7, 18, 0), lambda: None, False)
    head_sum(cm, rp, full, yt.at[1], yf.at[1], ys.at[1], yr.at[1], finish_result, (7.05, 25, 44, 56), rounded)

    C = 2 * H
    R, L = ahead(cm.me, 1), ahead(cm.me, 3)
    c = {}

    def rows(k, half=None):
        if half is None:
            return pl.ds(pl.multiple_of(k * C, C), C)
        return pl.ds(pl.multiple_of(k * C + half * H, H), H)

    def go(name, src, dst, i, n):
        c[name] = cm.send(src, dst, xs.at[i], xr.at[i], cm.at_y(n))

    @cm.when(18.1)
    def _():
        low = o_dres[...].astype(jnp.bfloat16)
        o_dlow[...] = low
        for turn in (2, 1, 3):
            turned[turn - 1] = jnp.dot(low, ow[ahead(cm.me, turn)], preferred_element_type=jnp.float32)
            if turn == 2:
                go("e0", turned.at[1, pl.ds(0, H)], relay.at[0], 0, 1)
                go("e1", turned.at[1, pl.ds(H, H)], relay.at[1], 1, 3)
            else:
                go(("d", turn), turned.at[turn - 1], dgated.at[rows(cm.me)], 1 + turn, turn)
        dgated[rows(cm.me), :] = jnp.dot(low, ow[cm.me], preferred_element_type=jnp.float32)

    @cm.when(32)
    def _():
        c["e0"].wait_recv()
        go("f0", relay.at[0], dgated.at[rows(L, 0)], 5, 1)
        c["e1"].wait_recv()
        go("f1", relay.at[1], dgated.at[rows(R, 1)], 6, 3)

    N = 64

    @cm.when(38)
    def _():
        for name in (("d", 1), ("d", 3), "f0", "f1"):
            c[name].wait_recv()
        for i in range(T // N):
            at = pl.ds(i * N, N)
            dg = dgated[at, :]
            o_dproj[1, at, :] = (dg * conv_out[at, :]).astype(jnp.bfloat16)
            DC[at, :] = dg * proj[1, at, :]
        c["halo"] = cm.send(DC.at[pl.ds(0, 8)], DC.at[pl.ds(T, 8)], hs.at[0], hr.at[0], cm.along(31))

    @cm.when(41)
    def _():
        c["halo"].wait_recv()
        w0, w1, w2 = taps[0:1, :], taps[1:2, :], taps[2:3, :]
        sums = [jnp.zeros((1, 256), jnp.float32)] * 3
        for i in range(T // N):
            at = pl.ds(i * N, N)
            near, far = marks[at, 0:1], marks[at, 1:2]
            near_next, far_next = marks[at, 2:3], marks[at, 3:4]
            dc = DC[at, :]
            d_mixed = w0 * dc + w1 * near_next * DC[pl.ds(i * N + 1, N), :] + w2 * far_next * DC[pl.ds(i * N + 2, N), :]
            o_dproj[0, at, :] = (d_mixed * proj[2, at, :]).astype(jnp.bfloat16)
            o_dproj[2, at, :] = (d_mixed * proj[0, at, :]).astype(jnp.bfloat16)
            terms = (
                dc * mixed[pl.ds(i * N + 8, N), :],
                dc * near * mixed[pl.ds(i * N + 7, N), :],
                dc * far * mixed[pl.ds(i * N + 6, N), :],
            )
            sums = [s + jnp.sum(t, axis=0, keepdims=True) for s, t in zip(sums, terms)]
        for k in range(3):
            o_taps[k : k + 1, :] = sums[k]

    @cm.when(45)
    def _():
        right = jnp.concatenate([in_w[0], in_w[1], in_w[2]], axis=1)
        for i in range(4):
            at = pl.ds(i * C, C)
            left = jnp.concatenate([o_dproj[0, at, :], o_dproj[1, at, :], o_dproj[2, at, :]], axis=1)
            o_dm[at, :] = lax.dot_general(
                left, right, (((1,), (1,)), ((), ())), preferred_element_type=jnp.float32
            )

        def body(i, total):
            at = pl.ds(pl.multiple_of(i * 32, 32), 32)
            values = toks[at, :].astype(jnp.float32)
            scale = lax.rsqrt(jnp.mean(values * values, axis=-1, keepdims=True) + EPS)
            return total + jnp.sum(o_dm[at, :] * values * scale, axis=0, keepdims=True)

        o_mix[...] = lax.fori_loop(0, T // 32, body, jnp.zeros(o_mix.shape, jnp.float32))

    w = act.shape[1]
    e = EARLY // 2

    def done_a():
        rows = G[cm.x, cm.z, cm.core, :, pl.ds(0, w + e)]
        o_gate[...] = rows[:, :w]
        o_down[:, pl.ds(0, e)] = rows[:, w:]

    def done_b():
        rows = G[cm.x, cm.z, cm.core, :, pl.ds(w + e, w + e)]
        o_down[:, pl.ds(e, e)] = rows[:, :e]
        o_up[...] = rows[:, e:]

    times = {
        "block": (4, 5.2, 7.2, 8.4),
        "settle": (6.8, 8, 9.5, 11),
        "A": (6.9, 8.1, 9.6, 15, 32),
        "B": (11.1, 11.2, 11.3, 20, 36),
        "A2": (32.1, 32.2, 32.3, 36.1, 41.1),
        "B2": (36.2, 36.3, 36.4, 41.2, 46),
    }
    products = [(normed, [d_gate], 0), (cot, [act.at[:, pl.ds(0, EARLY)]], w), (normed, [d_up], w + EARLY)]
    grad_scatter(cm, products, G, RC, w + e, bufs, sems, times, done_a, done_b)
    cm.run()


def end_kernel(*refs):
    (dm, toks, gain, d_res, normed, d_proj, d_low, gated, act, cot, mix_gains, ffn_gains, taps) = refs[:13]
    (o_tok, o_in, o_out, o_down, o_mix, o_ffn, o_conv) = refs[13:20]
    (yt, yf, G, RC) = refs[20:24]
    bufs = refs[24:32]
    small, sm, sr = refs[32:35]
    ys, yr = refs[35:37]
    sems = refs[37:43]
    ss, sr_sem = refs[43:45]
    mine, theirs, hs, hr = refs[45:]
    H = toks.shape[0] // 2
    cm = Comm()
    greet_all(cm, [])

    def finish_tokens(half, total):
        at = pl.ds(half * H, H)
        return norm_back_rows(total, toks[at, :].astype(jnp.float32), gain[...], d_res[at, :])[0]

    @cm.when(-1)
    def _():
        small[16:24, :] = jnp.zeros((8, 128), jnp.float32)
        for k in range(8):
            small[k : k + 1, :] = mix_gains[:, 128 * k : 128 * (k + 1)]
            small[8 + k : 9 + k, :] = ffn_gains[:, 128 * k : 128 * (k + 1)]
        for k in range(3):
            for h in range(2):
                small[16 + 2 * k + h : 17 + 2 * k + h, :] = taps[k : k + 1, 128 * h : 128 * (h + 1)]

    head_sum(cm, dm, o_tok, yt, yf, ys, yr, finish_tokens, (0, 7, 19.5, 27), lambda: None)

    w = act.shape[1] - EARLY
    wa = w + 512
    heads = []

    def done_a():
        rows = G[cm.x, cm.z, cm.core, :, pl.ds(0, wa)]
        o_down[...] = rows[:, :w]
        o_in[0] = rows[:, w : w + 256]
        o_in[1] = rows[:, w + 256 :]

    def done_b():
        rows = G[cm.x, cm.z, cm.core, :, pl.ds(wa, 1280)]
        o_in[2] = rows[:, :256]
        for k in range(4):
            mine[k] = rows[:, 256 + 256 * k : 512 + 256 * k]
        for n in (1, 2, 3):
            heads.append(
                cm.send(mine.at[ahead(cm.me, n)], theirs.at[n - 1], hs.at[n - 1], hr.at[n - 1], cm.at_y(n))
            )

    @cm.when(950)
    def _():
        for copy in heads:
            copy.wait_recv()
        o_out[...] = (mine[cm.me] + theirs[0]) + (theirs[1] + theirs[2])

    times = {
        "block": (0.1, 1.5, 3, 4.5),
        "settle": (2.9, 4.4, 5.9, 6.9),
        "A": (3.02, 4.45, 5.95, 11, 25.5),
        "B": (6.95, 6.96, 6.97, 15.5, 31.5),
        "A2": (25.6, 25.7, 25.8, 28, 31),
        "B2": (31.6, 31.7, 31.8, 34, 37),
    }
    products = [(cot, [act.at[:, pl.ds(EARLY, w)]], 0), (normed, [d_proj.at[k] for k in range(3)], w), (d_low, [gated], w + 768)]
    grad_scatter(cm, products, G, RC, wa, bufs, sems, times, done_a, done_b)

    def small_done(gains, rest):
        o_mix[...] = gains[0:8]
        o_ffn[...] = gains[8:16]
        for k in range(3):
            for h in range(2):
                o_conv[k : k + 1, pl.ds(128 * h, 128)] = rest[2 * k + h : 2 * k + h + 1]

    small_sums(cm, small, sm, sr, ss, sr_sem, (-0.9, 0.05, 1.6, 3.05, 19), small_done)
    cm.run()


VMEM_SPEC = pl.BlockSpec(memory_space=pltpu.VMEM)


def call(kernel, name, cid, args, outs, scratch, limit):
    return pl.pallas_call(
        kernel,
        out_shape=outs,
        in_specs=[VMEM_SPEC] * len(args),
        out_specs=(VMEM_SPEC,) * len(outs),
        scratch_shapes=scratch,
        compiler_params=pltpu.CompilerParams(
            collective_id=cid, has_side_effects=True, vmem_limit_bytes=limit << 20
        ),
        cost_estimate=pl.CostEstimate(flops=1, bytes_accessed=1, transcendentals=0),
        name=name,
    )(*args)


def scatter_scratch(W, wa):
    f32 = jnp.float32
    wb = W - wa
    return [
        pltpu.VMEM((4, 4, 2, 32, W), f32),
        pltpu.VMEM((4, 4, 32, W), f32),
        pltpu.VMEM((2, 2, 32, wa), f32),
        pltpu.VMEM((2, 2, 32, wb), f32),
        pltpu.VMEM((2, 2, 2, 32, wa), f32),
        pltpu.VMEM((2, 2, 2, 32, wb), f32),
        pltpu.VMEM((2, 1, 16, wa), f32),
        pltpu.VMEM((2, 1, 16, wb), f32),
        pltpu.VMEM((2, 2, 1, 16, wa), f32),
        pltpu.VMEM((2, 2, 1, 16, wb), f32),
    ]


SCATTER_SEMS = [pltpu.SemaphoreType.DMA((n,)) for n in (4, 4, 12, 12, 12, 12)]


def front(gated, ow, tokens, cot, down, gain):
    T, D = tokens.shape
    f32, bf16, shape, dma = jnp.float32, jnp.bfloat16, jax.ShapeDtypeStruct, pltpu.SemaphoreType.DMA
    outs = (
        shape((T, D), bf16),
        shape((4, *ow.shape), bf16),
        shape((T // 4, D), bf16),
        shape((T, down.shape[1]), f32),
        shape((T // 4, D), f32),
        shape((T // 4, D), bf16),
        shape((T // 4, D), bf16),
    )
    scratch = [
        pltpu.VMEM((T, D), f32),
        pltpu.VMEM((4, *gated.shape), f32),
        pltpu.VMEM((4, 4, 2, 4, 32, ow.shape[1]), f32),
        dma((6,)),
        dma((6,)),
        dma((20,)),
        dma((20,)),
    ]
    return call(front_kernel, "front", 3, (gated, ow, tokens, cot, down, gain), outs, scratch, 24)


def middle(*args):
    dn, act, proj = args[0], args[7], args[10]
    T, D = dn.shape
    H = T // 8
    f32, bf16, shape, dma = jnp.float32, jnp.bfloat16, jax.ShapeDtypeStruct, pltpu.SemaphoreType.DMA
    w = act.shape[1]
    outs = (
        shape((T // 4, D), f32),
        shape((T // 4, D), bf16),
        shape((1, D), f32),
        shape((T, D), bf16),
        shape((32, w), f32),
        shape((32, w), f32),
        shape((32, EARLY), f32),
        shape(proj.shape, bf16),
        shape((T, D), f32),
        shape((3, 256), f32),
        shape((1, D), f32),
    )
    scratch = [
        pltpu.VMEM((T, D), f32),
        pltpu.VMEM((T, D), f32),
        pltpu.VMEM((3, 2 * H, 256), f32),
        pltpu.VMEM((2, H, 256), f32),
        pltpu.VMEM((T, 256), f32),
        pltpu.VMEM((T + 8, 256), f32),
        pltpu.VMEM((2, 2, H, D), f32),
        pltpu.VMEM((2, 2, 2, H, D), f32),
        *scatter_scratch(2 * w + EARLY, w + EARLY // 2),
        dma((2, 12)),
        dma((2, 12)),
        *SCATTER_SEMS,
        dma((7,)),
        dma((7,)),
        dma((1,)),
        dma((1,)),
    ]
    return call(middle_kernel, "middle", 5, args, outs, scratch, 36)


def end(*args):
    dm, act = args[0], args[8]
    T, D = dm.shape
    H = T // 8
    f32, shape, dma = jnp.float32, jax.ShapeDtypeStruct, pltpu.SemaphoreType.DMA
    w = act.shape[1] - EARLY
    outs = (
        shape((T, D), f32),
        shape((3, 32, 256), f32),
        shape((32, 256), f32),
        shape((32, w), f32),
        shape((8, 128), f32),
        shape((8, 128), f32),
        shape((3, 256), f32),
    )
    scratch = [
        pltpu.VMEM((2, H, D), f32),
        pltpu.VMEM((2, 2, H, D), f32),
        *scatter_scratch(w + 1792, w + 512),
        pltpu.VMEM((24, 128), f32),
        pltpu.VMEM((3, 24, 128), f32),
        pltpu.VMEM((4, 4, 24, 128), f32),
        dma((12,)),
        dma((12,)),
        *SCATTER_SEMS,
        dma((10,)),
        dma((10,)),
        pltpu.VMEM((4, 32, 256), f32),
        pltpu.VMEM((3, 32, 256), f32),
        dma((3,)),
        dma((3,)),
    ]
    return call(end_kernel, "end", 7, args, outs, scratch, 36)


def place(down_early, down_late, *arrays):
    n = len(arrays)
    early, late = down_early.shape[1], down_late.shape[1]

    def kernel(*refs):
        first, second, ins = refs[0], refs[1], refs[2 : n + 2]
        whole, outs, sems = refs[n + 2], refs[n + 3 : 2 * n + 3], refs[2 * n + 3]
        pairs = [
            (first, whole.at[:, pl.ds(0, early)]),
            (second, whole.at[:, pl.ds(early, late)]),
            *zip(ins, outs),
        ]
        copies = [pltpu.make_async_copy(a, b, sems.at[i]) for i, (a, b) in enumerate(pairs)]
        for copy in copies:
            copy.start()
        for copy in copies:
            copy.wait()

    anywhere = pl.BlockSpec(memory_space=pl.ANY)
    shapes = [jax.ShapeDtypeStruct((down_early.shape[0], early + late), jnp.float32)]
    shapes += [jax.ShapeDtypeStruct(a.shape, a.dtype) for a in arrays]
    return pl.pallas_call(
        kernel,
        out_shape=tuple(shapes),
        in_specs=[VMEM_SPEC] * (n + 2),
        out_specs=(anywhere,) * (n + 1),
        scratch_shapes=[pltpu.SemaphoreType.DMA((n + 2,))],
        compiler_params=pltpu.CompilerParams(vmem_limit_bytes=2 << 20),
        name="place",
    )(down_early, down_late, *arrays)


def from_behind(block, axis, distance):
    devices = range(lax.axis_size(axis))
    route = [(i - distance, i) for i in devices if i - distance in devices]
    return lax.ppermute(block, axis, route)


def rms_scale(values):
    return lax.rsqrt(jnp.mean(values * values, axis=-1, keepdims=True) + EPS)


def right_product(left, right):
    return lax.dot_general(
        left, right, (((1,), (1,)), ((), ())), preferred_element_type=jnp.float32
    )


def on_device(
    tokens,
    segment_ids,
    mix_gain,
    in_weight,
    conv_weight,
    out_weight,
    ffn_gain,
    gate_weight,
    up_weight,
    down_weight,
    cotangent,
):
    tok_rows = tokens.shape[0]
    first_row = lax.axis_index("seq") * tok_rows
    padded_ids = jnp.concatenate(
        [jnp.full((2,), -1, jnp.int32), segment_ids, jnp.full((2,), -2, jnp.int32)]
    )
    id_window = lax.dynamic_slice_in_dim(padded_ids, first_row, tok_rows + 4)
    near_ext = (id_window[2 : tok_rows + 4] == id_window[1 : tok_rows + 3]).astype(jnp.float32)
    far_ext = (id_window[2 : tok_rows + 4] == id_window[0 : tok_rows + 2]).astype(jnp.float32)
    near_own = near_ext[:tok_rows, None]
    far_own = far_ext[:tok_rows, None]
    inputs = tokens.astype(jnp.float32)
    mix_scale = rms_scale(inputs)
    mix_normed = (inputs * mix_scale * mix_gain).astype(jnp.bfloat16)
    projected = jnp.einsum("td,dkc->tkc", mix_normed, in_weight, preferred_element_type=jnp.float32)
    chan_b = projected[:, 0]
    chan_c = projected[:, 1]
    chan_x = projected[:, 2]
    mixed = chan_b * chan_x
    edge_rows = from_behind(mixed[tok_rows - 2 :], "seq", 1)
    extended = jnp.concatenate([edge_rows, mixed])
    kernel = conv_weight.astype(jnp.float32)
    prev_one = extended[1 : tok_rows + 1]
    prev_two = extended[0:tok_rows]
    conv_out = kernel[0] * mixed + kernel[1] * near_own * prev_one + kernel[2] * far_own * prev_two
    gated = (chan_c * conv_out).astype(jnp.bfloat16)
    ffn_normed, out_full, gated_rows, d_act, own_resid, own_cot, own_tok = front(
        gated, out_weight, tokens, cotangent, down_weight, ffn_gain[None]
    )
    gate = jnp.dot(ffn_normed, gate_weight, preferred_element_type=jnp.float32)
    upper = jnp.dot(ffn_normed, up_weight, preferred_element_type=jnp.float32)
    sigma = jax.nn.sigmoid(gate)
    act = (gate * sigma * upper).astype(jnp.bfloat16)
    d_gate = (d_act * upper * sigma * (1.0 + gate * (1.0 - sigma))).astype(jnp.bfloat16)
    d_up = (d_act * gate * sigma).astype(jnp.bfloat16)
    d_normed_part = right_product(d_gate, gate_weight) + right_product(d_up, up_weight)
    marks = jnp.stack(
        [near_own[:, 0], far_own[:, 0], near_ext[1 : tok_rows + 1], far_ext[2 : tok_rows + 2]], axis=1
    )
    d_resid, d_resid_low, grad_ffn_gain, result, gate_share, up_share, down_early, d_projected, d_mix_part, grad_conv, grad_mix_gain = middle(
        d_normed_part,
        own_resid,
        ffn_gain[None],
        own_cot,
        ffn_normed,
        d_gate,
        d_up,
        act,
        down_weight,
        out_full,
        projected.transpose(1, 0, 2),
        jnp.concatenate([jnp.zeros((6, mixed.shape[1]), jnp.float32), extended]),
        conv_out,
        marks,
        kernel,
        in_weight.transpose(1, 0, 2),
        tokens,
        cotangent,
    )
    grad_tokens, in_share, out_share, down_share, mix_total, ffn_total, conv_total = end(
        d_mix_part,
        own_tok,
        mix_gain[None],
        d_resid,
        mix_normed,
        d_projected,
        d_resid_low,
        gated_rows,
        act,
        cotangent,
        grad_mix_gain,
        grad_ffn_gain,
        grad_conv,
    )
    (
        down_share,
        result,
        grad_tokens,
        mix_total,
        in_share,
        conv_total,
        out_share,
        ffn_total,
        gate_share,
        up_share,
    ) = place(
        down_early,
        down_share,
        result,
        grad_tokens,
        mix_total,
        in_share,
        conv_total,
        out_share,
        ffn_total,
        gate_share,
        up_share,
    )
    return (
        result,
        grad_tokens,
        mix_total.reshape(-1),
        in_share.transpose(1, 0, 2),
        conv_total,
        out_share,
        ffn_total.reshape(-1),
        gate_share,
        up_share,
        down_share,
    )


def solution(mesh):
    placed = (
        P("seq", None),
        P(),
        P(),
        P(None, None, "head"),
        P(None, "head"),
        P(None, "head"),
        P(),
        P(None, "head"),
        P(None, "head"),
        P(None, "head"),
        P("seq", None),
    )
    return jax.shard_map(
        on_device,
        mesh=mesh,
        in_specs=placed,
        out_specs=(
            P("seq", None),
            P("seq", None),
            P(),
            P("seq", None, "head"),
            P(None, "head"),
            P("seq", "head"),
            P(),
            P("seq", "head"),
            P("seq", "head"),
            P("seq", "head"),
        ),
        check_vma=False,
    )
```

```python
import jax
import jax.numpy as jnp
from jax import lax
from jax.experimental import pallas as pl
from jax.experimental.pallas import tpu as pltpu
from jax.sharding import PartitionSpec as P

EPS = 1e-05
MESH = pl.DeviceIdType.MESH


def norm_back_rows(grad_normed, values, gain, extra):
    scale = lax.rsqrt(jnp.mean(values * values, axis=-1, keepdims=True) + EPS)
    weighted = grad_normed * gain
    inner = jnp.mean(weighted * values, axis=-1, keepdims=True)
    grad_values = extra + (scale * weighted - values * (scale * scale * scale) * inner)
    return grad_values, jnp.sum(grad_normed * values * scale, axis=0, keepdims=True)


class Comm:
    def __init__(self):
        seq = lax.axis_index("seq")
        self.me = lax.axis_index("head")
        self.core = lax.rem(seq, 2)
        self.z = lax.rem(lax.div(seq, 2), 4)
        self.x = lax.div(seq, 8)
        self.every = []
        self.steps = []

    def at_x(self, n):
        return {"seq": (ahead(self.x, n) * 4 + self.z) * 2 + self.core, "head": self.me}

    def at_z(self, n):
        return {"seq": (self.x * 4 + ahead(self.z, n)) * 2 + self.core, "head": self.me}

    def at_y(self, n):
        return {"seq": (self.x * 4 + self.z) * 2 + self.core, "head": ahead(self.me, n)}

    def twin(self, n=1):
        return {"seq": (self.x * 4 + self.z) * 2 + (1 - self.core), "head": self.me}

    def along(self, n):
        return {"seq": lax.rem((self.x * 4 + self.z) * 2 + self.core + n, 32), "head": self.me}

    def greet(self, devices):
        barrier = pltpu.get_barrier_semaphore()
        for device in devices:
            pl.semaphore_signal(barrier, inc=1, device_id=device, device_id_type=MESH)
        pl.semaphore_wait(barrier, len(devices))

    def send(self, src, dst, s_sem, r_sem, dev):
        copy = pltpu.make_async_remote_copy(
            src_ref=src, dst_ref=dst, send_sem=s_sem, recv_sem=r_sem, device_id=dev, device_id_type=MESH
        )
        copy.start()
        self.every.append(copy)
        return copy

    def when(self, time):
        def add(fn):
            self.steps.append((time, len(self.steps), fn))
            return fn

        return add

    def run(self):
        for _, _, fn in sorted(self.steps, key=lambda s: s[:2]):
            fn()
        for copy in self.every:
            copy.wait_send()


def ahead(k, n):
    return lax.rem(k + n, 4)


def add_up(dst, *srcs):
    n, r = dst.shape[:2]
    q = r // 8

    def body(i, carry):
        b, at = lax.div(i, q), pl.ds(pl.multiple_of(lax.rem(i, q) * 8, 8), 8)
        total = dst[b, at, :]
        for src in srcs:
            total = total + src[b, at, :]
        dst[b, at, :] = total
        return carry

    lax.fori_loop(0, n * q, body, 0)


def head_sum(cm, p, o, t, f, s_sem, r_sem, finish, times, closing, share=True):
    T = p.shape[0]
    C = T // 4
    H = C // 2
    R, L, O = ahead(cm.me, 1), ahead(cm.me, 3), ahead(cm.me, 2)
    me = cm.me
    c = {}

    def rows(k, half):
        return pl.ds(pl.multiple_of(k * C + half * H, H), H)

    def go(name, src, dst, i, n):
        c[name] = cm.send(src, dst, s_sem.at[i], r_sem.at[i], cm.at_y(n))

    @cm.when(times[0])
    def _():
        go("a0", p.at[rows(O, 0)], t.at[0], 0, 1)
        go("a1", p.at[rows(O, 1)], t.at[1], 1, 3)
        go("a2", p.at[rows(R, 1)], f.at[0, 1], 2, 1)
        go("a3", p.at[rows(L, 0)], f.at[1, 0], 3, 3)

    @cm.when(times[1])
    def _():
        c["a0"].wait_recv()
        t[0] = p[rows(R, 0), :] + t[0]
        go("a4", t.at[0], f.at[0, 0], 4, 1)
        c["a1"].wait_recv()
        t[1] = p[rows(L, 1), :] + t[1]
        go("a5", t.at[1], f.at[1, 1], 5, 3)

    @cm.when(times[2])
    def _():
        c["a3"].wait_recv()
        c["a4"].wait_recv()
        first = finish(0, p[rows(me, 0), :] + f[0, 0] + f[1, 0])
        if not share:
            c["a2"].wait_recv()
            c["a5"].wait_recv()
            o[0:H, :] = first
            o[H:C, :] = finish(1, p[rows(me, 1), :] + f[0, 1] + f[1, 1])
            return
        o[rows(me, 0), :] = first
        go("b0", o.at[rows(me, 0)], o.at[rows(me, 0)], 6, 1)
        c["a2"].wait_recv()
        c["a5"].wait_recv()
        o[rows(me, 1), :] = finish(1, p[rows(me, 1), :] + f[0, 1] + f[1, 1])
        go("c1", o.at[rows(me, 1)], o.at[rows(me, 1)], 9, 3)
        go("b1", o.at[rows(me, 1)], o.at[rows(me, 1)], 7, 1)
        go("c0", o.at[rows(me, 0)], o.at[rows(me, 0)], 8, 3)

    if not share:
        return

    @cm.when(times[3])
    def _():
        c["b0"].wait_recv()
        go("d0", o.at[rows(L, 0)], o.at[rows(L, 0)], 10, 1)
        c["c1"].wait_recv()
        go("d1", o.at[rows(R, 1)], o.at[rows(R, 1)], 11, 3)

    @cm.when(900)
    def _():
        for name in ("b1", "c0", "d0", "d1"):
            c[name].wait_recv()
        closing()


def scatter_ring(cm, chunk, t, f, s_sem, r_sem, base, to, times, done):
    c = {}

    def go(name, src, dst, i, n):
        c[name] = cm.send(src, dst, s_sem.at[base + i], r_sem.at[base + i], to(n))

    @cm.when(times[0])
    def _():
        go("a0", chunk(2, 0), t.at[0], 0, 1)
        go("a1", chunk(2, 1), t.at[1], 1, 3)

    @cm.when(times[1])
    def _():
        go("a2", chunk(1, 1), f.at[0, 1], 2, 1)

    @cm.when(times[2])
    def _():
        go("a3", chunk(3, 0), f.at[1, 0], 3, 3)

    @cm.when(times[3])
    def _():
        c["a0"].wait_recv()
        add_up(t.at[0], chunk(1, 0))
        go("a4", t.at[0], f.at[0, 0], 4, 1)
        c["a1"].wait_recv()
        add_up(t.at[1], chunk(3, 1))
        go("a5", t.at[1], f.at[1, 1], 5, 3)

    @cm.when(times[4])
    def _():
        c["a3"].wait_recv()
        c["a4"].wait_recv()
        add_up(chunk(0, 0), f.at[0, 0], f.at[1, 0])
        c["a2"].wait_recv()
        c["a5"].wait_recv()
        add_up(chunk(0, 1), f.at[0, 1], f.at[1, 1])
        done()


def grad_scatter(cm, products_a, products_b, G, RC, wa, bufs, sems, times, done_a, done_b):
    tA, tB, fA, fB, t2A, t2B, f2A, f2B = bufs
    cs, cr, as_, ar, bs, br = sems
    W = G.shape[-1]
    quarter = products_a[0][0].shape[1] // 4
    got = {}

    cols_a, cols_b = pl.ds(0, wa), pl.ds(wa, W - wa)

    def block(part, turn):
        k = ahead(cm.x, turn)
        products, cols, i = (products_a, cols_a, turn) if part == "a" else (products_b, cols_b, 4 + turn)
        for left, rights, at in products:
            right = jnp.concatenate([r[...] for r in rights], axis=1)
            w = right.shape[1]
            lhs = left[:, pl.ds(pl.multiple_of(k * quarter, quarter), quarter)]
            value = lax.dot_general(
                lhs, right, (((0,), (0,)), ((), ())), preferred_element_type=jnp.float32
            )
            G[k, :, :, :, pl.ds(at, w)] = value.reshape(4, 2, 32, w)
        got[part, turn] = cm.send(
            G.at[k, :, 1 - cm.core, :, cols], RC.at[k, :, :, cols], cs.at[i], cr.at[i], cm.twin()
        )

    def settle(part, turn):
        k = ahead(cm.x, turn)
        cols = cols_a if part == "a" else cols_b
        got[part, turn].wait_recv()
        add_up(G.at[k, :, cm.core, :, cols], RC.at[k, :, :, cols])

    for part in "ba":
        for i, turn in enumerate((2, 1, 3, 0)):
            cm.when(times["block_" + part][i])(lambda part=part, turn=turn: block(part, turn))
            cm.when(times["settle_" + part][i])(lambda part=part, turn=turn: settle(part, turn))

    core = cm.core

    def a1(turn, half):
        return G.at[ahead(cm.x, turn), pl.ds(half * 2, 2), core, :, cols_a]

    def b1(turn, half):
        return G.at[pl.ds(half * 2, 2), ahead(cm.z, turn), core, :, cols_b]

    def a2(turn, half):
        return G.at[cm.x, pl.ds(ahead(cm.z, turn), 1), core, pl.ds(half * 16, 16), cols_a]

    def b2(turn, half):
        return G.at[pl.ds(ahead(cm.x, turn), 1), cm.z, core, pl.ds(half * 16, 16), cols_b]

    nothing = lambda: None
    scatter_ring(cm, a1, tA, fA, as_, ar, 0, cm.at_x, times["A"], nothing)
    scatter_ring(cm, b1, tB, fB, bs, br, 0, cm.at_z, times["B"], nothing)
    scatter_ring(cm, a2, t2A, f2A, as_, ar, 6, cm.at_z, times["A2"], done_a)
    scatter_ring(cm, b2, t2B, f2B, bs, br, 6, cm.at_x, times["B2"], done_b)


def small_sums(cm, small, sm, sr, s_sem, r_sem, times, done):
    axes = [(cm.at_z, cm.z), (cm.at_x, cm.x), (cm.at_y, cm.me)]
    first = {}

    @cm.when(times[0])
    def _():
        first["c"] = cm.send(small, sr.at[3, 0], s_sem.at[9], r_sem.at[9], cm.twin())

    @cm.when(times[1])
    def _():
        first["c"].wait_recv()
        sm[0] = small[...] + sr[3, 0]

    for a, (to, here) in enumerate(axes):
        copies = []

        def begin(a=a, to=to, here=here, copies=copies):
            sr[a, here] = sm[a]
            for n in (1, 2, 3):
                i = a * 3 + n - 1
                copies.append(cm.send(sm.at[a], sr.at[a, here], s_sem.at[i], r_sem.at[i], to(n)))

        def end(a=a, copies=copies):
            for copy in copies:
                copy.wait_recv()
            total = (sr[a, 0] + sr[a, 1]) + (sr[a, 2] + sr[a, 3])
            if a < 2:
                sm[a + 1] = total
            else:
                done(total[0:16], sm[2][16:24])

        cm.when(times[1] + 0.01)(begin) if a == 0 else cm.when(times[1 + a] + 0.01)(begin)
        cm.when(times[2 + a])(end)


def greet_all(cm, more):
    cm.greet([axis(n) for n in (1, 2, 3) for axis in (cm.at_x, cm.at_z, cm.at_y)] + [cm.twin()] + more)


def front_kernel(
    gated, ow, tokens, cot, down, gain, o_normed, o_full, o_own, o_dact, o_resid, o_cot, o_tok, resid, GF, WF, ys, yr, ws, wr
):
    cm = Comm()
    x, z, c, me = cm.x, cm.z, cm.core, cm.me
    R, L, O = ahead(me, 1), ahead(me, 3), ahead(me, 2)
    cm.greet([cm.at_x(1), cm.at_x(3), cm.at_z(1), cm.at_z(3), cm.at_y(1), cm.at_y(2), cm.at_y(3), cm.twin()])
    T = gated.shape[0]
    N = T // 2
    piece = ((x * 4 + z) * 2 + c) * 32
    h = {}

    def weight(name, ref, i, dev):
        h[name] = cm.send(ref, ref, ws.at[i], wr.at[i], dev)

    def gate(name, ref, i, n):
        h[name] = cm.send(ref, ref, ys.at[i], yr.at[i], cm.at_y(n))

    low, high = pl.ds(0, 2), pl.ds(2, 2)
    WF[x, z, c, me] = ow[pl.ds(pl.multiple_of(piece, 32), 32), :].astype(jnp.float32)
    for n in (1, 2, 3):
        weight(("y", n), WF.at[x, z, c, me], n - 1, cm.at_y(n))
    GF[me] = gated[...].astype(jnp.float32)
    first, second = pl.ds(0, N), pl.ds(N, N)
    gate("r0", GF.at[me, first], 0, 1)
    gate("l1", GF.at[me, second], 1, 3)
    gate("r1", GF.at[me, second], 2, 1)
    gate("l0", GF.at[me, first], 3, 3)
    for n in (1, 2, 3):
        h["y", n].wait_recv()
    weight("ax1", WF.at[x, z, c, low], 3, cm.at_x(1))
    weight("ax3", WF.at[x, z, c, low], 4, cm.at_x(3))
    weight("bz1", WF.at[x, z, c, high], 5, cm.at_z(1))
    weight("bz3", WF.at[x, z, c, high], 6, cm.at_z(3))
    resid[...] = tokens[...].astype(jnp.float32) + lax.dot_general(
        gated[...], ow[...], (((1,), (1,)), ((), ())), preferred_element_type=jnp.float32
    )
    mine = pl.ds(pl.multiple_of(me * (T // 4), T // 4), T // 4)
    o_cot[...] = cot[mine, :]
    o_tok[...] = tokens[mine, :]
    xl, xr, zl, zr = ahead(x, 3), ahead(x, 1), ahead(z, 3), ahead(z, 1)
    h["ax1"].wait_recv()
    weight("ax1f", WF.at[xl, z, c, 0], 7, cm.at_x(1))
    h["ax3"].wait_recv()
    weight("ax3f", WF.at[xr, z, c, 1], 8, cm.at_x(3))
    h["bz1"].wait_recv()
    weight("bz1f", WF.at[x, zl, c, 2], 9, cm.at_z(1))
    h["bz3"].wait_recv()
    weight("bz3f", WF.at[x, zr, c, 3], 10, cm.at_z(3))
    h["ax1f"].wait_recv()
    h["ax3f"].wait_recv()
    weight("az1", WF.at[:, z, c, low], 11, cm.at_z(1))
    weight("az3", WF.at[:, z, c, low], 12, cm.at_z(3))
    h["bz1f"].wait_recv()
    h["bz3f"].wait_recv()
    weight("bx1", WF.at[x, :, c, high], 13, cm.at_x(1))
    weight("bx3", WF.at[x, :, c, high], 14, cm.at_x(3))
    o_dact[...] = jnp.dot(cot[...], down[...], preferred_element_type=jnp.float32)
    h["r0"].wait_recv()
    gate("r0f", GF.at[L, first], 4, 1)
    h["l1"].wait_recv()
    gate("l1f", GF.at[R, second], 5, 3)
    h["az1"].wait_recv()
    weight("az1f", WF.at[:, zl, c, 0], 15, cm.at_z(1))
    h["az3"].wait_recv()
    weight("az3f", WF.at[:, zr, c, 1], 16, cm.at_z(3))
    h["bx1"].wait_recv()
    weight("bx1f", WF.at[xl, :, c, 2], 17, cm.at_x(1))
    h["bx3"].wait_recv()
    weight("bx3f", WF.at[xr, :, c, 3], 18, cm.at_x(3))
    for name in ("az1f", "az3f", "bx1f", "bx3f"):
        h[name].wait_recv()
    weight("twin", WF.at[:, :, c], 19, cm.twin())
    h["r1"].wait_recv()
    h["l0"].wait_recv()
    h["twin"].wait_recv()
    for k in range(4):
        o_full[k] = WF[:, :, :, k].reshape(1024, 256).astype(jnp.bfloat16)

    def add(k):
        low_gated = GF[k].astype(jnp.bfloat16)
        resid[...] += lax.dot_general(
            low_gated, o_full[k], (((1,), (1,)), ((), ())), preferred_element_type=jnp.float32
        )

    add(L)
    add(R)
    h["r0f"].wait_recv()
    h["l1f"].wait_recv()
    add(O)
    for k in range(4):
        o_own[:, 256 * k : 256 * (k + 1)] = GF[k, mine, :].astype(jnp.bfloat16)
    o_resid[...] = resid[mine, :]

    def body(i, carry):
        rows = pl.ds(pl.multiple_of(i * 32, 32), 32)
        values = resid[rows, :]
        scale = lax.rsqrt(jnp.mean(values * values, axis=-1, keepdims=True) + EPS)
        o_normed[rows, :] = (values * scale * gain[...]).astype(jnp.bfloat16)
        return carry

    lax.fori_loop(0, T // 32, body, 0)
    cm.run()


EARLY = 256


def middle_kernel(*refs):
    (dn, own_resid, gain, own_cot, normed, d_gate, d_up, act, down, ow) = refs[:10]
    (proj, mixed, conv_out, marks, taps, in_w, toks, cot) = refs[10:18]
    (o_dres, o_dlow, o_gain, o_res, o_gate, o_up, o_down, o_dproj, o_dm, o_taps, o_mix) = refs[18:29]
    (rp, full, turned, relay, dgated, DC, yt, yf, G, RC) = refs[29:39]
    bufs, (ys, yr), sems, (xs, xr), (hs, hr) = refs[39:47], refs[47:49], refs[49:55], refs[55:57], refs[57:]
    H = own_resid.shape[0] // 2
    T = 8 * H
    cm = Comm()
    greet_all(cm, [cm.along(1), cm.along(31)])

    def finish_dres(half, total):
        mine = pl.ds(half * H, H)
        rows, gains = norm_back_rows(
            total, own_resid[mine, :], gain[...], own_cot[mine, :].astype(jnp.float32)
        )
        o_gain[...] = gains if half == 0 else o_gain[...] + gains
        return rows

    def finish_result(half, total):
        return total + own_resid[pl.ds(half * H, H), :]

    def rounded():
        o_res[...] = full[...].astype(jnp.bfloat16)

    @cm.when(6.1)
    def _():
        rp[...] = lax.dot_general(
            act[...], down[...], (((1,), (1,)), ((), ())), preferred_element_type=jnp.float32
        )

    head_sum(cm, dn, o_dres, yt.at[0], yf.at[0], ys.at[0], yr.at[0], finish_dres, (0, 6, 18, 0), lambda: None, False)
    head_sum(cm, rp, full, yt.at[1], yf.at[1], ys.at[1], yr.at[1], finish_result, (6.2, 25, 44, 56), rounded)

    C = 2 * H
    R, L = ahead(cm.me, 1), ahead(cm.me, 3)
    c = {}

    def rows(k, half=None):
        if half is None:
            return pl.ds(pl.multiple_of(k * C, C), C)
        return pl.ds(pl.multiple_of(k * C + half * H, H), H)

    def go(name, src, dst, i, n):
        c[name] = cm.send(src, dst, xs.at[i], xr.at[i], cm.at_y(n))

    @cm.when(18.1)
    def _():
        low = o_dres[...].astype(jnp.bfloat16)
        o_dlow[...] = low
        for turn in (2, 1, 3):
            turned[turn - 1] = jnp.dot(low, ow[ahead(cm.me, turn)], preferred_element_type=jnp.float32)
            if turn == 2:
                go("e0", turned.at[1, pl.ds(0, H)], relay.at[0], 0, 1)
                go("e1", turned.at[1, pl.ds(H, H)], relay.at[1], 1, 3)
            else:
                go(("d", turn), turned.at[turn - 1], dgated.at[rows(cm.me)], 1 + turn, turn)
        dgated[rows(cm.me), :] = jnp.dot(low, ow[cm.me], preferred_element_type=jnp.float32)

    @cm.when(32)
    def _():
        c["e0"].wait_recv()
        go("f0", relay.at[0], dgated.at[rows(L, 0)], 5, 1)
        c["e1"].wait_recv()
        go("f1", relay.at[1], dgated.at[rows(R, 1)], 6, 3)

    N = 64

    @cm.when(38)
    def _():
        for name in (("d", 1), ("d", 3), "f0", "f1"):
            c[name].wait_recv()
        for i in range(T // N):
            at = pl.ds(i * N, N)
            dg = dgated[at, :]
            o_dproj[1, at, :] = (dg * conv_out[at, :]).astype(jnp.bfloat16)
            DC[at, :] = dg * proj[1, at, :]
        c["halo"] = cm.send(DC.at[pl.ds(0, 8)], DC.at[pl.ds(T, 8)], hs.at[0], hr.at[0], cm.along(31))

    @cm.when(41)
    def _():
        c["halo"].wait_recv()
        w0, w1, w2 = taps[0:1, :], taps[1:2, :], taps[2:3, :]
        sums = [jnp.zeros((1, 256), jnp.float32)] * 3
        for i in range(T // N):
            at = pl.ds(i * N, N)
            near, far = marks[at, 0:1], marks[at, 1:2]
            near_next, far_next = marks[at, 2:3], marks[at, 3:4]
            dc = DC[at, :]
            d_mixed = w0 * dc + w1 * near_next * DC[pl.ds(i * N + 1, N), :] + w2 * far_next * DC[pl.ds(i * N + 2, N), :]
            o_dproj[0, at, :] = (d_mixed * proj[2, at, :]).astype(jnp.bfloat16)
            o_dproj[2, at, :] = (d_mixed * proj[0, at, :]).astype(jnp.bfloat16)
            terms = (
                dc * mixed[pl.ds(i * N + 8, N), :],
                dc * near * mixed[pl.ds(i * N + 7, N), :],
                dc * far * mixed[pl.ds(i * N + 6, N), :],
            )
            sums = [s + jnp.sum(t, axis=0, keepdims=True) for s, t in zip(sums, terms)]
        for k in range(3):
            o_taps[k : k + 1, :] = sums[k]

    @cm.when(45)
    def _():
        right = jnp.concatenate([in_w[0], in_w[1], in_w[2]], axis=1)
        for i in range(4):
            at = pl.ds(i * C, C)
            left = jnp.concatenate([o_dproj[0, at, :], o_dproj[1, at, :], o_dproj[2, at, :]], axis=1)
            o_dm[at, :] = lax.dot_general(
                left, right, (((1,), (1,)), ((), ())), preferred_element_type=jnp.float32
            )

        def body(i, total):
            at = pl.ds(pl.multiple_of(i * 32, 32), 32)
            values = toks[at, :].astype(jnp.float32)
            scale = lax.rsqrt(jnp.mean(values * values, axis=-1, keepdims=True) + EPS)
            return total + jnp.sum(o_dm[at, :] * values * scale, axis=0, keepdims=True)

        o_mix[...] = lax.fori_loop(0, T // 32, body, jnp.zeros(o_mix.shape, jnp.float32))

    w = act.shape[1]
    e = EARLY // 2

    def done_a():
        rows = G[cm.x, cm.z, cm.core, :, pl.ds(0, w + e)]
        o_gate[...] = rows[:, :w]
        o_down[:, pl.ds(0, e)] = rows[:, w:]

    def done_b():
        rows = G[cm.x, cm.z, cm.core, :, pl.ds(w + e, w + e)]
        o_down[:, pl.ds(e, e)] = rows[:, :e]
        o_up[...] = rows[:, e:]

    times = {
        "block_b": (0.1, 0.2, 0.3, 0.4),
        "block_a": (0.5, 1.3, 2.1, 2.9),
        "settle_b": (1.21, 1.22, 1.23, 1.24),
        "settle_a": (2, 2.8, 3.6, 4.4),
        "B": (1.25, 1.26, 1.27, 11.5, 27),
        "A": (2.01, 2.81, 3.61, 12.5, 28.5),
        "B2": (27.1, 27.2, 27.3, 32.1, 35),
        "A2": (28.6, 28.7, 28.8, 31, 34.5),
    }
    products_a = [(normed, [d_gate], 0), (cot, [act.at[:, pl.ds(0, e)]], w)]
    products_b = [(cot, [act.at[:, pl.ds(e, e)]], w + e), (normed, [d_up], w + EARLY)]
    grad_scatter(cm, products_a, products_b, G, RC, w + e, bufs, sems, times, done_a, done_b)
    cm.run()


def end_kernel(*refs):
    (dm, toks, gain, d_res, normed, d_proj, d_low, gated, act, cot, mix_gains, ffn_gains, taps) = refs[:13]
    (o_tok, o_in, o_out, o_down, o_mix, o_ffn, o_conv) = refs[13:20]
    (yt, yf, G, RC) = refs[20:24]
    bufs = refs[24:32]
    small, sm, sr = refs[32:35]
    ys, yr = refs[35:37]
    sems = refs[37:43]
    ss, sr_sem = refs[43:45]
    mine, theirs, hs, hr = refs[45:]
    H = toks.shape[0] // 2
    cm = Comm()
    greet_all(cm, [])

    def finish_tokens(half, total):
        at = pl.ds(half * H, H)
        return norm_back_rows(total, toks[at, :].astype(jnp.float32), gain[...], d_res[at, :])[0]

    @cm.when(-1)
    def _():
        small[16:24, :] = jnp.zeros((8, 128), jnp.float32)
        for k in range(8):
            small[k : k + 1, :] = mix_gains[:, 128 * k : 128 * (k + 1)]
            small[8 + k : 9 + k, :] = ffn_gains[:, 128 * k : 128 * (k + 1)]
        for k in range(3):
            for h in range(2):
                small[16 + 2 * k + h : 17 + 2 * k + h, :] = taps[k : k + 1, 128 * h : 128 * (h + 1)]

    head_sum(cm, dm, o_tok, yt, yf, ys, yr, finish_tokens, (0, 8, 19.5, 27), lambda: None)

    w = act.shape[1] - EARLY
    wa = w + 512
    heads = []

    def done_a():
        rows = G[cm.x, cm.z, cm.core, :, pl.ds(0, wa)]
        o_down[...] = rows[:, :w]
        o_in[0] = rows[:, w : w + 256]
        o_in[1] = rows[:, w + 256 :]

    def done_b():
        rows = G[cm.x, cm.z, cm.core, :, pl.ds(wa, 1280)]
        o_in[2] = rows[:, :256]
        for k in range(4):
            mine[k] = rows[:, 256 + 256 * k : 512 + 256 * k]
        for n in (1, 2, 3):
            heads.append(
                cm.send(mine.at[ahead(cm.me, n)], theirs.at[n - 1], hs.at[n - 1], hr.at[n - 1], cm.at_y(n))
            )

    @cm.when(950)
    def _():
        for copy in heads:
            copy.wait_recv()
        o_out[...] = (mine[cm.me] + theirs[0]) + (theirs[1] + theirs[2])

    times = {
        "block_b": (0.1, 0.2, 0.3, 0.4),
        "block_a": (0.5, 1.5, 2.6, 3.6),
        "settle_b": (1.41, 1.42, 1.43, 1.44),
        "settle_a": (2.5, 3.5, 4.5, 5.5),
        "B": (1.45, 1.46, 1.47, 13, 29),
        "A": (2.51, 3.51, 4.51, 15, 33),
        "B2": (29.1, 29.2, 29.3, 34.5, 40),
        "A2": (33.1, 33.2, 33.3, 36.5, 40.5),
    }
    products_a = [
        (cot, [act.at[:, pl.ds(EARLY, w)]], 0),
        (normed, [d_proj.at[0], d_proj.at[1]], w),
    ]
    products_b = [(normed, [d_proj.at[2]], wa), (d_low, [gated], wa + 256)]
    grad_scatter(cm, products_a, products_b, G, RC, wa, bufs, sems, times, done_a, done_b)

    def small_done(gains, rest):
        o_mix[...] = gains[0:8]
        o_ffn[...] = gains[8:16]
        for k in range(3):
            for h in range(2):
                o_conv[k : k + 1, pl.ds(128 * h, 128)] = rest[2 * k + h : 2 * k + h + 1]

    small_sums(cm, small, sm, sr, ss, sr_sem, (-0.9, 1.443, 8.1, 19.6, 38), small_done)
    cm.run()


VMEM_SPEC = pl.BlockSpec(memory_space=pltpu.VMEM)


def call(kernel, name, cid, args, outs, scratch, limit):
    return pl.pallas_call(
        kernel,
        out_shape=outs,
        in_specs=[VMEM_SPEC] * len(args),
        out_specs=(VMEM_SPEC,) * len(outs),
        scratch_shapes=scratch,
        compiler_params=pltpu.CompilerParams(
            collective_id=cid, has_side_effects=True, vmem_limit_bytes=limit << 20
        ),
        cost_estimate=pl.CostEstimate(flops=1, bytes_accessed=1, transcendentals=0),
        name=name,
    )(*args)


def scatter_scratch(W, wa):
    f32 = jnp.float32
    wb = W - wa
    return [
        pltpu.VMEM((4, 4, 2, 32, W), f32),
        pltpu.VMEM((4, 4, 32, W), f32),
        pltpu.VMEM((2, 2, 32, wa), f32),
        pltpu.VMEM((2, 2, 32, wb), f32),
        pltpu.VMEM((2, 2, 2, 32, wa), f32),
        pltpu.VMEM((2, 2, 2, 32, wb), f32),
        pltpu.VMEM((2, 1, 16, wa), f32),
        pltpu.VMEM((2, 1, 16, wb), f32),
        pltpu.VMEM((2, 2, 1, 16, wa), f32),
        pltpu.VMEM((2, 2, 1, 16, wb), f32),
    ]


SCATTER_SEMS = [pltpu.SemaphoreType.DMA((n,)) for n in (8, 8, 12, 12, 12, 12)]


def front(gated, ow, tokens, cot, down, gain):
    T, D = tokens.shape
    f32, bf16, shape, dma = jnp.float32, jnp.bfloat16, jax.ShapeDtypeStruct, pltpu.SemaphoreType.DMA
    outs = (
        shape((T, D), bf16),
        shape((4, *ow.shape), bf16),
        shape((T // 4, D), bf16),
        shape((T, down.shape[1]), f32),
        shape((T // 4, D), f32),
        shape((T // 4, D), bf16),
        shape((T // 4, D), bf16),
    )
    scratch = [
        pltpu.VMEM((T, D), f32),
        pltpu.VMEM((4, *gated.shape), f32),
        pltpu.VMEM((4, 4, 2, 4, 32, ow.shape[1]), f32),
        dma((6,)),
        dma((6,)),
        dma((20,)),
        dma((20,)),
    ]
    return call(front_kernel, "front", 3, (gated, ow, tokens, cot, down, gain), outs, scratch, 24)


def middle(*args):
    dn, act, proj = args[0], args[7], args[10]
    T, D = dn.shape
    H = T // 8
    f32, bf16, shape, dma = jnp.float32, jnp.bfloat16, jax.ShapeDtypeStruct, pltpu.SemaphoreType.DMA
    w = act.shape[1]
    outs = (
        shape((T // 4, D), f32),
        shape((T // 4, D), bf16),
        shape((1, D), f32),
        shape((T, D), bf16),
        shape((32, w), f32),
        shape((32, w), f32),
        shape((32, EARLY), f32),
        shape(proj.shape, bf16),
        shape((T, D), f32),
        shape((3, 256), f32),
        shape((1, D), f32),
    )
    scratch = [
        pltpu.VMEM((T, D), f32),
        pltpu.VMEM((T, D), f32),
        pltpu.VMEM((3, 2 * H, 256), f32),
        pltpu.VMEM((2, H, 256), f32),
        pltpu.VMEM((T, 256), f32),
        pltpu.VMEM((T + 8, 256), f32),
        pltpu.VMEM((2, 2, H, D), f32),
        pltpu.VMEM((2, 2, 2, H, D), f32),
        *scatter_scratch(2 * w + EARLY, w + EARLY // 2),
        dma((2, 12)),
        dma((2, 12)),
        *SCATTER_SEMS,
        dma((7,)),
        dma((7,)),
        dma((1,)),
        dma((1,)),
    ]
    return call(middle_kernel, "middle", 5, args, outs, scratch, 36)


def end(*args):
    dm, act = args[0], args[8]
    T, D = dm.shape
    H = T // 8
    f32, shape, dma = jnp.float32, jax.ShapeDtypeStruct, pltpu.SemaphoreType.DMA
    w = act.shape[1] - EARLY
    outs = (
        shape((T, D), f32),
        shape((3, 32, 256), f32),
        shape((32, 256), f32),
        shape((32, w), f32),
        shape((8, 128), f32),
        shape((8, 128), f32),
        shape((3, 256), f32),
    )
    scratch = [
        pltpu.VMEM((2, H, D), f32),
        pltpu.VMEM((2, 2, H, D), f32),
        *scatter_scratch(w + 1792, w + 512),
        pltpu.VMEM((24, 128), f32),
        pltpu.VMEM((3, 24, 128), f32),
        pltpu.VMEM((4, 4, 24, 128), f32),
        dma((12,)),
        dma((12,)),
        *SCATTER_SEMS,
        dma((10,)),
        dma((10,)),
        pltpu.VMEM((4, 32, 256), f32),
        pltpu.VMEM((3, 32, 256), f32),
        dma((3,)),
        dma((3,)),
    ]
    return call(end_kernel, "end", 7, args, outs, scratch, 36)


def place(down_early, down_late, *arrays):
    n = len(arrays)
    early, late = down_early.shape[1], down_late.shape[1]

    def kernel(*refs):
        first, second, ins = refs[0], refs[1], refs[2 : n + 2]
        whole, outs, sems = refs[n + 2], refs[n + 3 : 2 * n + 3], refs[2 * n + 3]
        pairs = [
            (first, whole.at[:, pl.ds(0, early)]),
            (second, whole.at[:, pl.ds(early, late)]),
            *zip(ins, outs),
        ]
        copies = [pltpu.make_async_copy(a, b, sems.at[i]) for i, (a, b) in enumerate(pairs)]
        for copy in copies:
            copy.start()
        for copy in copies:
            copy.wait()

    anywhere = pl.BlockSpec(memory_space=pl.ANY)
    shapes = [jax.ShapeDtypeStruct((down_early.shape[0], early + late), jnp.float32)]
    shapes += [jax.ShapeDtypeStruct(a.shape, a.dtype) for a in arrays]
    return pl.pallas_call(
        kernel,
        out_shape=tuple(shapes),
        in_specs=[VMEM_SPEC] * (n + 2),
        out_specs=(anywhere,) * (n + 1),
        scratch_shapes=[pltpu.SemaphoreType.DMA((n + 2,))],
        compiler_params=pltpu.CompilerParams(vmem_limit_bytes=2 << 20),
        name="place",
    )(down_early, down_late, *arrays)


def from_behind(block, axis, distance):
    devices = range(lax.axis_size(axis))
    route = [(i - distance, i) for i in devices if i - distance in devices]
    return lax.ppermute(block, axis, route)


def rms_scale(values):
    return lax.rsqrt(jnp.mean(values * values, axis=-1, keepdims=True) + EPS)


def right_product(left, right):
    return lax.dot_general(
        left, right, (((1,), (1,)), ((), ())), preferred_element_type=jnp.float32
    )


def on_device(
    tokens,
    segment_ids,
    mix_gain,
    in_weight,
    conv_weight,
    out_weight,
    ffn_gain,
    gate_weight,
    up_weight,
    down_weight,
    cotangent,
):
    tok_rows = tokens.shape[0]
    first_row = lax.axis_index("seq") * tok_rows
    padded_ids = jnp.concatenate(
        [jnp.full((2,), -1, jnp.int32), segment_ids, jnp.full((2,), -2, jnp.int32)]
    )
    id_window = lax.dynamic_slice_in_dim(padded_ids, first_row, tok_rows + 4)
    near_ext = (id_window[2 : tok_rows + 4] == id_window[1 : tok_rows + 3]).astype(jnp.float32)
    far_ext = (id_window[2 : tok_rows + 4] == id_window[0 : tok_rows + 2]).astype(jnp.float32)
    near_own = near_ext[:tok_rows, None]
    far_own = far_ext[:tok_rows, None]
    inputs = tokens.astype(jnp.float32)
    mix_scale = rms_scale(inputs)
    mix_normed = (inputs * mix_scale * mix_gain).astype(jnp.bfloat16)
    projected = jnp.einsum("td,dkc->tkc", mix_normed, in_weight, preferred_element_type=jnp.float32)
    chan_b = projected[:, 0]
    chan_c = projected[:, 1]
    chan_x = projected[:, 2]
    mixed = chan_b * chan_x
    edge_rows = from_behind(mixed[tok_rows - 2 :], "seq", 1)
    extended = jnp.concatenate([edge_rows, mixed])
    kernel = conv_weight.astype(jnp.float32)
    prev_one = extended[1 : tok_rows + 1]
    prev_two = extended[0:tok_rows]
    conv_out = kernel[0] * mixed + kernel[1] * near_own * prev_one + kernel[2] * far_own * prev_two
    gated = (chan_c * conv_out).astype(jnp.bfloat16)
    ffn_normed, out_full, gated_rows, d_act, own_resid, own_cot, own_tok = front(
        gated, out_weight, tokens, cotangent, down_weight, ffn_gain[None]
    )
    gate = jnp.dot(ffn_normed, gate_weight, preferred_element_type=jnp.float32)
    upper = jnp.dot(ffn_normed, up_weight, preferred_element_type=jnp.float32)
    sigma = jax.nn.sigmoid(gate)
    act = (gate * sigma * upper).astype(jnp.bfloat16)
    d_gate = (d_act * upper * sigma * (1.0 + gate * (1.0 - sigma))).astype(jnp.bfloat16)
    d_up = (d_act * gate * sigma).astype(jnp.bfloat16)
    d_normed_part = right_product(d_gate, gate_weight) + right_product(d_up, up_weight)
    marks = jnp.stack(
        [near_own[:, 0], far_own[:, 0], near_ext[1 : tok_rows + 1], far_ext[2 : tok_rows + 2]], axis=1
    )
    d_resid, d_resid_low, grad_ffn_gain, result, gate_share, up_share, down_early, d_projected, d_mix_part, grad_conv, grad_mix_gain = middle(
        d_normed_part,
        own_resid,
        ffn_gain[None],
        own_cot,
        ffn_normed,
        d_gate,
        d_up,
        act,
        down_weight,
        out_full,
        projected.transpose(1, 0, 2),
        jnp.concatenate([jnp.zeros((6, mixed.shape[1]), jnp.float32), extended]),
        conv_out,
        marks,
        kernel,
        in_weight.transpose(1, 0, 2),
        tokens,
        cotangent,
    )
    grad_tokens, in_share, out_share, down_share, mix_total, ffn_total, conv_total = end(
        d_mix_part,
        own_tok,
        mix_gain[None],
        d_resid,
        mix_normed,
        d_projected,
        d_resid_low,
        gated_rows,
        act,
        cotangent,
        grad_mix_gain,
        grad_ffn_gain,
        grad_conv,
    )
    (
        down_share,
        result,
        grad_tokens,
        mix_total,
        in_share,
        conv_total,
        out_share,
        ffn_total,
        gate_share,
        up_share,
    ) = place(
        down_early,
        down_share,
        result,
        grad_tokens,
        mix_total,
        in_share,
        conv_total,
        out_share,
        ffn_total,
        gate_share,
        up_share,
    )
    return (
        result,
        grad_tokens,
        mix_total.reshape(-1),
        in_share.transpose(1, 0, 2),
        conv_total,
        out_share,
        ffn_total.reshape(-1),
        gate_share,
        up_share,
        down_share,
    )


def solution(mesh):
    placed = (
        P("seq", None),
        P(),
        P(),
        P(None, None, "head"),
        P(None, "head"),
        P(None, "head"),
        P(),
        P(None, "head"),
        P(None, "head"),
        P(None, "head"),
        P("seq", None),
    )
    return jax.shard_map(
        on_device,
        mesh=mesh,
        in_specs=placed,
        out_specs=(
            P("seq", None),
            P("seq", None),
            P(),
            P("seq", None, "head"),
            P(None, "head"),
            P("seq", "head"),
            P(),
            P("seq", "head"),
            P("seq", "head"),
            P("seq", "head"),
        ),
        check_vma=False,
    )
```

```python
import jax
import jax.numpy as jnp
from jax import lax
from jax.experimental import pallas as pl
from jax.experimental.pallas import tpu as pltpu
from jax.sharding import PartitionSpec as P

EPS = 1e-05
MESH = pl.DeviceIdType.MESH


def norm_back_rows(grad_normed, values, gain, extra):
    scale = lax.rsqrt(jnp.mean(values * values, axis=-1, keepdims=True) + EPS)
    weighted = grad_normed * gain
    inner = jnp.mean(weighted * values, axis=-1, keepdims=True)
    grad_values = extra + (scale * weighted - values * (scale * scale * scale) * inner)
    return grad_values, jnp.sum(grad_normed * values * scale, axis=0, keepdims=True)


class Comm:
    def __init__(self):
        seq = lax.axis_index("seq")
        self.me = lax.axis_index("head")
        self.core = lax.rem(seq, 2)
        self.z = lax.rem(lax.div(seq, 2), 4)
        self.x = lax.div(seq, 8)
        self.every = []
        self.steps = []

    def at_x(self, n):
        return {"seq": (ahead(self.x, n) * 4 + self.z) * 2 + self.core, "head": self.me}

    def at_z(self, n):
        return {"seq": (self.x * 4 + ahead(self.z, n)) * 2 + self.core, "head": self.me}

    def at_y(self, n):
        return {"seq": (self.x * 4 + self.z) * 2 + self.core, "head": ahead(self.me, n)}

    def twin(self, n=1):
        return {"seq": (self.x * 4 + self.z) * 2 + (1 - self.core), "head": self.me}

    def along(self, n):
        return {"seq": lax.rem((self.x * 4 + self.z) * 2 + self.core + n, 32), "head": self.me}

    def greet(self, devices):
        barrier = pltpu.get_barrier_semaphore()
        for device in devices:
            pl.semaphore_signal(barrier, inc=1, device_id=device, device_id_type=MESH)
        pl.semaphore_wait(barrier, len(devices))

    def send(self, src, dst, s_sem, r_sem, dev):
        copy = pltpu.make_async_remote_copy(
            src_ref=src, dst_ref=dst, send_sem=s_sem, recv_sem=r_sem, device_id=dev, device_id_type=MESH
        )
        copy.start()
        self.every.append(copy)
        return copy

    def when(self, time):
        def add(fn):
            self.steps.append((time, len(self.steps), fn))
            return fn

        return add

    def run(self):
        for _, _, fn in sorted(self.steps, key=lambda s: s[:2]):
            fn()
        for copy in self.every:
            copy.wait_send()


def ahead(k, n):
    return lax.rem(k + n, 4)


def add_up(dst, *srcs):
    n, r = dst.shape[:2]
    q = r // 8

    def body(i, carry):
        b, at = lax.div(i, q), pl.ds(pl.multiple_of(lax.rem(i, q) * 8, 8), 8)
        total = dst[b, at, :]
        for src in srcs:
            total = total + src[b, at, :]
        dst[b, at, :] = total
        return carry

    lax.fori_loop(0, n * q, body, 0)


def head_sum(cm, p, o, t, f, s_sem, r_sem, finish, times, closing, share=True):
    T = p.shape[0]
    C = T // 4
    H = C // 2
    R, L, O = ahead(cm.me, 1), ahead(cm.me, 3), ahead(cm.me, 2)
    me = cm.me
    c = {}

    def rows(k, half):
        return pl.ds(pl.multiple_of(k * C + half * H, H), H)

    def go(name, src, dst, i, n):
        c[name] = cm.send(src, dst, s_sem.at[i], r_sem.at[i], cm.at_y(n))

    @cm.when(times[0])
    def _():
        go("a0", p.at[rows(O, 0)], t.at[0], 0, 1)
        go("a1", p.at[rows(O, 1)], t.at[1], 1, 3)
        go("a2", p.at[rows(R, 1)], f.at[0, 1], 2, 1)
        go("a3", p.at[rows(L, 0)], f.at[1, 0], 3, 3)

    @cm.when(times[1])
    def _():
        c["a0"].wait_recv()
        t[0] = p[rows(R, 0), :] + t[0]
        go("a4", t.at[0], f.at[0, 0], 4, 1)
        c["a1"].wait_recv()
        t[1] = p[rows(L, 1), :] + t[1]
        go("a5", t.at[1], f.at[1, 1], 5, 3)

    @cm.when(times[2])
    def _():
        c["a3"].wait_recv()
        c["a4"].wait_recv()
        first = finish(0, p[rows(me, 0), :] + f[0, 0] + f[1, 0])
        if not share:
            c["a2"].wait_recv()
            c["a5"].wait_recv()
            o[0:H, :] = first
            o[H:C, :] = finish(1, p[rows(me, 1), :] + f[0, 1] + f[1, 1])
            return
        o[rows(me, 0), :] = first
        go("b0", o.at[rows(me, 0)], o.at[rows(me, 0)], 6, 1)
        c["a2"].wait_recv()
        c["a5"].wait_recv()
        o[rows(me, 1), :] = finish(1, p[rows(me, 1), :] + f[0, 1] + f[1, 1])
        go("c1", o.at[rows(me, 1)], o.at[rows(me, 1)], 9, 3)
        go("b1", o.at[rows(me, 1)], o.at[rows(me, 1)], 7, 1)
        go("c0", o.at[rows(me, 0)], o.at[rows(me, 0)], 8, 3)

    if not share:
        return

    @cm.when(times[3])
    def _():
        c["b0"].wait_recv()
        go("d0", o.at[rows(L, 0)], o.at[rows(L, 0)], 10, 1)
        c["c1"].wait_recv()
        go("d1", o.at[rows(R, 1)], o.at[rows(R, 1)], 11, 3)

    @cm.when(900)
    def _():
        for name in ("b1", "c0", "d0", "d1"):
            c[name].wait_recv()
        closing()


def scatter_ring(cm, chunk, t, f, s_sem, r_sem, base, to, times, done):
    c = {}

    def go(name, src, dst, i, n):
        c[name] = cm.send(src, dst, s_sem.at[base + i], r_sem.at[base + i], to(n))

    @cm.when(times[0])
    def _():
        go("a0", chunk(2, 0), t.at[0], 0, 1)
        go("a1", chunk(2, 1), t.at[1], 1, 3)

    @cm.when(times[1])
    def _():
        go("a2", chunk(1, 1), f.at[0, 1], 2, 1)

    @cm.when(times[2])
    def _():
        go("a3", chunk(3, 0), f.at[1, 0], 3, 3)

    @cm.when(times[3])
    def _():
        c["a0"].wait_recv()
        add_up(t.at[0], chunk(1, 0))
        go("a4", t.at[0], f.at[0, 0], 4, 1)
        c["a1"].wait_recv()
        add_up(t.at[1], chunk(3, 1))
        go("a5", t.at[1], f.at[1, 1], 5, 3)

    @cm.when(times[4])
    def _():
        c["a3"].wait_recv()
        c["a4"].wait_recv()
        add_up(chunk(0, 0), f.at[0, 0], f.at[1, 0])
        c["a2"].wait_recv()
        c["a5"].wait_recv()
        add_up(chunk(0, 1), f.at[0, 1], f.at[1, 1])
        done()


def grad_scatter(cm, products_a, products_b, G, RC, wa, bufs, sems, times, done_a, done_b):
    tA, tB, fA, fB, t2A, t2B, f2A, f2B = bufs
    cs, cr, as_, ar, bs, br = sems
    W = G.shape[-1]
    quarter = products_a[0][0].shape[1] // 4
    got = {}

    cols_a, cols_b = pl.ds(0, wa), pl.ds(wa, W - wa)

    def block(part, turn):
        k = ahead(cm.x, turn)
        products, cols, i = (products_a, cols_a, turn) if part == "a" else (products_b, cols_b, 4 + turn)
        for left, rights, at in products:
            right = jnp.concatenate([r[...] for r in rights], axis=1)
            w = right.shape[1]
            lhs = left[:, pl.ds(pl.multiple_of(k * quarter, quarter), quarter)]
            value = lax.dot_general(
                lhs, right, (((0,), (0,)), ((), ())), preferred_element_type=jnp.float32
            )
            G[k, :, :, :, pl.ds(at, w)] = value.reshape(4, 2, 32, w)
        got[part, turn] = cm.send(
            G.at[k, :, 1 - cm.core, :, cols], RC.at[k, :, :, cols], cs.at[i], cr.at[i], cm.twin()
        )

    def settle(part, turn):
        k = ahead(cm.x, turn)
        cols = cols_a if part == "a" else cols_b
        got[part, turn].wait_recv()
        add_up(G.at[k, :, cm.core, :, cols], RC.at[k, :, :, cols])

    for part in "ba":
        for i, turn in enumerate((2, 1, 3, 0)):
            cm.when(times["block_" + part][i])(lambda part=part, turn=turn: block(part, turn))
            cm.when(times["settle_" + part][i])(lambda part=part, turn=turn: settle(part, turn))

    core = cm.core

    def a1(turn, half):
        return G.at[ahead(cm.x, turn), pl.ds(half * 2, 2), core, :, cols_a]

    def b1(turn, half):
        return G.at[pl.ds(half * 2, 2), ahead(cm.z, turn), core, :, cols_b]

    def a2(turn, half):
        return G.at[cm.x, pl.ds(ahead(cm.z, turn), 1), core, pl.ds(half * 16, 16), cols_a]

    def b2(turn, half):
        return G.at[pl.ds(ahead(cm.x, turn), 1), cm.z, core, pl.ds(half * 16, 16), cols_b]

    nothing = lambda: None
    scatter_ring(cm, a1, tA, fA, as_, ar, 0, cm.at_x, times["A"], nothing)
    scatter_ring(cm, b1, tB, fB, bs, br, 0, cm.at_z, times["B"], nothing)
    scatter_ring(cm, a2, t2A, f2A, as_, ar, 6, cm.at_z, times["A2"], done_a)
    scatter_ring(cm, b2, t2B, f2B, bs, br, 6, cm.at_x, times["B2"], done_b)


def small_sums(cm, small, sm, sr, s_sem, r_sem, times, done):
    axes = [(cm.at_z, cm.z), (cm.at_x, cm.x), (cm.at_y, cm.me)]
    first = {}

    @cm.when(times[0])
    def _():
        first["c"] = cm.send(small, sr.at[3, 0], s_sem.at[9], r_sem.at[9], cm.twin())

    @cm.when(times[1])
    def _():
        first["c"].wait_recv()
        sm[0] = small[...] + sr[3, 0]

    for a, (to, here) in enumerate(axes):
        copies = []

        def begin(a=a, to=to, here=here, copies=copies):
            sr[a, here] = sm[a]
            for n in (1, 2, 3):
                i = a * 3 + n - 1
                copies.append(cm.send(sm.at[a], sr.at[a, here], s_sem.at[i], r_sem.at[i], to(n)))

        def end(a=a, copies=copies):
            for copy in copies:
                copy.wait_recv()
            total = (sr[a, 0] + sr[a, 1]) + (sr[a, 2] + sr[a, 3])
            if a < 2:
                sm[a + 1] = total
            else:
                done(total[0:16], sm[2][16:24])

        cm.when(times[1] + 0.01)(begin) if a == 0 else cm.when(times[1 + a] + 0.01)(begin)
        cm.when(times[2 + a])(end)


def greet_all(cm, more):
    cm.greet([axis(n) for n in (1, 2, 3) for axis in (cm.at_x, cm.at_z, cm.at_y)] + [cm.twin()] + more)


def front_kernel(
    gated, ow, tokens, cot, down, gain, o_normed, o_full, o_own, o_dact, o_resid, o_cot, o_tok, resid, GF, WF, ys, yr, ws, wr
):
    cm = Comm()
    x, z, c, me = cm.x, cm.z, cm.core, cm.me
    R, L, O = ahead(me, 1), ahead(me, 3), ahead(me, 2)
    cm.greet([cm.at_x(1), cm.at_x(3), cm.at_z(1), cm.at_z(3), cm.at_y(1), cm.at_y(2), cm.at_y(3), cm.twin()])
    T = gated.shape[0]
    N = T // 2
    piece = ((x * 4 + z) * 2 + c) * 32
    h = {}

    def weight(name, ref, i, dev):
        h[name] = cm.send(ref, ref, ws.at[i], wr.at[i], dev)

    def gate(name, ref, i, n):
        h[name] = cm.send(ref, ref, ys.at[i], yr.at[i], cm.at_y(n))

    low, high = pl.ds(0, 2), pl.ds(2, 2)
    WF[x, z, c, me] = ow[pl.ds(pl.multiple_of(piece, 32), 32), :].astype(jnp.float32)
    for n in (1, 2, 3):
        weight(("y", n), WF.at[x, z, c, me], n - 1, cm.at_y(n))
    GF[me] = gated[...].astype(jnp.float32)
    first, second = pl.ds(0, N), pl.ds(N, N)
    gate("r0", GF.at[me, first], 0, 1)
    gate("l1", GF.at[me, second], 1, 3)
    gate("r1", GF.at[me, second], 2, 1)
    gate("l0", GF.at[me, first], 3, 3)
    for n in (1, 2, 3):
        h["y", n].wait_recv()
    weight("ax1", WF.at[x, z, c, low], 3, cm.at_x(1))
    weight("ax3", WF.at[x, z, c, low], 4, cm.at_x(3))
    weight("bz1", WF.at[x, z, c, high], 5, cm.at_z(1))
    weight("bz3", WF.at[x, z, c, high], 6, cm.at_z(3))
    resid[...] = tokens[...].astype(jnp.float32) + lax.dot_general(
        gated[...], ow[...], (((1,), (1,)), ((), ())), preferred_element_type=jnp.float32
    )
    mine = pl.ds(pl.multiple_of(me * (T // 4), T // 4), T // 4)
    o_cot[...] = cot[mine, :]
    o_tok[...] = tokens[mine, :]
    xl, xr, zl, zr = ahead(x, 3), ahead(x, 1), ahead(z, 3), ahead(z, 1)
    h["ax1"].wait_recv()
    weight("ax1f", WF.at[xl, z, c, 0], 7, cm.at_x(1))
    h["ax3"].wait_recv()
    weight("ax3f", WF.at[xr, z, c, 1], 8, cm.at_x(3))
    h["bz1"].wait_recv()
    weight("bz1f", WF.at[x, zl, c, 2], 9, cm.at_z(1))
    h["bz3"].wait_recv()
    weight("bz3f", WF.at[x, zr, c, 3], 10, cm.at_z(3))
    h["ax1f"].wait_recv()
    h["ax3f"].wait_recv()
    weight("az1", WF.at[:, z, c, low], 11, cm.at_z(1))
    weight("az3", WF.at[:, z, c, low], 12, cm.at_z(3))
    h["bz1f"].wait_recv()
    h["bz3f"].wait_recv()
    weight("bx1", WF.at[x, :, c, high], 13, cm.at_x(1))
    weight("bx3", WF.at[x, :, c, high], 14, cm.at_x(3))
    zo, xo = ahead(z, 2), ahead(x, 2)
    weight("t0", WF.at[:, z, c, low], 19, cm.twin())
    weight("t1", WF.at[x, :, c, high], 20, cm.twin())
    o_dact[...] = jnp.dot(cot[...], down[...], preferred_element_type=jnp.float32)
    h["r0"].wait_recv()
    gate("r0f", GF.at[L, first], 4, 1)
    h["l1"].wait_recv()
    gate("l1f", GF.at[R, second], 5, 3)
    h["az1"].wait_recv()
    weight("az1f", WF.at[:, zl, c, 0], 15, cm.at_z(1))
    weight("t2", WF.at[:, zl, c, low], 21, cm.twin())
    h["az3"].wait_recv()
    weight("az3f", WF.at[:, zr, c, 1], 16, cm.at_z(3))
    weight("t3", WF.at[:, zr, c, low], 22, cm.twin())
    h["bx1"].wait_recv()
    weight("bx1f", WF.at[xl, :, c, 2], 17, cm.at_x(1))
    weight("t4", WF.at[xl, :, c, high], 23, cm.twin())
    h["bx3"].wait_recv()
    weight("bx3f", WF.at[xr, :, c, 3], 18, cm.at_x(3))
    weight("t5", WF.at[xr, :, c, high], 24, cm.twin())
    h["az1f"].wait_recv()
    h["az3f"].wait_recv()
    weight("t6", WF.at[:, zo, c, low], 25, cm.twin())
    h["bx1f"].wait_recv()
    h["bx3f"].wait_recv()
    weight("t7", WF.at[xo, :, c, high], 26, cm.twin())
    h["r1"].wait_recv()
    h["l0"].wait_recv()
    for k in range(8):
        h[f"t{k}"].wait_recv()
    for k in range(4):
        o_full[k] = WF[:, :, :, k].reshape(1024, 256).astype(jnp.bfloat16)

    def add(*heads):
        resid[...] += lax.dot_general(
            jnp.concatenate([GF[k].astype(jnp.bfloat16) for k in heads], axis=1),
            jnp.concatenate([o_full[k] for k in heads], axis=1),
            (((1,), (1,)), ((), ())),
            preferred_element_type=jnp.float32,
        )

    add(L, R)
    h["r0f"].wait_recv()
    h["l1f"].wait_recv()
    add(O)
    for k in range(4):
        o_own[:, 256 * k : 256 * (k + 1)] = GF[k, mine, :].astype(jnp.bfloat16)
    o_resid[...] = resid[mine, :]

    def body(i, carry):
        rows = pl.ds(pl.multiple_of(i * 32, 32), 32)
        values = resid[rows, :]
        scale = lax.rsqrt(jnp.mean(values * values, axis=-1, keepdims=True) + EPS)
        o_normed[rows, :] = (values * scale * gain[...]).astype(jnp.bfloat16)
        return carry

    lax.fori_loop(0, T // 32, body, 0)
    cm.run()


EARLY = 256


def middle_kernel(*refs):
    (dn, own_resid, gain, own_cot, normed, d_gate, d_up, act, down, ow) = refs[:10]
    (proj, mixed, conv_out, marks, taps, in_w, toks, cot) = refs[10:18]
    (o_dres, o_dlow, o_gain, o_res, o_gate, o_up, o_down, o_dproj, o_dm, o_taps, o_mix) = refs[18:29]
    (rp, full, turned, relay, dgated, DC, yt, yf, G, RC) = refs[29:39]
    bufs, (ys, yr), sems, (xs, xr), (hs, hr) = refs[39:47], refs[47:49], refs[49:55], refs[55:57], refs[57:]
    H = own_resid.shape[0] // 2
    T = 8 * H
    cm = Comm()
    greet_all(cm, [cm.along(1), cm.along(31)])

    def finish_dres(half, total):
        mine = pl.ds(half * H, H)
        rows, gains = norm_back_rows(
            total, own_resid[mine, :], gain[...], own_cot[mine, :].astype(jnp.float32)
        )
        o_gain[...] = gains if half == 0 else o_gain[...] + gains
        return rows

    def finish_result(half, total):
        return total + own_resid[pl.ds(half * H, H), :]

    def rounded():
        o_res[...] = full[...].astype(jnp.bfloat16)

    @cm.when(6.1)
    def _():
        rp[...] = lax.dot_general(
            act[...], down[...], (((1,), (1,)), ((), ())), preferred_element_type=jnp.float32
        )

    head_sum(cm, dn, o_dres, yt.at[0], yf.at[0], ys.at[0], yr.at[0], finish_dres, (0, 6, 18, 0), lambda: None, False)
    head_sum(cm, rp, full, yt.at[1], yf.at[1], ys.at[1], yr.at[1], finish_result, (6.2, 25, 44, 56), rounded)

    C = 2 * H
    R, L = ahead(cm.me, 1), ahead(cm.me, 3)
    c = {}

    def rows(k, half=None):
        if half is None:
            return pl.ds(pl.multiple_of(k * C, C), C)
        return pl.ds(pl.multiple_of(k * C + half * H, H), H)

    def go(name, src, dst, i, n):
        c[name] = cm.send(src, dst, xs.at[i], xr.at[i], cm.at_y(n))

    @cm.when(18.1)
    def _():
        low = o_dres[...].astype(jnp.bfloat16)
        o_dlow[...] = low
        for turn in (2, 1, 3):
            turned[turn - 1] = jnp.dot(low, ow[ahead(cm.me, turn)], preferred_element_type=jnp.float32)
            if turn == 2:
                go("e0", turned.at[1, pl.ds(0, H)], relay.at[0], 0, 1)
                go("e1", turned.at[1, pl.ds(H, H)], relay.at[1], 1, 3)
            else:
                go(("d", turn), turned.at[turn - 1], dgated.at[rows(cm.me)], 1 + turn, turn)
        dgated[rows(cm.me), :] = jnp.dot(low, ow[cm.me], preferred_element_type=jnp.float32)

    @cm.when(32)
    def _():
        c["e0"].wait_recv()
        go("f0", relay.at[0], dgated.at[rows(L, 0)], 5, 1)
        c["e1"].wait_recv()
        go("f1", relay.at[1], dgated.at[rows(R, 1)], 6, 3)

    N = 64

    @cm.when(38)
    def _():
        for name in (("d", 1), ("d", 3), "f0", "f1"):
            c[name].wait_recv()
        for i in range(T // N):
            at = pl.ds(i * N, N)
            dg = dgated[at, :]
            o_dproj[1, at, :] = (dg * conv_out[at, :]).astype(jnp.bfloat16)
            DC[at, :] = dg * proj[1, at, :]
        c["halo"] = cm.send(DC.at[pl.ds(0, 8)], DC.at[pl.ds(T, 8)], hs.at[0], hr.at[0], cm.along(31))

    @cm.when(41)
    def _():
        c["halo"].wait_recv()
        w0, w1, w2 = taps[0:1, :], taps[1:2, :], taps[2:3, :]
        sums = [jnp.zeros((1, 256), jnp.float32)] * 3
        for i in range(T // N):
            at = pl.ds(i * N, N)
            near, far = marks[at, 0:1], marks[at, 1:2]
            near_next, far_next = marks[at, 2:3], marks[at, 3:4]
            dc = DC[at, :]
            d_mixed = w0 * dc + w1 * near_next * DC[pl.ds(i * N + 1, N), :] + w2 * far_next * DC[pl.ds(i * N + 2, N), :]
            o_dproj[0, at, :] = (d_mixed * proj[2, at, :]).astype(jnp.bfloat16)
            o_dproj[2, at, :] = (d_mixed * proj[0, at, :]).astype(jnp.bfloat16)
            terms = (
                dc * mixed[pl.ds(i * N + 8, N), :],
                dc * near * mixed[pl.ds(i * N + 7, N), :],
                dc * far * mixed[pl.ds(i * N + 6, N), :],
            )
            sums = [s + jnp.sum(t, axis=0, keepdims=True) for s, t in zip(sums, terms)]
        for k in range(3):
            o_taps[k : k + 1, :] = sums[k]

    @cm.when(45)
    def _():
        right = jnp.concatenate([in_w[0], in_w[1], in_w[2]], axis=1)
        for i in range(4):
            at = pl.ds(i * C, C)
            left = jnp.concatenate([o_dproj[0, at, :], o_dproj[1, at, :], o_dproj[2, at, :]], axis=1)
            o_dm[at, :] = lax.dot_general(
                left, right, (((1,), (1,)), ((), ())), preferred_element_type=jnp.float32
            )

        def body(i, total):
            at = pl.ds(pl.multiple_of(i * 32, 32), 32)
            values = toks[at, :].astype(jnp.float32)
            scale = lax.rsqrt(jnp.mean(values * values, axis=-1, keepdims=True) + EPS)
            return total + jnp.sum(o_dm[at, :] * values * scale, axis=0, keepdims=True)

        o_mix[...] = lax.fori_loop(0, T // 32, body, jnp.zeros(o_mix.shape, jnp.float32))

    w = act.shape[1]
    e = EARLY // 2

    def done_a():
        rows = G[cm.x, cm.z, cm.core, :, pl.ds(0, w + e)]
        o_gate[...] = rows[:, :w]
        o_down[:, pl.ds(0, e)] = rows[:, w:]

    def done_b():
        rows = G[cm.x, cm.z, cm.core, :, pl.ds(w + e, w + e)]
        o_down[:, pl.ds(e, e)] = rows[:, :e]
        o_up[...] = rows[:, e:]

    times = {
        "block_b": (0.1, 0.2, 0.3, 0.4),
        "block_a": (0.5, 1.3, 2.1, 2.9),
        "settle_b": (1.21, 1.22, 1.23, 1.24),
        "settle_a": (2, 2.8, 3.6, 4.4),
        "B": (1.25, 1.26, 1.27, 11.5, 27),
        "A": (2.01, 2.81, 3.61, 12.5, 28.5),
        "B2": (27.1, 27.2, 27.3, 32.1, 35),
        "A2": (28.6, 28.7, 28.8, 31, 34.5),
    }
    products_a = [(normed, [d_gate], 0), (cot, [act.at[:, pl.ds(0, e)]], w)]
    products_b = [(cot, [act.at[:, pl.ds(e, e)]], w + e), (normed, [d_up], w + EARLY)]
    grad_scatter(cm, products_a, products_b, G, RC, w + e, bufs, sems, times, done_a, done_b)
    cm.run()


def end_kernel(*refs):
    (dm, toks, gain, d_res, normed, d_proj, d_low, gated, act, cot, mix_gains, ffn_gains, taps) = refs[:13]
    (o_tok, o_in, o_out, o_down, o_mix, o_ffn, o_conv) = refs[13:20]
    (yt, yf, G, RC) = refs[20:24]
    bufs = refs[24:32]
    small, sm, sr = refs[32:35]
    ys, yr = refs[35:37]
    sems = refs[37:43]
    ss, sr_sem = refs[43:45]
    mine, theirs, hs, hr = refs[45:]
    H = toks.shape[0] // 2
    cm = Comm()
    greet_all(cm, [])

    def finish_tokens(half, total):
        at = pl.ds(half * H, H)
        return norm_back_rows(total, toks[at, :].astype(jnp.float32), gain[...], d_res[at, :])[0]

    @cm.when(-1)
    def _():
        small[16:24, :] = jnp.zeros((8, 128), jnp.float32)
        for k in range(8):
            small[k : k + 1, :] = mix_gains[:, 128 * k : 128 * (k + 1)]
            small[8 + k : 9 + k, :] = ffn_gains[:, 128 * k : 128 * (k + 1)]
        for k in range(3):
            for h in range(2):
                small[16 + 2 * k + h : 17 + 2 * k + h, :] = taps[k : k + 1, 128 * h : 128 * (h + 1)]

    head_sum(cm, dm, o_tok, yt, yf, ys, yr, finish_tokens, (0, 8, 19.5, 27), lambda: None)

    w = act.shape[1] - EARLY
    wa = w + 512
    heads = []

    def done_a():
        rows = G[cm.x, cm.z, cm.core, :, pl.ds(0, wa)]
        o_down[...] = rows[:, :w]
        o_in[0] = rows[:, w : w + 256]
        o_in[1] = rows[:, w + 256 :]

    def done_b():
        rows = G[cm.x, cm.z, cm.core, :, pl.ds(wa, 1280)]
        o_in[2] = rows[:, :256]
        for k in range(4):
            mine[k] = rows[:, 256 + 256 * k : 512 + 256 * k]
        for n in (1, 2, 3):
            heads.append(
                cm.send(mine.at[ahead(cm.me, n)], theirs.at[n - 1], hs.at[n - 1], hr.at[n - 1], cm.at_y(n))
            )

    @cm.when(950)
    def _():
        for copy in heads:
            copy.wait_recv()
        o_out[...] = (mine[cm.me] + theirs[0]) + (theirs[1] + theirs[2])

    times = {
        "block_b": (0.1, 0.2, 0.3, 0.4),
        "block_a": (0.5, 1.5, 2.6, 3.6),
        "settle_b": (1.41, 1.42, 1.43, 1.44),
        "settle_a": (2.5, 3.5, 4.5, 5.5),
        "B": (1.45, 1.46, 1.47, 13, 29),
        "A": (2.51, 3.51, 4.51, 15, 33),
        "B2": (29.1, 29.2, 29.3, 34.5, 40),
        "A2": (33.1, 33.2, 33.3, 36.5, 40.5),
    }
    products_a = [
        (cot, [act.at[:, pl.ds(EARLY, w)]], 0),
        (normed, [d_proj.at[0], d_proj.at[1]], w),
    ]
    products_b = [(normed, [d_proj.at[2]], wa), (d_low, [gated], wa + 256)]
    grad_scatter(cm, products_a, products_b, G, RC, wa, bufs, sems, times, done_a, done_b)

    def small_done(gains, rest):
        o_mix[...] = gains[0:8]
        o_ffn[...] = gains[8:16]
        for k in range(3):
            for h in range(2):
                o_conv[k : k + 1, pl.ds(128 * h, 128)] = rest[2 * k + h : 2 * k + h + 1]

    small_sums(cm, small, sm, sr, ss, sr_sem, (-0.9, 1.443, 8.1, 19.6, 38), small_done)
    cm.run()


VMEM_SPEC = pl.BlockSpec(memory_space=pltpu.VMEM)


def call(kernel, name, cid, args, outs, scratch, limit):
    return pl.pallas_call(
        kernel,
        out_shape=outs,
        in_specs=[VMEM_SPEC] * len(args),
        out_specs=(VMEM_SPEC,) * len(outs),
        scratch_shapes=scratch,
        compiler_params=pltpu.CompilerParams(
            collective_id=cid, has_side_effects=True, vmem_limit_bytes=limit << 20
        ),
        cost_estimate=pl.CostEstimate(flops=1, bytes_accessed=1, transcendentals=0),
        name=name,
    )(*args)


def scatter_scratch(W, wa):
    f32 = jnp.float32
    wb = W - wa
    return [
        pltpu.VMEM((4, 4, 2, 32, W), f32),
        pltpu.VMEM((4, 4, 32, W), f32),
        pltpu.VMEM((2, 2, 32, wa), f32),
        pltpu.VMEM((2, 2, 32, wb), f32),
        pltpu.VMEM((2, 2, 2, 32, wa), f32),
        pltpu.VMEM((2, 2, 2, 32, wb), f32),
        pltpu.VMEM((2, 1, 16, wa), f32),
        pltpu.VMEM((2, 1, 16, wb), f32),
        pltpu.VMEM((2, 2, 1, 16, wa), f32),
        pltpu.VMEM((2, 2, 1, 16, wb), f32),
    ]


SCATTER_SEMS = [pltpu.SemaphoreType.DMA((n,)) for n in (8, 8, 12, 12, 12, 12)]


def front(gated, ow, tokens, cot, down, gain):
    T, D = tokens.shape
    f32, bf16, shape, dma = jnp.float32, jnp.bfloat16, jax.ShapeDtypeStruct, pltpu.SemaphoreType.DMA
    outs = (
        shape((T, D), bf16),
        shape((4, *ow.shape), bf16),
        shape((T // 4, D), bf16),
        shape((T, down.shape[1]), f32),
        shape((T // 4, D), f32),
        shape((T // 4, D), bf16),
        shape((T // 4, D), bf16),
    )
    scratch = [
        pltpu.VMEM((T, D), f32),
        pltpu.VMEM((4, *gated.shape), f32),
        pltpu.VMEM((4, 4, 2, 4, 32, ow.shape[1]), f32),
        dma((6,)),
        dma((6,)),
        dma((27,)),
        dma((27,)),
    ]
    return call(front_kernel, "front", 3, (gated, ow, tokens, cot, down, gain), outs, scratch, 24)


def middle(*args):
    dn, act, proj = args[0], args[7], args[10]
    T, D = dn.shape
    H = T // 8
    f32, bf16, shape, dma = jnp.float32, jnp.bfloat16, jax.ShapeDtypeStruct, pltpu.SemaphoreType.DMA
    w = act.shape[1]
    outs = (
        shape((T // 4, D), f32),
        shape((T // 4, D), bf16),
        shape((1, D), f32),
        shape((T, D), bf16),
        shape((32, w), f32),
        shape((32, w), f32),
        shape((32, EARLY), f32),
        shape(proj.shape, bf16),
        shape((T, D), f32),
        shape((3, 256), f32),
        shape((1, D), f32),
    )
    scratch = [
        pltpu.VMEM((T, D), f32),
        pltpu.VMEM((T, D), f32),
        pltpu.VMEM((3, 2 * H, 256), f32),
        pltpu.VMEM((2, H, 256), f32),
        pltpu.VMEM((T, 256), f32),
        pltpu.VMEM((T + 8, 256), f32),
        pltpu.VMEM((2, 2, H, D), f32),
        pltpu.VMEM((2, 2, 2, H, D), f32),
        *scatter_scratch(2 * w + EARLY, w + EARLY // 2),
        dma((2, 12)),
        dma((2, 12)),
        *SCATTER_SEMS,
        dma((7,)),
        dma((7,)),
        dma((1,)),
        dma((1,)),
    ]
    return call(middle_kernel, "middle", 5, args, outs, scratch, 36)


def end(*args):
    dm, act = args[0], args[8]
    T, D = dm.shape
    H = T // 8
    f32, shape, dma = jnp.float32, jax.ShapeDtypeStruct, pltpu.SemaphoreType.DMA
    w = act.shape[1] - EARLY
    outs = (
        shape((T, D), f32),
        shape((3, 32, 256), f32),
        shape((32, 256), f32),
        shape((32, w), f32),
        shape((8, 128), f32),
        shape((8, 128), f32),
        shape((3, 256), f32),
    )
    scratch = [
        pltpu.VMEM((2, H, D), f32),
        pltpu.VMEM((2, 2, H, D), f32),
        *scatter_scratch(w + 1792, w + 512),
        pltpu.VMEM((24, 128), f32),
        pltpu.VMEM((3, 24, 128), f32),
        pltpu.VMEM((4, 4, 24, 128), f32),
        dma((12,)),
        dma((12,)),
        *SCATTER_SEMS,
        dma((10,)),
        dma((10,)),
        pltpu.VMEM((4, 32, 256), f32),
        pltpu.VMEM((3, 32, 256), f32),
        dma((3,)),
        dma((3,)),
    ]
    return call(end_kernel, "end", 7, args, outs, scratch, 36)


def place(down_early, down_late, *arrays):
    n = len(arrays)
    early, late = down_early.shape[1], down_late.shape[1]

    def kernel(*refs):
        first, second, ins = refs[0], refs[1], refs[2 : n + 2]
        whole, outs, sems = refs[n + 2], refs[n + 3 : 2 * n + 3], refs[2 * n + 3]
        pairs = [
            (first, whole.at[:, pl.ds(0, early)]),
            (second, whole.at[:, pl.ds(early, late)]),
            *zip(ins, outs),
        ]
        copies = [pltpu.make_async_copy(a, b, sems.at[i]) for i, (a, b) in enumerate(pairs)]
        for copy in copies:
            copy.start()
        for copy in copies:
            copy.wait()

    anywhere = pl.BlockSpec(memory_space=pl.ANY)
    shapes = [jax.ShapeDtypeStruct((down_early.shape[0], early + late), jnp.float32)]
    shapes += [jax.ShapeDtypeStruct(a.shape, a.dtype) for a in arrays]
    return pl.pallas_call(
        kernel,
        out_shape=tuple(shapes),
        in_specs=[VMEM_SPEC] * (n + 2),
        out_specs=(anywhere,) * (n + 1),
        scratch_shapes=[pltpu.SemaphoreType.DMA((n + 2,))],
        compiler_params=pltpu.CompilerParams(vmem_limit_bytes=2 << 20),
        name="place",
    )(down_early, down_late, *arrays)


def from_behind(block, axis, distance):
    devices = range(lax.axis_size(axis))
    route = [(i - distance, i) for i in devices if i - distance in devices]
    return lax.ppermute(block, axis, route)


def rms_scale(values):
    return lax.rsqrt(jnp.mean(values * values, axis=-1, keepdims=True) + EPS)


def right_product(left, right):
    return lax.dot_general(
        left, right, (((1,), (1,)), ((), ())), preferred_element_type=jnp.float32
    )


def on_device(
    tokens,
    segment_ids,
    mix_gain,
    in_weight,
    conv_weight,
    out_weight,
    ffn_gain,
    gate_weight,
    up_weight,
    down_weight,
    cotangent,
):
    tok_rows = tokens.shape[0]
    first_row = lax.axis_index("seq") * tok_rows
    padded_ids = jnp.concatenate(
        [jnp.full((2,), -1, jnp.int32), segment_ids, jnp.full((2,), -2, jnp.int32)]
    )
    id_window = lax.dynamic_slice_in_dim(padded_ids, first_row, tok_rows + 4)
    near_ext = (id_window[2 : tok_rows + 4] == id_window[1 : tok_rows + 3]).astype(jnp.float32)
    far_ext = (id_window[2 : tok_rows + 4] == id_window[0 : tok_rows + 2]).astype(jnp.float32)
    near_own = near_ext[:tok_rows, None]
    far_own = far_ext[:tok_rows, None]
    inputs = tokens.astype(jnp.float32)
    mix_scale = rms_scale(inputs)
    mix_normed = (inputs * mix_scale * mix_gain).astype(jnp.bfloat16)
    projected = jnp.einsum("td,dkc->tkc", mix_normed, in_weight, preferred_element_type=jnp.float32)
    chan_b = projected[:, 0]
    chan_c = projected[:, 1]
    chan_x = projected[:, 2]
    mixed = chan_b * chan_x
    edge_rows = from_behind(mixed[tok_rows - 2 :], "seq", 1)
    extended = jnp.concatenate([edge_rows, mixed])
    kernel = conv_weight.astype(jnp.float32)
    prev_one = extended[1 : tok_rows + 1]
    prev_two = extended[0:tok_rows]
    conv_out = kernel[0] * mixed + kernel[1] * near_own * prev_one + kernel[2] * far_own * prev_two
    gated = (chan_c * conv_out).astype(jnp.bfloat16)
    ffn_normed, out_full, gated_rows, d_act, own_resid, own_cot, own_tok = front(
        gated, out_weight, tokens, cotangent, down_weight, ffn_gain[None]
    )
    gate = jnp.dot(ffn_normed, gate_weight, preferred_element_type=jnp.float32)
    upper = jnp.dot(ffn_normed, up_weight, preferred_element_type=jnp.float32)
    sigma = jax.nn.sigmoid(gate)
    act = (gate * sigma * upper).astype(jnp.bfloat16)
    d_gate = (d_act * upper * sigma * (1.0 + gate * (1.0 - sigma))).astype(jnp.bfloat16)
    d_up = (d_act * gate * sigma).astype(jnp.bfloat16)
    d_normed_part = right_product(d_gate, gate_weight) + right_product(d_up, up_weight)
    marks = jnp.stack(
        [near_own[:, 0], far_own[:, 0], near_ext[1 : tok_rows + 1], far_ext[2 : tok_rows + 2]], axis=1
    )
    d_resid, d_resid_low, grad_ffn_gain, result, gate_share, up_share, down_early, d_projected, d_mix_part, grad_conv, grad_mix_gain = middle(
        d_normed_part,
        own_resid,
        ffn_gain[None],
        own_cot,
        ffn_normed,
        d_gate,
        d_up,
        act,
        down_weight,
        out_full,
        projected.transpose(1, 0, 2),
        jnp.concatenate([jnp.zeros((6, mixed.shape[1]), jnp.float32), extended]),
        conv_out,
        marks,
        kernel,
        in_weight.transpose(1, 0, 2),
        tokens,
        cotangent,
    )
    grad_tokens, in_share, out_share, down_share, mix_total, ffn_total, conv_total = end(
        d_mix_part,
        own_tok,
        mix_gain[None],
        d_resid,
        mix_normed,
        d_projected,
        d_resid_low,
        gated_rows,
        act,
        cotangent,
        grad_mix_gain,
        grad_ffn_gain,
        grad_conv,
    )
    (
        down_share,
        result,
        grad_tokens,
        mix_total,
        in_share,
        conv_total,
        out_share,
        ffn_total,
        gate_share,
        up_share,
    ) = place(
        down_early,
        down_share,
        result,
        grad_tokens,
        mix_total,
        in_share,
        conv_total,
        out_share,
        ffn_total,
        gate_share,
        up_share,
    )
    return (
        result,
        grad_tokens,
        mix_total.reshape(-1),
        in_share.transpose(1, 0, 2),
        conv_total,
        out_share,
        ffn_total.reshape(-1),
        gate_share,
        up_share,
        down_share,
    )


def solution(mesh):
    placed = (
        P("seq", None),
        P(),
        P(),
        P(None, None, "head"),
        P(None, "head"),
        P(None, "head"),
        P(),
        P(None, "head"),
        P(None, "head"),
        P(None, "head"),
        P("seq", None),
    )
    return jax.shard_map(
        on_device,
        mesh=mesh,
        in_specs=placed,
        out_specs=(
            P("seq", None),
            P("seq", None),
            P(),
            P("seq", None, "head"),
            P(None, "head"),
            P("seq", "head"),
            P(),
            P("seq", "head"),
            P("seq", "head"),
            P("seq", "head"),
        ),
        check_vma=False,
    )
```

```python
import jax
import jax.numpy as jnp
from jax import lax
from jax.experimental import pallas as pl
from jax.experimental.pallas import tpu as pltpu
from jax.sharding import PartitionSpec as P

EPS = 1e-05
MESH = pl.DeviceIdType.MESH


def norm_back_rows(grad_normed, values, gain, extra):
    scale = lax.rsqrt(jnp.mean(values * values, axis=-1, keepdims=True) + EPS)
    weighted = grad_normed * gain
    inner = jnp.mean(weighted * values, axis=-1, keepdims=True)
    grad_values = extra + (scale * weighted - values * (scale * scale * scale) * inner)
    return grad_values, jnp.sum(grad_normed * values * scale, axis=0, keepdims=True)


class Comm:
    def __init__(self):
        seq = lax.axis_index("seq")
        self.me = lax.axis_index("head")
        self.core = lax.rem(seq, 2)
        self.z = lax.rem(lax.div(seq, 2), 4)
        self.x = lax.div(seq, 8)
        self.every = []
        self.steps = []

    def at_x(self, n):
        return {"seq": (ahead(self.x, n) * 4 + self.z) * 2 + self.core, "head": self.me}

    def at_z(self, n):
        return {"seq": (self.x * 4 + ahead(self.z, n)) * 2 + self.core, "head": self.me}

    def at_y(self, n):
        return {"seq": (self.x * 4 + self.z) * 2 + self.core, "head": ahead(self.me, n)}

    def twin(self, n=1):
        return {"seq": (self.x * 4 + self.z) * 2 + (1 - self.core), "head": self.me}

    def along(self, n):
        return {"seq": lax.rem((self.x * 4 + self.z) * 2 + self.core + n, 32), "head": self.me}

    def greet(self, devices):
        barrier = pltpu.get_barrier_semaphore()
        for device in devices:
            pl.semaphore_signal(barrier, inc=1, device_id=device, device_id_type=MESH)
        pl.semaphore_wait(barrier, len(devices))

    def send(self, src, dst, s_sem, r_sem, dev):
        copy = pltpu.make_async_remote_copy(
            src_ref=src, dst_ref=dst, send_sem=s_sem, recv_sem=r_sem, device_id=dev, device_id_type=MESH
        )
        copy.start()
        self.every.append(copy)
        return copy

    def when(self, time):
        def add(fn):
            self.steps.append((time, len(self.steps), fn))
            return fn

        return add

    def run(self):
        for _, _, fn in sorted(self.steps, key=lambda s: s[:2]):
            fn()
        for copy in self.every:
            copy.wait_send()


def ahead(k, n):
    return lax.rem(k + n, 4)


def add_up(dst, *srcs):
    n, r = dst.shape[:2]
    q = r // 8

    def body(i, carry):
        b, at = lax.div(i, q), pl.ds(pl.multiple_of(lax.rem(i, q) * 8, 8), 8)
        total = dst[b, at, :]
        for src in srcs:
            total = total + src[b, at, :]
        dst[b, at, :] = total
        return carry

    lax.fori_loop(0, n * q, body, 0)


def head_sum(cm, p, o, t, f, s_sem, r_sem, finish, times, closing, share=True):
    T = p.shape[0]
    C = T // 4
    H = C // 2
    R, L, O = ahead(cm.me, 1), ahead(cm.me, 3), ahead(cm.me, 2)
    me = cm.me
    c = {}

    def rows(k, half):
        return pl.ds(pl.multiple_of(k * C + half * H, H), H)

    def go(name, src, dst, i, n):
        c[name] = cm.send(src, dst, s_sem.at[i], r_sem.at[i], cm.at_y(n))

    @cm.when(times[0])
    def _():
        go("a0", p.at[rows(O, 0)], t.at[0], 0, 1)
        go("a1", p.at[rows(O, 1)], t.at[1], 1, 3)
        go("a2", p.at[rows(R, 1)], f.at[0, 1], 2, 1)
        go("a3", p.at[rows(L, 0)], f.at[1, 0], 3, 3)

    @cm.when(times[1])
    def _():
        c["a0"].wait_recv()
        t[0] = p[rows(R, 0), :] + t[0]
        go("a4", t.at[0], f.at[0, 0], 4, 1)
        c["a1"].wait_recv()
        t[1] = p[rows(L, 1), :] + t[1]
        go("a5", t.at[1], f.at[1, 1], 5, 3)

    @cm.when(times[2])
    def _():
        c["a3"].wait_recv()
        c["a4"].wait_recv()
        first = finish(0, p[rows(me, 0), :] + f[0, 0] + f[1, 0])
        if not share:
            c["a2"].wait_recv()
            c["a5"].wait_recv()
            o[0:H, :] = first
            o[H:C, :] = finish(1, p[rows(me, 1), :] + f[0, 1] + f[1, 1])
            return
        o[rows(me, 0), :] = first
        go("b0", o.at[rows(me, 0)], o.at[rows(me, 0)], 6, 1)
        c["a2"].wait_recv()
        c["a5"].wait_recv()
        o[rows(me, 1), :] = finish(1, p[rows(me, 1), :] + f[0, 1] + f[1, 1])
        go("c1", o.at[rows(me, 1)], o.at[rows(me, 1)], 9, 3)
        go("b1", o.at[rows(me, 1)], o.at[rows(me, 1)], 7, 1)
        go("c0", o.at[rows(me, 0)], o.at[rows(me, 0)], 8, 3)

    if not share:
        return

    @cm.when(times[3])
    def _():
        c["b0"].wait_recv()
        go("d0", o.at[rows(L, 0)], o.at[rows(L, 0)], 10, 1)
        c["c1"].wait_recv()
        go("d1", o.at[rows(R, 1)], o.at[rows(R, 1)], 11, 3)

    @cm.when(900)
    def _():
        for name in ("b1", "c0", "d0", "d1"):
            c[name].wait_recv()
        closing()


def scatter_ring(cm, chunk, t, f, s_sem, r_sem, base, to, times, done):
    c = {}

    def go(name, src, dst, i, n):
        c[name] = cm.send(src, dst, s_sem.at[base + i], r_sem.at[base + i], to(n))

    @cm.when(times[0])
    def _():
        go("a0", chunk(2, 0), t.at[0], 0, 1)
        go("a1", chunk(2, 1), t.at[1], 1, 3)

    @cm.when(times[1])
    def _():
        go("a2", chunk(1, 1), f.at[0, 1], 2, 1)

    @cm.when(times[2])
    def _():
        go("a3", chunk(3, 0), f.at[1, 0], 3, 3)

    @cm.when(times[3])
    def _():
        c["a0"].wait_recv()
        add_up(t.at[0], chunk(1, 0))
        go("a4", t.at[0], f.at[0, 0], 4, 1)
        c["a1"].wait_recv()
        add_up(t.at[1], chunk(3, 1))
        go("a5", t.at[1], f.at[1, 1], 5, 3)

    @cm.when(times[4])
    def _():
        c["a3"].wait_recv()
        c["a4"].wait_recv()
        add_up(chunk(0, 0), f.at[0, 0], f.at[1, 0])
        c["a2"].wait_recv()
        c["a5"].wait_recv()
        add_up(chunk(0, 1), f.at[0, 1], f.at[1, 1])
        done()


def grad_scatter(cm, products_a, products_b, G, RC, wa, bufs, sems, times, done_a, done_b):
    tA, tB, fA, fB, t2A, t2B, f2A, f2B = bufs
    cs, cr, as_, ar, bs, br = sems
    W = G.shape[-1]
    quarter = products_a[0][0].shape[1] // 4
    got = {}

    cols_a, cols_b = pl.ds(0, wa), pl.ds(wa, W - wa)

    def block(part, turn):
        k = ahead(cm.x, turn)
        products, cols, i = (products_a, cols_a, turn) if part == "a" else (products_b, cols_b, 4 + turn)
        for left, rights, at in products:
            right = jnp.concatenate([r[...] for r in rights], axis=1)
            w = right.shape[1]
            lhs = left[:, pl.ds(pl.multiple_of(k * quarter, quarter), quarter)]
            value = lax.dot_general(
                lhs, right, (((0,), (0,)), ((), ())), preferred_element_type=jnp.float32
            )
            G[k, :, :, :, pl.ds(at, w)] = value.reshape(4, 2, 32, w)
        got[part, turn] = cm.send(
            G.at[k, :, 1 - cm.core, :, cols], RC.at[k, :, :, cols], cs.at[i], cr.at[i], cm.twin()
        )

    def settle(part, turn):
        k = ahead(cm.x, turn)
        cols = cols_a if part == "a" else cols_b
        got[part, turn].wait_recv()
        add_up(G.at[k, :, cm.core, :, cols], RC.at[k, :, :, cols])

    for part in "ba":
        for i, turn in enumerate((2, 1, 3, 0)):
            cm.when(times["block_" + part][i])(lambda part=part, turn=turn: block(part, turn))
            cm.when(times["settle_" + part][i])(lambda part=part, turn=turn: settle(part, turn))

    core = cm.core

    def a1(turn, half):
        return G.at[ahead(cm.x, turn), pl.ds(half * 2, 2), core, :, cols_a]

    def b1(turn, half):
        return G.at[pl.ds(half * 2, 2), ahead(cm.z, turn), core, :, cols_b]

    def a2(turn, half):
        return G.at[cm.x, pl.ds(ahead(cm.z, turn), 1), core, pl.ds(half * 16, 16), cols_a]

    def b2(turn, half):
        return G.at[pl.ds(ahead(cm.x, turn), 1), cm.z, core, pl.ds(half * 16, 16), cols_b]

    nothing = lambda: None
    scatter_ring(cm, a1, tA, fA, as_, ar, 0, cm.at_x, times["A"], nothing)
    scatter_ring(cm, b1, tB, fB, bs, br, 0, cm.at_z, times["B"], nothing)
    scatter_ring(cm, a2, t2A, f2A, as_, ar, 6, cm.at_z, times["A2"], done_a)
    scatter_ring(cm, b2, t2B, f2B, bs, br, 6, cm.at_x, times["B2"], done_b)


def small_sums(cm, small, sm, sr, s_sem, r_sem, times, done):
    axes = [(cm.at_z, cm.z), (cm.at_x, cm.x), (cm.at_y, cm.me)]
    first = {}

    @cm.when(times[0])
    def _():
        first["c"] = cm.send(small, sr.at[3, 0], s_sem.at[9], r_sem.at[9], cm.twin())

    @cm.when(times[1])
    def _():
        first["c"].wait_recv()
        sm[0] = small[...] + sr[3, 0]

    for a, (to, here) in enumerate(axes):
        copies = []

        def begin(a=a, to=to, here=here, copies=copies):
            sr[a, here] = sm[a]
            for n in (1, 2, 3):
                i = a * 3 + n - 1
                copies.append(cm.send(sm.at[a], sr.at[a, here], s_sem.at[i], r_sem.at[i], to(n)))

        def end(a=a, copies=copies):
            for copy in copies:
                copy.wait_recv()
            total = (sr[a, 0] + sr[a, 1]) + (sr[a, 2] + sr[a, 3])
            if a < 2:
                sm[a + 1] = total
            else:
                done(total[0:16], sm[2][16:24])

        cm.when(times[1] + 0.01)(begin) if a == 0 else cm.when(times[1 + a] + 0.01)(begin)
        cm.when(times[2 + a])(end)


def greet_all(cm, more):
    cm.greet([axis(n) for n in (1, 2, 3) for axis in (cm.at_x, cm.at_z, cm.at_y)] + [cm.twin()] + more)


def front_kernel(
    gated, ow, tokens, cot, down, gain, o_normed, o_full, o_own, o_dact, o_resid, o_cot, o_tok, resid, GF, WF, ys, yr, ws, wr
):
    cm = Comm()
    x, z, c, me = cm.x, cm.z, cm.core, cm.me
    R, L, O = ahead(me, 1), ahead(me, 3), ahead(me, 2)
    cm.greet([cm.at_x(1), cm.at_x(3), cm.at_z(1), cm.at_z(3), cm.at_y(1), cm.at_y(2), cm.at_y(3), cm.twin()])
    T = gated.shape[0]
    N = T // 2
    piece = ((x * 4 + z) * 2 + c) * 32
    h = {}

    def weight(name, ref, i, dev):
        h[name] = cm.send(ref, ref, ws.at[i], wr.at[i], dev)

    def gate(name, ref, i, n):
        h[name] = cm.send(ref, ref, ys.at[i], yr.at[i], cm.at_y(n))

    low, high = pl.ds(0, 2), pl.ds(2, 2)
    WF[x, z, c, me] = ow[pl.ds(pl.multiple_of(piece, 32), 32), :].astype(jnp.float32)
    for n in (1, 2, 3):
        weight(("y", n), WF.at[x, z, c, me], n - 1, cm.at_y(n))
    GF[me] = gated[...].astype(jnp.float32)
    first, second = pl.ds(0, N), pl.ds(N, N)
    gate("r0", GF.at[me, first], 0, 1)
    gate("l1", GF.at[me, second], 1, 3)
    gate("r1", GF.at[me, second], 2, 1)
    gate("l0", GF.at[me, first], 3, 3)
    for n in (1, 2, 3):
        h["y", n].wait_recv()
    weight("ax1", WF.at[x, z, c, low], 3, cm.at_x(1))
    weight("ax3", WF.at[x, z, c, low], 4, cm.at_x(3))
    weight("bz1", WF.at[x, z, c, high], 5, cm.at_z(1))
    weight("bz3", WF.at[x, z, c, high], 6, cm.at_z(3))
    resid[...] = tokens[...].astype(jnp.float32) + lax.dot_general(
        gated[...], ow[...], (((1,), (1,)), ((), ())), preferred_element_type=jnp.float32
    )
    mine = pl.ds(pl.multiple_of(me * (T // 4), T // 4), T // 4)
    o_cot[...] = cot[mine, :]
    o_tok[...] = tokens[mine, :]
    xl, xr, zl, zr = ahead(x, 3), ahead(x, 1), ahead(z, 3), ahead(z, 1)
    h["ax1"].wait_recv()
    weight("ax1f", WF.at[xl, z, c, 0], 7, cm.at_x(1))
    h["ax3"].wait_recv()
    weight("ax3f", WF.at[xr, z, c, 1], 8, cm.at_x(3))
    h["bz1"].wait_recv()
    weight("bz1f", WF.at[x, zl, c, 2], 9, cm.at_z(1))
    h["bz3"].wait_recv()
    weight("bz3f", WF.at[x, zr, c, 3], 10, cm.at_z(3))
    h["ax1f"].wait_recv()
    h["ax3f"].wait_recv()
    weight("az1", WF.at[:, z, c, low], 11, cm.at_z(1))
    weight("az3", WF.at[:, z, c, low], 12, cm.at_z(3))
    h["bz1f"].wait_recv()
    h["bz3f"].wait_recv()
    weight("bx1", WF.at[x, :, c, high], 13, cm.at_x(1))
    weight("bx3", WF.at[x, :, c, high], 14, cm.at_x(3))
    zo, xo = ahead(z, 2), ahead(x, 2)
    weight("t0", WF.at[:, z, c, low], 19, cm.twin())
    weight("t1", WF.at[x, :, c, high], 20, cm.twin())
    o_dact[...] = jnp.dot(cot[...], down[...], preferred_element_type=jnp.float32)
    h["r0"].wait_recv()
    gate("r0f", GF.at[L, first], 4, 1)
    h["l1"].wait_recv()
    gate("l1f", GF.at[R, second], 5, 3)
    h["az1"].wait_recv()
    weight("az1f", WF.at[:, zl, c, 0], 15, cm.at_z(1))
    weight("t2", WF.at[:, zl, c, low], 21, cm.twin())
    h["az3"].wait_recv()
    weight("az3f", WF.at[:, zr, c, 1], 16, cm.at_z(3))
    weight("t3", WF.at[:, zr, c, low], 22, cm.twin())
    h["bx1"].wait_recv()
    weight("bx1f", WF.at[xl, :, c, 2], 17, cm.at_x(1))
    weight("t4", WF.at[xl, :, c, high], 23, cm.twin())
    h["bx3"].wait_recv()
    weight("bx3f", WF.at[xr, :, c, 3], 18, cm.at_x(3))
    weight("t5", WF.at[xr, :, c, high], 24, cm.twin())
    h["az1f"].wait_recv()
    h["az3f"].wait_recv()
    weight("t6", WF.at[:, zo, c, low], 25, cm.twin())
    h["bx1f"].wait_recv()
    h["bx3f"].wait_recv()
    weight("t7", WF.at[xo, :, c, high], 26, cm.twin())
    h["r1"].wait_recv()
    h["l0"].wait_recv()
    for k in range(8):
        h[f"t{k}"].wait_recv()
    for k in range(4):
        o_full[k] = WF[:, :, :, k].reshape(1024, 256).astype(jnp.bfloat16)

    def add(*heads):
        resid[...] += lax.dot_general(
            jnp.concatenate([GF[k].astype(jnp.bfloat16) for k in heads], axis=1),
            jnp.concatenate([o_full[k] for k in heads], axis=1),
            (((1,), (1,)), ((), ())),
            preferred_element_type=jnp.float32,
        )

    add(L, R)
    h["r0f"].wait_recv()
    h["l1f"].wait_recv()
    add(O)
    for k in range(4):
        o_own[:, 256 * k : 256 * (k + 1)] = GF[k, mine, :].astype(jnp.bfloat16)
    o_resid[...] = resid[mine, :]

    def body(i, carry):
        rows = pl.ds(pl.multiple_of(i * 32, 32), 32)
        values = resid[rows, :]
        scale = lax.rsqrt(jnp.mean(values * values, axis=-1, keepdims=True) + EPS)
        o_normed[rows, :] = (values * scale * gain[...]).astype(jnp.bfloat16)
        return carry

    lax.fori_loop(0, T // 32, body, 0)
    cm.run()


EARLY = 256


def middle_kernel(*refs):
    (dn, own_resid, gain, own_cot, normed, d_gate, d_up, act, down, ow) = refs[:10]
    (proj, mixed, conv_out, marks, taps, in_w, toks, cot) = refs[10:18]
    (o_dres, o_dlow, o_gain, o_res, o_gate, o_up, o_down, o_dproj, o_dm, o_taps, o_mix) = refs[18:29]
    (rp, full, turned, relay, dgated, DC, yt, yf, G, RC) = refs[29:39]
    bufs, (ys, yr), sems, (xs, xr), (hs, hr) = refs[39:47], refs[47:49], refs[49:55], refs[55:57], refs[57:]
    H = own_resid.shape[0] // 2
    T = 8 * H
    cm = Comm()
    greet_all(cm, [cm.along(1), cm.along(31)])

    def finish_dres(half, total):
        mine = pl.ds(half * H, H)
        rows, gains = norm_back_rows(
            total, own_resid[mine, :], gain[...], own_cot[mine, :].astype(jnp.float32)
        )
        o_gain[...] = gains if half == 0 else o_gain[...] + gains
        return rows

    def finish_result(half, total):
        return total + own_resid[pl.ds(half * H, H), :]

    def rounded():
        o_res[...] = full[...].astype(jnp.bfloat16)

    @cm.when(6.1)
    def _():
        rp[...] = lax.dot_general(
            act[...], down[...], (((1,), (1,)), ((), ())), preferred_element_type=jnp.float32
        )

    head_sum(cm, dn, o_dres, yt.at[0], yf.at[0], ys.at[0], yr.at[0], finish_dres, (0, 6, 18, 0), lambda: None, False)
    head_sum(cm, rp, full, yt.at[1], yf.at[1], ys.at[1], yr.at[1], finish_result, (6.2, 25, 44, 56), rounded)

    C = 2 * H
    R, L = ahead(cm.me, 1), ahead(cm.me, 3)
    c = {}

    def rows(k, half=None):
        if half is None:
            return pl.ds(pl.multiple_of(k * C, C), C)
        return pl.ds(pl.multiple_of(k * C + half * H, H), H)

    def go(name, src, dst, i, n):
        c[name] = cm.send(src, dst, xs.at[i], xr.at[i], cm.at_y(n))

    @cm.when(18.1)
    def _():
        low = o_dres[...].astype(jnp.bfloat16)
        o_dlow[...] = low
        for turn in (2, 1, 3):
            turned[turn - 1] = jnp.dot(low, ow[ahead(cm.me, turn)], preferred_element_type=jnp.float32)
            if turn == 2:
                go("e0", turned.at[1, pl.ds(0, H)], relay.at[0], 0, 1)
                go("e1", turned.at[1, pl.ds(H, H)], relay.at[1], 1, 3)
            else:
                go(("d", turn), turned.at[turn - 1], dgated.at[rows(cm.me)], 1 + turn, turn)
        dgated[rows(cm.me), :] = jnp.dot(low, ow[cm.me], preferred_element_type=jnp.float32)

    @cm.when(32)
    def _():
        c["e0"].wait_recv()
        go("f0", relay.at[0], dgated.at[rows(L, 0)], 5, 1)
        c["e1"].wait_recv()
        go("f1", relay.at[1], dgated.at[rows(R, 1)], 6, 3)

    N = 64

    @cm.when(38)
    def _():
        for name in (("d", 1), ("d", 3), "f0", "f1"):
            c[name].wait_recv()
        for i in range(T // N):
            at = pl.ds(i * N, N)
            dg = dgated[at, :]
            o_dproj[1, at, :] = (dg * conv_out[at, :]).astype(jnp.bfloat16)
            DC[at, :] = dg * proj[1, at, :]
        c["halo"] = cm.send(DC.at[pl.ds(0, 8)], DC.at[pl.ds(T, 8)], hs.at[0], hr.at[0], cm.along(31))

    @cm.when(41)
    def _():
        c["halo"].wait_recv()
        w0, w1, w2 = taps[0:1, :], taps[1:2, :], taps[2:3, :]
        sums = [jnp.zeros((1, 256), jnp.float32)] * 3
        for i in range(T // N):
            at = pl.ds(i * N, N)
            near, far = marks[at, 0:1], marks[at, 1:2]
            near_next, far_next = marks[at, 2:3], marks[at, 3:4]
            dc = DC[at, :]
            d_mixed = w0 * dc + w1 * near_next * DC[pl.ds(i * N + 1, N), :] + w2 * far_next * DC[pl.ds(i * N + 2, N), :]
            o_dproj[0, at, :] = (d_mixed * proj[2, at, :]).astype(jnp.bfloat16)
            o_dproj[2, at, :] = (d_mixed * proj[0, at, :]).astype(jnp.bfloat16)
            terms = (
                dc * mixed[pl.ds(i * N + 8, N), :],
                dc * near * mixed[pl.ds(i * N + 7, N), :],
                dc * far * mixed[pl.ds(i * N + 6, N), :],
            )
            sums = [s + jnp.sum(t, axis=0, keepdims=True) for s, t in zip(sums, terms)]
        for k in range(3):
            o_taps[k : k + 1, :] = sums[k]

    @cm.when(45)
    def _():
        right = jnp.concatenate([in_w[0], in_w[1], in_w[2]], axis=1)
        for i in range(4):
            at = pl.ds(i * C, C)
            left = jnp.concatenate([o_dproj[0, at, :], o_dproj[1, at, :], o_dproj[2, at, :]], axis=1)
            o_dm[at, :] = lax.dot_general(
                left, right, (((1,), (1,)), ((), ())), preferred_element_type=jnp.float32
            )

        def body(i, total):
            at = pl.ds(pl.multiple_of(i * 32, 32), 32)
            values = toks[at, :].astype(jnp.float32)
            scale = lax.rsqrt(jnp.mean(values * values, axis=-1, keepdims=True) + EPS)
            return total + jnp.sum(o_dm[at, :] * values * scale, axis=0, keepdims=True)

        o_mix[...] = lax.fori_loop(0, T // 32, body, jnp.zeros(o_mix.shape, jnp.float32))

    w = act.shape[1]
    e = EARLY // 2

    def done_a():
        rows = G[cm.x, cm.z, cm.core, :, pl.ds(0, w + e)]
        o_gate[...] = rows[:, :w]
        o_down[:, pl.ds(0, e)] = rows[:, w:]

    def done_b():
        rows = G[cm.x, cm.z, cm.core, :, pl.ds(w + e, w + e)]
        o_down[:, pl.ds(e, e)] = rows[:, :e]
        o_up[...] = rows[:, e:]

    times = {
        "block_b": (0.1, 0.2, 0.3, 0.4),
        "block_a": (0.5, 1.3, 2.1, 2.9),
        "settle_b": (1.21, 1.22, 1.23, 1.24),
        "settle_a": (2, 2.8, 3.6, 4.4),
        "B": (1.25, 1.26, 1.27, 11.5, 27),
        "A": (2.01, 2.81, 3.61, 12.5, 28.5),
        "B2": (27.1, 27.2, 27.3, 32.1, 35),
        "A2": (28.6, 28.7, 28.8, 31, 34.5),
    }
    products_a = [(normed, [d_gate], 0), (cot, [act.at[:, pl.ds(0, e)]], w)]
    products_b = [(cot, [act.at[:, pl.ds(e, e)]], w + e), (normed, [d_up], w + EARLY)]
    grad_scatter(cm, products_a, products_b, G, RC, w + e, bufs, sems, times, done_a, done_b)
    cm.run()


def end_kernel(*refs):
    (dm, toks, gain, d_res, normed, d_proj, d_low, gated, act, cot, mix_gains, ffn_gains, taps) = refs[:13]
    (o_tok, o_in, o_out, o_down, o_mix, o_ffn, o_conv) = refs[13:20]
    (yt, yf, G, RC) = refs[20:24]
    bufs = refs[24:32]
    small, sm, sr = refs[32:35]
    ys, yr = refs[35:37]
    sems = refs[37:43]
    ss, sr_sem = refs[43:45]
    mine, theirs, hs, hr = refs[45:]
    H = toks.shape[0] // 2
    cm = Comm()
    greet_all(cm, [])

    def finish_tokens(half, total):
        at = pl.ds(half * H, H)
        return norm_back_rows(total, toks[at, :].astype(jnp.float32), gain[...], d_res[at, :])[0]

    @cm.when(-1)
    def _():
        small[16:24, :] = jnp.zeros((8, 128), jnp.float32)
        for k in range(8):
            small[k : k + 1, :] = mix_gains[:, 128 * k : 128 * (k + 1)]
            small[8 + k : 9 + k, :] = ffn_gains[:, 128 * k : 128 * (k + 1)]
        for k in range(3):
            for h in range(2):
                small[16 + 2 * k + h : 17 + 2 * k + h, :] = taps[k : k + 1, 128 * h : 128 * (h + 1)]

    head_sum(cm, dm, o_tok, yt, yf, ys, yr, finish_tokens, (0, 8, 19.5, 27), lambda: None)

    w = act.shape[1] - EARLY
    wa = w + 512
    heads = []

    def done_a():
        rows = G[cm.x, cm.z, cm.core, :, pl.ds(0, wa)]
        o_down[...] = rows[:, :w]
        o_in[0] = rows[:, w : w + 256]
        o_in[1] = rows[:, w + 256 :]

    def done_b():
        rows = G[cm.x, cm.z, cm.core, :, pl.ds(wa, 1280)]
        o_in[2] = rows[:, :256]
        for k in range(4):
            mine[k] = rows[:, 256 + 256 * k : 512 + 256 * k]
        for n in (1, 2, 3):
            heads.append(
                cm.send(mine.at[ahead(cm.me, n)], theirs.at[n - 1], hs.at[n - 1], hr.at[n - 1], cm.at_y(n))
            )

    @cm.when(950)
    def _():
        for copy in heads:
            copy.wait_recv()
        o_out[...] = (mine[cm.me] + theirs[0]) + (theirs[1] + theirs[2])

    times = {
        "block_b": (0.1, 0.2, 0.3, 0.4),
        "block_a": (0.5, 1.5, 2.6, 3.6),
        "settle_b": (1.41, 1.42, 1.43, 1.44),
        "settle_a": (2.5, 3.5, 4.5, 5.5),
        "B": (1.45, 1.46, 1.47, 13, 29),
        "A": (2.51, 3.51, 4.51, 15, 33),
        "B2": (29.1, 29.2, 29.3, 34.5, 40),
        "A2": (33.1, 33.2, 33.3, 36.5, 40.5),
    }
    products_a = [
        (cot, [act.at[:, pl.ds(EARLY, w)]], 0),
        (normed, [d_proj.at[0], d_proj.at[1]], w),
    ]
    products_b = [(normed, [d_proj.at[2]], wa), (d_low, [gated], wa + 256)]
    grad_scatter(cm, products_a, products_b, G, RC, wa, bufs, sems, times, done_a, done_b)

    def small_done(gains, rest):
        o_mix[...] = gains[0:8]
        o_ffn[...] = gains[8:16]
        for k in range(3):
            for h in range(2):
                o_conv[k : k + 1, pl.ds(128 * h, 128)] = rest[2 * k + h : 2 * k + h + 1]

    small_sums(cm, small, sm, sr, ss, sr_sem, (-0.9, 1.443, 8.1, 19.6, 38), small_done)
    cm.run()


VMEM_SPEC = pl.BlockSpec(memory_space=pltpu.VMEM)


def call(kernel, name, cid, args, outs, scratch, limit):
    return pl.pallas_call(
        kernel,
        out_shape=outs,
        in_specs=[VMEM_SPEC] * len(args),
        out_specs=(VMEM_SPEC,) * len(outs),
        scratch_shapes=scratch,
        compiler_params=pltpu.CompilerParams(
            collective_id=cid, has_side_effects=True, vmem_limit_bytes=limit << 20
        ),
        cost_estimate=pl.CostEstimate(flops=1, bytes_accessed=1, transcendentals=0),
        name=name,
    )(*args)


def scatter_scratch(W, wa):
    f32 = jnp.float32
    wb = W - wa
    return [
        pltpu.VMEM((4, 4, 2, 32, W), f32),
        pltpu.VMEM((4, 4, 32, W), f32),
        pltpu.VMEM((2, 2, 32, wa), f32),
        pltpu.VMEM((2, 2, 32, wb), f32),
        pltpu.VMEM((2, 2, 2, 32, wa), f32),
        pltpu.VMEM((2, 2, 2, 32, wb), f32),
        pltpu.VMEM((2, 1, 16, wa), f32),
        pltpu.VMEM((2, 1, 16, wb), f32),
        pltpu.VMEM((2, 2, 1, 16, wa), f32),
        pltpu.VMEM((2, 2, 1, 16, wb), f32),
    ]


SCATTER_SEMS = [pltpu.SemaphoreType.DMA((n,)) for n in (8, 8, 12, 12, 12, 12)]


def front(gated, ow, tokens, cot, down, gain):
    T, D = tokens.shape
    f32, bf16, shape, dma = jnp.float32, jnp.bfloat16, jax.ShapeDtypeStruct, pltpu.SemaphoreType.DMA
    outs = (
        shape((T, D), bf16),
        shape((4, *ow.shape), bf16),
        shape((T // 4, D), bf16),
        shape((T, down.shape[1]), f32),
        shape((T // 4, D), f32),
        shape((T // 4, D), bf16),
        shape((T // 4, D), bf16),
    )
    scratch = [
        pltpu.VMEM((T, D), f32),
        pltpu.VMEM((4, *gated.shape), f32),
        pltpu.VMEM((4, 4, 2, 4, 32, ow.shape[1]), f32),
        dma((6,)),
        dma((6,)),
        dma((27,)),
        dma((27,)),
    ]
    return call(front_kernel, "front", 3, (gated, ow, tokens, cot, down, gain), outs, scratch, 24)


def middle(*args):
    dn, act, proj = args[0], args[7], args[10]
    T, D = dn.shape
    H = T // 8
    f32, bf16, shape, dma = jnp.float32, jnp.bfloat16, jax.ShapeDtypeStruct, pltpu.SemaphoreType.DMA
    w = act.shape[1]
    outs = (
        shape((T // 4, D), f32),
        shape((T // 4, D), bf16),
        shape((1, D), f32),
        shape((T, D), bf16),
        shape((32, w), f32),
        shape((32, w), f32),
        shape((32, EARLY), f32),
        shape(proj.shape, bf16),
        shape((T, D), f32),
        shape((3, 256), f32),
        shape((1, D), f32),
    )
    scratch = [
        pltpu.VMEM((T, D), f32),
        pltpu.VMEM((T, D), f32),
        pltpu.VMEM((3, 2 * H, 256), f32),
        pltpu.VMEM((2, H, 256), f32),
        pltpu.VMEM((T, 256), f32),
        pltpu.VMEM((T + 8, 256), f32),
        pltpu.VMEM((2, 2, H, D), f32),
        pltpu.VMEM((2, 2, 2, H, D), f32),
        *scatter_scratch(2 * w + EARLY, w + EARLY // 2),
        dma((2, 12)),
        dma((2, 12)),
        *SCATTER_SEMS,
        dma((7,)),
        dma((7,)),
        dma((1,)),
        dma((1,)),
    ]
    return call(middle_kernel, "middle", 5, args, outs, scratch, 30)


def end(*args):
    dm, act = args[0], args[8]
    T, D = dm.shape
    H = T // 8
    f32, shape, dma = jnp.float32, jax.ShapeDtypeStruct, pltpu.SemaphoreType.DMA
    w = act.shape[1] - EARLY
    outs = (
        shape((T, D), f32),
        shape((3, 32, 256), f32),
        shape((32, 256), f32),
        shape((32, w), f32),
        shape((8, 128), f32),
        shape((8, 128), f32),
        shape((3, 256), f32),
    )
    scratch = [
        pltpu.VMEM((2, H, D), f32),
        pltpu.VMEM((2, 2, H, D), f32),
        *scatter_scratch(w + 1792, w + 512),
        pltpu.VMEM((24, 128), f32),
        pltpu.VMEM((3, 24, 128), f32),
        pltpu.VMEM((4, 4, 24, 128), f32),
        dma((12,)),
        dma((12,)),
        *SCATTER_SEMS,
        dma((10,)),
        dma((10,)),
        pltpu.VMEM((4, 32, 256), f32),
        pltpu.VMEM((3, 32, 256), f32),
        dma((3,)),
        dma((3,)),
    ]
    return call(end_kernel, "end", 7, args, outs, scratch, 36)


def place(down_early, down_late, *arrays):
    n = len(arrays)
    early, late = down_early.shape[1], down_late.shape[1]

    def kernel(*refs):
        first, second, ins = refs[0], refs[1], refs[2 : n + 2]
        whole, outs, sems = refs[n + 2], refs[n + 3 : 2 * n + 3], refs[2 * n + 3]
        pairs = [
            (first, whole.at[:, pl.ds(0, early)]),
            (second, whole.at[:, pl.ds(early, late)]),
            *zip(ins, outs),
        ]
        copies = [pltpu.make_async_copy(a, b, sems.at[i]) for i, (a, b) in enumerate(pairs)]
        for copy in copies:
            copy.start()
        for copy in copies:
            copy.wait()

    anywhere = pl.BlockSpec(memory_space=pl.ANY)
    shapes = [jax.ShapeDtypeStruct((down_early.shape[0], early + late), jnp.float32)]
    shapes += [jax.ShapeDtypeStruct(a.shape, a.dtype) for a in arrays]
    return pl.pallas_call(
        kernel,
        out_shape=tuple(shapes),
        in_specs=[VMEM_SPEC] * (n + 2),
        out_specs=(anywhere,) * (n + 1),
        scratch_shapes=[pltpu.SemaphoreType.DMA((n + 2,))],
        compiler_params=pltpu.CompilerParams(vmem_limit_bytes=2 << 20),
        name="place",
    )(down_early, down_late, *arrays)


def from_behind(block, axis, distance):
    devices = range(lax.axis_size(axis))
    route = [(i - distance, i) for i in devices if i - distance in devices]
    return lax.ppermute(block, axis, route)


def rms_scale(values):
    return lax.rsqrt(jnp.mean(values * values, axis=-1, keepdims=True) + EPS)


def right_product(left, right):
    return lax.dot_general(
        left, right, (((1,), (1,)), ((), ())), preferred_element_type=jnp.float32
    )


def on_device(
    tokens,
    segment_ids,
    mix_gain,
    in_weight,
    conv_weight,
    out_weight,
    ffn_gain,
    gate_weight,
    up_weight,
    down_weight,
    cotangent,
):
    tok_rows = tokens.shape[0]
    first_row = lax.axis_index("seq") * tok_rows
    padded_ids = jnp.concatenate(
        [jnp.full((2,), -1, jnp.int32), segment_ids, jnp.full((2,), -2, jnp.int32)]
    )
    id_window = lax.dynamic_slice_in_dim(padded_ids, first_row, tok_rows + 4)
    near_ext = (id_window[2 : tok_rows + 4] == id_window[1 : tok_rows + 3]).astype(jnp.float32)
    far_ext = (id_window[2 : tok_rows + 4] == id_window[0 : tok_rows + 2]).astype(jnp.float32)
    near_own = near_ext[:tok_rows, None]
    far_own = far_ext[:tok_rows, None]
    inputs = tokens.astype(jnp.float32)
    mix_scale = rms_scale(inputs)
    mix_normed = (inputs * mix_scale * mix_gain).astype(jnp.bfloat16)
    projected = jnp.einsum("td,dkc->tkc", mix_normed, in_weight, preferred_element_type=jnp.float32)
    chan_b = projected[:, 0]
    chan_c = projected[:, 1]
    chan_x = projected[:, 2]
    mixed = chan_b * chan_x
    edge_rows = from_behind(mixed[tok_rows - 2 :], "seq", 1)
    extended = jnp.concatenate([edge_rows, mixed])
    kernel = conv_weight.astype(jnp.float32)
    prev_one = extended[1 : tok_rows + 1]
    prev_two = extended[0:tok_rows]
    conv_out = kernel[0] * mixed + kernel[1] * near_own * prev_one + kernel[2] * far_own * prev_two
    gated = (chan_c * conv_out).astype(jnp.bfloat16)
    ffn_normed, out_full, gated_rows, d_act, own_resid, own_cot, own_tok = front(
        gated, out_weight, tokens, cotangent, down_weight, ffn_gain[None]
    )
    gate = jnp.dot(ffn_normed, gate_weight, preferred_element_type=jnp.float32)
    upper = jnp.dot(ffn_normed, up_weight, preferred_element_type=jnp.float32)
    sigma = jax.nn.sigmoid(gate)
    act = (gate * sigma * upper).astype(jnp.bfloat16)
    d_gate = (d_act * upper * sigma * (1.0 + gate * (1.0 - sigma))).astype(jnp.bfloat16)
    d_up = (d_act * gate * sigma).astype(jnp.bfloat16)
    d_normed_part = right_product(d_gate, gate_weight) + right_product(d_up, up_weight)
    marks = jnp.stack(
        [near_own[:, 0], far_own[:, 0], near_ext[1 : tok_rows + 1], far_ext[2 : tok_rows + 2]], axis=1
    )
    d_resid, d_resid_low, grad_ffn_gain, result, gate_share, up_share, down_early, d_projected, d_mix_part, grad_conv, grad_mix_gain = middle(
        d_normed_part,
        own_resid,
        ffn_gain[None],
        own_cot,
        ffn_normed,
        d_gate,
        d_up,
        act,
        down_weight,
        out_full,
        projected.transpose(1, 0, 2),
        jnp.concatenate([jnp.zeros((6, mixed.shape[1]), jnp.float32), extended]),
        conv_out,
        marks,
        kernel,
        in_weight.transpose(1, 0, 2),
        tokens,
        cotangent,
    )
    grad_tokens, in_share, out_share, down_share, mix_total, ffn_total, conv_total = end(
        d_mix_part,
        own_tok,
        mix_gain[None],
        d_resid,
        mix_normed,
        d_projected,
        d_resid_low,
        gated_rows,
        act,
        cotangent,
        grad_mix_gain,
        grad_ffn_gain,
        grad_conv,
    )
    (
        down_share,
        result,
        grad_tokens,
        mix_total,
        in_share,
        conv_total,
        out_share,
        ffn_total,
        gate_share,
        up_share,
    ) = place(
        down_early,
        down_share,
        result,
        grad_tokens,
        mix_total,
        in_share,
        conv_total,
        out_share,
        ffn_total,
        gate_share,
        up_share,
    )
    return (
        result,
        grad_tokens,
        mix_total.reshape(-1),
        in_share.transpose(1, 0, 2),
        conv_total,
        out_share,
        ffn_total.reshape(-1),
        gate_share,
        up_share,
        down_share,
    )


def solution(mesh):
    placed = (
        P("seq", None),
        P(),
        P(),
        P(None, None, "head"),
        P(None, "head"),
        P(None, "head"),
        P(),
        P(None, "head"),
        P(None, "head"),
        P(None, "head"),
        P("seq", None),
    )
    return jax.shard_map(
        on_device,
        mesh=mesh,
        in_specs=placed,
        out_specs=(
            P("seq", None),
            P("seq", None),
            P(),
            P("seq", None, "head"),
            P(None, "head"),
            P("seq", "head"),
            P(),
            P("seq", "head"),
            P("seq", "head"),
            P("seq", "head"),
        ),
        check_vma=False,
    )
```
